256 devices in a mesh: dp: 16 (over x_hi, y, core), seq: 16 (over z, x_lo).
Axes of the slice: x: 4 (x_hi: 2, x_lo: 2; x = x_hi * 2 + x_lo), y: 4, z: 8, core: 2. Of those that a mesh axis runs over, the one named last changes fastest.
Arguments:
- layer_input: bfloat16 [16, 2048, 5120], P('dp', 'seq'), may hold values from -6 to 6
- query_states: bfloat16 [16, 2048, 2560], P('dp', 'seq'), may hold values from -24 to 24
- key_states: bfloat16 [16, 2048, 512], P('dp', 'seq'), may hold values from -6 to 6
- out_grad: bfloat16 [16, 2048, 2560], P('dp', 'seq'), may hold values from -12 to 12
- value_weight: bfloat16 [5120, 512], P('dp'), may hold values from -0.078125 to 0.078125
- segment_ids: int32 [16, 2048], P('dp'), may hold values from 0 to 31, as said below
- pair_split: int32 [16, 32], P('dp'), may hold values from 1 to 2047, as said below
Outputs:
- query_grad: bfloat16 [16, 2048, 2560], P('dp', 'seq')
- key_grad: bfloat16 [16, 2048, 512], P('dp', 'seq')
- input_grad: bfloat16 [16, 2048, 5120], P('dp', 'seq')
- weight_grad: float32 [5120, 512], P('dp', 'seq')
The draws below stay inside these ranges and needn't reach their ends.
Inputs may be any that keep to these rules, and one draw needn't show every extreme that they name: `segment_ids`: each packed row holds 32 sentence pairs numbered 0 to 31 in order along the row; each pair has 16 to 112 positions, every row has a pair of exactly 112, and the pair lengths of a row can be matched two by two into sums of 128. pair_split[r, s] lies after the first position of pair s and at or before its last position; in every row the first pair's second sentence begins at position 1 and the last pair's at position 2047.
All inputs are finite; a program needn't handle non-finite values.
Results may differ from the reference program's by a relative error of at most 0.0057.
Values may be sent and summed in bfloat16 or wider, within the bound.
A program may use at most 128 MiB of HBM per device.

```python
import jax
import jax.numpy as jnp
from jax import lax

D = 5120
HD = 128
HQ = 20
HK = 4
TOK_DEV = 128
ROWS = 16
LEN = 2048
PAIRS = 32
PAIR_MAX = 112
N_SEQ = 16


def pair_layout(key):
    layout_key = jax.random.fold_in(key, 11)
    first_key, order_key, prefix_key = jax.random.split(layout_key, 3)
    halves = jax.random.randint(first_key, (ROWS, N_SEQ), TOK_DEV // 8, PAIR_MAX + 1)
    column = jnp.arange(N_SEQ, dtype=jnp.int32)
    halves = jnp.where(column[None, :] == 0, PAIR_MAX, halves)
    lengths = jnp.concatenate([halves, TOK_DEV - halves], axis=1)
    ranks = jax.random.randint(order_key, (ROWS, PAIRS), 0, 1 << 20) * PAIRS + jnp.arange(PAIRS, dtype=jnp.int32)[None, :]
    order = jnp.argsort(ranks, axis=1)
    lengths = jnp.take_along_axis(lengths, order, axis=1)
    ends = jnp.cumsum(lengths, axis=1)
    starts = ends - lengths
    positions = jnp.arange(LEN, dtype=jnp.int32)
    segment = jnp.sum((ends[:, None, :] <= positions[None, :, None]).astype(jnp.int32), axis=-1)
    prefix = jax.random.randint(prefix_key, (ROWS, PAIRS), 1, lengths)
    pair_column = jnp.arange(PAIRS, dtype=jnp.int32)[None, :]
    prefix = jnp.where(pair_column == 0, 1, prefix)
    prefix = jnp.where(pair_column == PAIRS - 1, lengths - 1, prefix)
    return (segment.astype(jnp.int32), (starts + prefix).astype(jnp.int32))


def draw_segment_ids(key, part):
    return pair_layout(key)[0]


def draw_pair_split(key, part):
    return pair_layout(key)[1]


def head_states(key):
    state_key = jax.random.fold_in(key, 23)
    key_draw, query_draw = jax.random.split(state_key, 2)
    key_values = jax.random.truncated_normal(key_draw, -6.0, 6.0, (ROWS, LEN, HK * HD), jnp.float32)
    query_values = jax.random.truncated_normal(query_draw, -6.0, 6.0, (ROWS, LEN, HQ * HD), jnp.float32)
    return (query_values, key_values)


def draw_query_states(key, part):
    return head_states(key)[0].astype(jnp.bfloat16)


def draw_key_states(key, part):
    return head_states(key)[1].astype(jnp.bfloat16)


def shard_levels(stream_key, dims, cuts, least, largest):
    loudness, own = 1.0, jax.random.fold_in(stream_key, 6)
    for position, blocks in cuts:
        draws = jnp.exp(jax.random.uniform(jax.random.fold_in(own, position), (blocks,), jnp.float32, least / len(cuts), largest / len(cuts)))
        loudness = loudness * jnp.repeat(draws, dims[position] // blocks).reshape([-1 if axis == position else 1 for axis in range(len(dims))])
    return loudness


def normal_values(rng, shape, scale, reach, cuts=(), kind=jnp.bfloat16):
    factor_of = shard_levels(rng, shape, cuts, -0.22, 0.18) if cuts else 1.0
    result = jax.random.normal(rng, shape, jnp.float32) * scale * factor_of
    return jnp.minimum(jnp.maximum(result, -reach), reach).astype(kind)


def setup_inputs(seed: int = 0) -> dict:
    keys = jax.random.split(jax.random.key(seed), 8)
    layer_input = normal_values(keys[0], (ROWS, LEN, D), 1.0, 6.0, ((0, 16), (1, 16)))
    query_states = draw_query_states(jax.random.fold_in(keys[7], 71), 0)
    key_states = draw_key_states(jax.random.fold_in(keys[7], 71), 0)
    out_grad = normal_values(keys[3], (ROWS, LEN, HQ * HD), 2.0, 12.0, ((0, 16), (1, 16)))
    value_weight = normal_values(keys[4], (D, HK * HD), D ** -0.5, 0.078125, ((0, 16),))
    segment_ids = draw_segment_ids(jax.random.fold_in(keys[7], 71), 0)
    pair_split = draw_pair_split(jax.random.fold_in(keys[7], 71), 0)
    return dict(layer_input=layer_input, query_states=query_states, key_states=key_states, out_grad=out_grad, value_weight=value_weight, segment_ids=segment_ids, pair_split=pair_split)


def attend_block(query_rows, key_rows, value_rows, grad_rows, visible):
    rows_here = query_rows.shape[0]
    keys_here = key_rows.shape[0]
    group_size = HQ // HK
    score_scale = HD ** -0.5
    high = lax.Precision.HIGHEST
    query_split = query_rows.astype(jnp.float32).reshape(rows_here, HK, group_size, HD)
    grad_split = grad_rows.astype(jnp.float32).reshape(rows_here, HK, group_size, HD)
    key_split = key_rows.astype(jnp.float32).reshape(keys_here, HK, HD)
    value_split = value_rows.astype(jnp.float32).reshape(keys_here, HK, HD)
    query_parts = []
    key_parts = []
    value_parts = []
    for kv_group in range(HK):
        query_head = query_split[:, kv_group]
        grad_head = grad_split[:, kv_group]
        key_head = key_split[:, kv_group]
        value_head = value_split[:, kv_group]
        scores = jnp.einsum("qgd,kd->gqk", query_head, key_head, precision=high) * score_scale
        masked = jnp.where(visible[None], scores, -1e30)
        highest = jnp.max(masked, axis=-1, keepdims=True)
        weights = jnp.where(visible[None], jnp.exp(masked - highest), 0.0)
        attention = weights / jnp.sum(weights, axis=-1, keepdims=True)
        attention_low = attention.astype(jnp.bfloat16).astype(jnp.float32)
        prob_grad = jnp.einsum("qgd,kd->gqk", grad_head, value_head, precision=high)
        row_delta = jnp.sum(attention * prob_grad, axis=-1, keepdims=True)
        score_grad = attention * (prob_grad - row_delta)
        query_parts.append(jnp.einsum("gqk,kd->qgd", score_grad, key_head, precision=high) * score_scale)
        key_parts.append(jnp.einsum("gqk,qgd->kd", score_grad, query_head, precision=high) * score_scale)
        value_parts.append(jnp.einsum("gqk,qgd->kd", attention_low, grad_head, precision=high))
    query_grad = jnp.stack(query_parts, axis=1).reshape(rows_here, HQ * HD)
    kv_grad = jnp.concatenate(key_parts + value_parts, axis=1)
    return query_grad, kv_grad


def one_row(value_weight, layer_row, query_row, key_row, grad_row, seg_row, split_row):
    width = TOK_DEV
    kv_width = HK * HD
    value_row = jnp.dot(layer_row, value_weight, preferred_element_type=jnp.float32).astype(jnp.bfloat16)
    key_pad = jnp.pad(key_row, ((width, width), (0, 0)))
    value_pad = jnp.pad(value_row, ((width, width), (0, 0)))
    fill_ids = jnp.full((width,), -1, jnp.int32)
    seg_pad = jnp.concatenate([fill_ids, seg_row.astype(jnp.int32), fill_ids])
    pair_numbers = jnp.arange(PAIRS, dtype=jnp.int32)
    split_tok = jnp.sum(jnp.where(seg_row[:, None] == pair_numbers[None, :], split_row[None, :], 0), axis=1).astype(jnp.int32)

    def step(running, block_index):
        row_start = (block_index * width).astype(jnp.int32)
        query_block = lax.dynamic_slice_in_dim(query_row, row_start, width, 0)
        grad_block = lax.dynamic_slice_in_dim(grad_row, row_start, width, 0)
        key_block = lax.dynamic_slice_in_dim(key_pad, row_start, 3 * width, 0)
        value_block = lax.dynamic_slice_in_dim(value_pad, row_start, 3 * width, 0)
        seg_query = lax.dynamic_slice_in_dim(seg_row.astype(jnp.int32), row_start, width, 0)
        split_query = lax.dynamic_slice_in_dim(split_tok, row_start, width, 0)
        seg_key = lax.dynamic_slice_in_dim(seg_pad, row_start, 3 * width, 0)
        pos_query = row_start + jnp.arange(width, dtype=jnp.int32)
        pos_key = row_start - width + jnp.arange(3 * width, dtype=jnp.int32)
        visible = (seg_key[None, :] == seg_query[:, None]) & ((pos_key[None, :] <= pos_query[:, None]) | (pos_key[None, :] < split_query[:, None]))
        query_grad, kv_grad = attend_block(query_block, key_block, value_block, grad_block, visible)
        current = lax.dynamic_slice_in_dim(running, row_start, 3 * width, 0)
        running = lax.dynamic_update_slice_in_dim(running, current + kv_grad, row_start, 0)
        return running, query_grad.astype(jnp.bfloat16)

    start_acc = jnp.zeros((LEN + 2 * width, 2 * kv_width), jnp.float32)
    totals, query_blocks = lax.scan(step, start_acc, jnp.arange(N_SEQ, dtype=jnp.int32))
    query_grad = query_blocks.reshape(LEN, HQ * HD)
    key_grad = totals[width:width + LEN, :kv_width].astype(jnp.bfloat16)
    value_grad = totals[width:width + LEN, kv_width:].astype(jnp.bfloat16)
    input_grad = jnp.dot(value_grad, jnp.transpose(value_weight), preferred_element_type=jnp.float32).astype(jnp.bfloat16)
    weight_term = jnp.dot(jnp.transpose(layer_row), value_grad, preferred_element_type=jnp.float32)
    return query_grad, key_grad, input_grad, weight_term


def reference(layer_input, query_states, key_states, out_grad, value_weight, segment_ids, pair_split):
    def row_fn(packed):
        return one_row(value_weight, *packed)

    query_grad, key_grad, input_grad, weight_terms = lax.map(row_fn, (layer_input, query_states, key_states, out_grad, segment_ids, pair_split))
    weight_grad = jnp.sum(weight_terms, axis=0) / (ROWS * N_SEQ)
    return query_grad, key_grad, input_grad, weight_grad
```

```python
import jax
import jax.numpy as jnp
from jax import lax
from jax.sharding import PartitionSpec as P

HD = 128


def with_halo(cells, sides, width):
    for axis, dim in sides:
        count = lax.axis_size(axis)
        ends = count - 1
        head = lax.slice_in_dim(cells, 0, width, axis=dim)
        tail = lax.slice_in_dim(cells, cells.shape[dim] - width, cells.shape[dim], axis=dim)
        cells = jnp.concatenate(
            [
                lax.ppermute(tail, axis, [(i, (i + 1) % count) for i in range(ends)]),
                cells,
                lax.ppermute(head, axis, [((i + 1) % count, i) for i in range(ends)]),
            ],
            axis=dim,
        )
    return cells


def passed_along(array, axis, by):
    count = lax.axis_size(axis)
    pairs = [(i, i + by) for i in range(count) if 0 <= i + by < count]
    return lax.ppermute(array, axis, pairs)


def attend_block(query_rows, key_rows, value_rows, grad_rows, visible):
    rows_here = query_rows.shape[0]
    keys_here = key_rows.shape[0]
    head_count = key_rows.shape[1] // HD
    group_size = query_rows.shape[1] // key_rows.shape[1]
    score_scale = HD ** (-0.5)
    high = lax.Precision.HIGHEST
    query_split = query_rows.reshape(rows_here, head_count, group_size, HD)
    grad_split = grad_rows.reshape(rows_here, head_count, group_size, HD)
    key_split = key_rows.reshape(keys_here, head_count, HD)
    value_split = value_rows.reshape(keys_here, head_count, HD)
    query_parts = []
    key_parts = []
    value_parts = []
    for kv_group in range(head_count):
        query_head = query_split[:, kv_group]
        grad_head = grad_split[:, kv_group]
        key_head = key_split[:, kv_group]
        value_head = value_split[:, kv_group]
        scores = (
            jnp.einsum("qgd,kd->gqk", query_head, key_head, preferred_element_type=jnp.float32)
            * score_scale
        )
        masked = jnp.where(visible[None], scores, -1e30)
        highest = jnp.max(masked, axis=-1, keepdims=True)
        weights = jnp.where(visible[None], jnp.exp(masked - highest), 0.0)
        attention = weights / jnp.sum(weights, axis=-1, keepdims=True)
        attention_low = attention.astype(jnp.bfloat16)
        prob_grad = jnp.einsum(
            "qgd,kd->gqk", grad_head, value_head, preferred_element_type=jnp.float32
        )
        row_delta = jnp.sum(attention * prob_grad, axis=-1, keepdims=True)
        score_grad = attention * (prob_grad - row_delta)
        key_wide = key_head.astype(jnp.float32)
        query_wide = query_head.astype(jnp.float32)
        query_parts.append(
            jnp.einsum("gqk,kd->qgd", score_grad, key_wide, precision=high) * score_scale
        )
        key_parts.append(
            jnp.einsum("gqk,qgd->kd", score_grad, query_wide, precision=high) * score_scale
        )
        value_parts.append(
            jnp.einsum("gqk,qgd->kd", attention_low, grad_head, preferred_element_type=jnp.float32)
        )
    query_grad = jnp.stack(query_parts, axis=1).reshape(rows_here, -1)
    kv_grad = jnp.concatenate(key_parts + value_parts, axis=1)
    return (query_grad, kv_grad)


def local(layer_input, query_states, key_states, out_grad, value_weight, segment_ids, pair_split):
    layer_rows = layer_input[0]
    tok_count = layer_rows.shape[0]
    kv_width = key_states.shape[2]
    row_base = lax.axis_index("seq") * tok_count
    columns = layer_rows
    value_rows = jnp.dot(
        columns,
        lax.all_gather(value_weight, "dp", axis=0, tiled=True),
        preferred_element_type=jnp.float32,
    )
    value_low = value_rows.astype(jnp.bfloat16)
    both_states = jnp.concatenate([key_states[0], value_low], axis=1)
    extended = with_halo(both_states, (("seq", 0),), tok_count)
    key_block = extended[:, :kv_width]
    value_block = extended[:, kv_width:]
    seg_row = segment_ids[0]
    fill_ids = jnp.full((tok_count,), -1, jnp.int32)
    padded_ids = jnp.concatenate([fill_ids, seg_row, fill_ids])
    seg_key = lax.dynamic_slice_in_dim(padded_ids, row_base, tok_count + 2 * tok_count, 0)
    seg_query = lax.dynamic_slice_in_dim(seg_row, row_base, tok_count, 0)
    pair_numbers = jnp.arange(pair_split.shape[1], dtype=jnp.int32)
    split_query = jnp.sum(
        jnp.where(seg_query[:, None] == pair_numbers[None, :], pair_split[0][None, :], 0), axis=1
    )
    pos_query = row_base + jnp.arange(tok_count, dtype=jnp.int32)
    pos_key = row_base - tok_count + jnp.arange(tok_count + 2 * tok_count, dtype=jnp.int32)
    visible = (seg_key[None, :] == seg_query[:, None]) & (
        (pos_key[None, :] <= pos_query[:, None]) | (pos_key[None, :] < split_query[:, None])
    )
    query_grad, kv_grad = attend_block(
        query_states[0], key_block, value_block, out_grad[0], visible
    )
    lower_rim = kv_grad[:tok_count]
    upper_rim = kv_grad[tok_count + tok_count :]
    center = kv_grad[tok_count : tok_count + tok_count]
    from_upper = passed_along(lower_rim, "seq", -1)
    from_lower = passed_along(upper_rim, "seq", 1)
    center = center + from_upper + from_lower
    key_grad = center[:, :kv_width].astype(jnp.bfloat16)
    value_grad = center[:, kv_width:].astype(jnp.bfloat16)
    input_grad = lax.dot_general(
        value_grad,
        lax.all_gather(value_weight, "dp", axis=0, tiled=True),
        (((1,), (1,)), ((), ())),
        preferred_element_type=jnp.float32,
    )
    dp_count = lax.axis_size("dp")
    model_width = layer_rows.shape[1]
    input_blocks = lax.all_to_all(
        layer_rows.reshape(tok_count, dp_count, model_width // dp_count).transpose(1, 0, 2),
        "dp",
        0,
        0,
        tiled=True,
    )
    grad_rows = lax.all_gather(value_grad, "dp", axis=0, tiled=False)
    own_rows = jnp.einsum(
        "rtk,rtc->kc", input_blocks, grad_rows, preferred_element_type=jnp.float32
    )
    summed = lax.psum_scatter(own_rows, "seq", scatter_dimension=1, tiled=True)
    devices_all = lax.axis_size("dp") * lax.axis_size("seq")
    weight_grad = summed / devices_all
    return (
        query_grad.astype(jnp.bfloat16)[None],
        key_grad[None],
        input_grad.astype(jnp.bfloat16)[None],
        weight_grad,
    )


def solution(mesh):
    return jax.shard_map(
        local,
        mesh=mesh,
        in_specs=(
            P("dp", "seq", None),
            P("dp", "seq", None),
            P("dp", "seq", None),
            P("dp", "seq", None),
            P("dp", None),
            P("dp", None),
            P("dp", None),
        ),
        out_specs=(
            P("dp", "seq", None),
            P("dp", "seq", None),
            P("dp", "seq", None),
            P("dp", "seq"),
        ),
        check_vma=False,
    )
```

```python
import jax
import jax.numpy as jnp
from jax import lax
from jax.sharding import PartitionSpec as P

HD = 128


def with_halo(cells, sides, width):
    for axis, dim in sides:
        count = lax.axis_size(axis)
        ends = count - 1
        head = lax.slice_in_dim(cells, 0, width, axis=dim)
        tail = lax.slice_in_dim(cells, cells.shape[dim] - width, cells.shape[dim], axis=dim)
        cells = jnp.concatenate(
            [
                lax.ppermute(tail, axis, [(i, (i + 1) % count) for i in range(ends)]),
                cells,
                lax.ppermute(head, axis, [((i + 1) % count, i) for i in range(ends)]),
            ],
            axis=dim,
        )
    return cells


def gathered(array, axis):
    count = lax.axis_size(axis)
    copies = jnp.broadcast_to(array[None], (count,) + array.shape)
    return lax.all_to_all(copies, axis, 0, 0, tiled=True)


def scattered_sum(array, axis):
    count = lax.axis_size(axis)
    rows, cols = array.shape
    pieces = array.reshape(rows, count, cols // count).transpose(1, 0, 2)
    return jnp.sum(lax.all_to_all(pieces, axis, 0, 0, tiled=True), axis=0)


def passed_along(array, axis, by):
    count = lax.axis_size(axis)
    pairs = [(i, i + by) for i in range(count) if 0 <= i + by < count]
    return lax.ppermute(array, axis, pairs)


def attend_block(query_rows, key_rows, value_rows, grad_rows, visible):
    rows_here = query_rows.shape[0]
    keys_here = key_rows.shape[0]
    head_count = key_rows.shape[1] // HD
    group_size = query_rows.shape[1] // key_rows.shape[1]
    score_scale = HD ** (-0.5)
    high = lax.Precision.HIGHEST
    query_split = query_rows.reshape(rows_here, head_count, group_size, HD)
    grad_split = grad_rows.reshape(rows_here, head_count, group_size, HD)
    key_split = key_rows.reshape(keys_here, head_count, HD)
    value_split = value_rows.reshape(keys_here, head_count, HD)
    query_parts = []
    key_parts = []
    value_parts = []
    for kv_group in range(head_count):
        query_head = query_split[:, kv_group]
        grad_head = grad_split[:, kv_group]
        key_head = key_split[:, kv_group]
        value_head = value_split[:, kv_group]
        scores = (
            jnp.einsum("qgd,kd->gqk", query_head, key_head, preferred_element_type=jnp.float32)
            * score_scale
        )
        masked = jnp.where(visible[None], scores, -1e30)
        highest = jnp.max(masked, axis=-1, keepdims=True)
        weights = jnp.where(visible[None], jnp.exp(masked - highest), 0.0)
        attention = weights / jnp.sum(weights, axis=-1, keepdims=True)
        attention_low = attention.astype(jnp.bfloat16)
        prob_grad = jnp.einsum(
            "qgd,kd->gqk", grad_head, value_head, preferred_element_type=jnp.float32
        )
        row_delta = jnp.sum(attention * prob_grad, axis=-1, keepdims=True)
        score_grad = attention * (prob_grad - row_delta)
        key_wide = key_head.astype(jnp.float32)
        query_wide = query_head.astype(jnp.float32)
        query_parts.append(
            jnp.einsum("gqk,kd->qgd", score_grad, key_wide, precision=high) * score_scale
        )
        key_parts.append(
            jnp.einsum("gqk,qgd->kd", score_grad, query_wide, precision=high) * score_scale
        )
        value_parts.append(
            jnp.einsum("gqk,qgd->kd", attention_low, grad_head, preferred_element_type=jnp.float32)
        )
    query_grad = jnp.stack(query_parts, axis=1).reshape(rows_here, -1)
    kv_grad = jnp.concatenate(key_parts + value_parts, axis=1)
    return (query_grad, kv_grad)


def local(layer_input, query_states, key_states, out_grad, value_weight, segment_ids, pair_split):
    layer_rows = layer_input[0]
    tok_count = layer_rows.shape[0]
    kv_width = key_states.shape[2]
    row_base = lax.axis_index("seq") * tok_count
    columns = layer_rows
    weight_full = gathered(value_weight, "dp").reshape(-1, value_weight.shape[1])
    value_rows = jnp.dot(columns, weight_full, preferred_element_type=jnp.float32)
    value_low = value_rows.astype(jnp.bfloat16)
    both_states = jnp.concatenate([key_states[0], value_low], axis=1)
    extended = with_halo(both_states, (("seq", 0),), tok_count)
    key_block = extended[:, :kv_width]
    value_block = extended[:, kv_width:]
    seg_row = segment_ids[0]
    fill_ids = jnp.full((tok_count,), -1, jnp.int32)
    padded_ids = jnp.concatenate([fill_ids, seg_row, fill_ids])
    seg_key = lax.dynamic_slice_in_dim(padded_ids, row_base, tok_count + 2 * tok_count, 0)
    seg_query = lax.dynamic_slice_in_dim(seg_row, row_base, tok_count, 0)
    pair_numbers = jnp.arange(pair_split.shape[1], dtype=jnp.int32)
    split_query = jnp.sum(
        jnp.where(seg_query[:, None] == pair_numbers[None, :], pair_split[0][None, :], 0), axis=1
    )
    pos_query = row_base + jnp.arange(tok_count, dtype=jnp.int32)
    pos_key = row_base - tok_count + jnp.arange(tok_count + 2 * tok_count, dtype=jnp.int32)
    visible = (seg_key[None, :] == seg_query[:, None]) & (
        (pos_key[None, :] <= pos_query[:, None]) | (pos_key[None, :] < split_query[:, None])
    )
    query_grad, kv_grad = attend_block(
        query_states[0], key_block, value_block, out_grad[0], visible
    )
    lower_rim = kv_grad[:tok_count]
    upper_rim = kv_grad[tok_count + tok_count :]
    center = kv_grad[tok_count : tok_count + tok_count]
    from_upper = passed_along(lower_rim, "seq", -1)
    from_lower = passed_along(upper_rim, "seq", 1)
    center = center + from_upper + from_lower
    key_grad = center[:, :kv_width].astype(jnp.bfloat16)
    value_grad = center[:, kv_width:].astype(jnp.bfloat16)
    input_grad = lax.dot_general(
        value_grad,
        weight_full,
        (((1,), (1,)), ((), ())),
        preferred_element_type=jnp.float32,
    )
    dp_count = lax.axis_size("dp")
    model_width = layer_rows.shape[1]
    input_blocks = lax.all_to_all(
        layer_rows.reshape(tok_count, dp_count, model_width // dp_count).transpose(1, 0, 2),
        "dp",
        0,
        0,
        tiled=True,
    )
    grad_rows = gathered(value_grad, "dp")
    own_rows = jnp.einsum(
        "rtk,rtc->kc", input_blocks, grad_rows, preferred_element_type=jnp.float32
    )
    summed = scattered_sum(own_rows, "seq")
    devices_all = lax.axis_size("dp") * lax.axis_size("seq")
    weight_grad = summed / devices_all
    return (
        query_grad.astype(jnp.bfloat16)[None],
        key_grad[None],
        input_grad.astype(jnp.bfloat16)[None],
        weight_grad,
    )


def solution(mesh):
    return jax.shard_map(
        local,
        mesh=mesh,
        in_specs=(
            P("dp", "seq", None),
            P("dp", "seq", None),
            P("dp", "seq", None),
            P("dp", "seq", None),
            P("dp", None),
            P("dp", None),
            P("dp", None),
        ),
        out_specs=(
            P("dp", "seq", None),
            P("dp", "seq", None),
            P("dp", "seq", None),
            P("dp", "seq"),
        ),
        check_vma=False,
    )
```

```python
import jax
import jax.numpy as jnp
from jax import lax
from jax.sharding import PartitionSpec as P

HD = 128


def with_halo(cells, sides, width):
    for axis, dim in sides:
        count = lax.axis_size(axis)
        ends = count - 1
        head = lax.slice_in_dim(cells, 0, width, axis=dim)
        tail = lax.slice_in_dim(cells, cells.shape[dim] - width, cells.shape[dim], axis=dim)
        cells = jnp.concatenate(
            [
                lax.ppermute(tail, axis, [(i, (i + 1) % count) for i in range(ends)]),
                cells,
                lax.ppermute(head, axis, [((i + 1) % count, i) for i in range(ends)]),
            ],
            axis=dim,
        )
    return cells


def gathered(array, axis):
    count = lax.axis_size(axis)
    copies = jnp.broadcast_to(array[None], (count,) + array.shape)
    return lax.all_to_all(copies, axis, 0, 0, tiled=True)


def scattered_sum(array, axis):
    count = lax.axis_size(axis)
    rows, cols = array.shape
    pieces = array.reshape(rows, count, cols // count).transpose(1, 0, 2)
    return jnp.sum(lax.all_to_all(pieces, axis, 0, 0, tiled=True), axis=0)


def passed_along(array, axis, by):
    count = lax.axis_size(axis)
    pairs = [(i, i + by) for i in range(count) if 0 <= i + by < count]
    return lax.ppermute(array, axis, pairs)


def split_heads(query_rows, key_rows):
    rows_here = query_rows.shape[0]
    keys_here = key_rows.shape[0]
    head_count = key_rows.shape[1] // HD
    group_size = query_rows.shape[1] // key_rows.shape[1]
    return rows_here, keys_here, head_count, group_size


def attend_first(query_rows, key_rows, grad_rows, visible):
    rows_here, keys_here, head_count, group_size = split_heads(query_rows, key_rows)
    score_scale = HD ** (-0.5)
    query_split = query_rows.reshape(rows_here, head_count, group_size, HD)
    grad_split = grad_rows.reshape(rows_here, head_count, group_size, HD)
    key_split = key_rows.reshape(keys_here, head_count, HD)
    attentions = []
    value_parts = []
    for kv_group in range(head_count):
        query_head = query_split[:, kv_group]
        grad_head = grad_split[:, kv_group]
        key_head = key_split[:, kv_group]
        scores = (
            jnp.einsum("qgd,kd->gqk", query_head, key_head, preferred_element_type=jnp.float32)
            * score_scale
        )
        masked = jnp.where(visible[None], scores, -1e30)
        highest = jnp.max(masked, axis=-1, keepdims=True)
        weights = jnp.where(visible[None], jnp.exp(masked - highest), 0.0)
        attention = weights / jnp.sum(weights, axis=-1, keepdims=True)
        attention_low = attention.astype(jnp.bfloat16)
        attentions.append(attention)
        value_parts.append(
            jnp.einsum("gqk,qgd->kd", attention_low, grad_head, preferred_element_type=jnp.float32)
        )
    return attentions, jnp.concatenate(value_parts, axis=1)


def attend_second(query_rows, key_rows, value_rows, grad_rows, attentions):
    rows_here, keys_here, head_count, group_size = split_heads(query_rows, key_rows)
    score_scale = HD ** (-0.5)
    high = lax.Precision.HIGHEST
    query_split = query_rows.reshape(rows_here, head_count, group_size, HD)
    grad_split = grad_rows.reshape(rows_here, head_count, group_size, HD)
    key_split = key_rows.reshape(keys_here, head_count, HD)
    value_split = value_rows.reshape(keys_here, head_count, HD)
    query_parts = []
    key_parts = []
    for kv_group in range(head_count):
        query_head = query_split[:, kv_group]
        grad_head = grad_split[:, kv_group]
        key_head = key_split[:, kv_group]
        value_head = value_split[:, kv_group]
        attention = attentions[kv_group]
        prob_grad = jnp.einsum(
            "qgd,kd->gqk", grad_head, value_head, preferred_element_type=jnp.float32
        )
        row_delta = jnp.sum(attention * prob_grad, axis=-1, keepdims=True)
        score_grad = attention * (prob_grad - row_delta)
        key_wide = key_head.astype(jnp.float32)
        query_wide = query_head.astype(jnp.float32)
        query_parts.append(
            jnp.einsum("gqk,kd->qgd", score_grad, key_wide, precision=high) * score_scale
        )
        key_parts.append(
            jnp.einsum("gqk,qgd->kd", score_grad, query_wide, precision=high) * score_scale
        )
    query_grad = jnp.stack(query_parts, axis=1).reshape(rows_here, -1)
    return query_grad, jnp.concatenate(key_parts, axis=1)


def rim_sum(grad_block, tok_count):
    lower_rim = grad_block[:tok_count]
    upper_rim = grad_block[tok_count + tok_count :]
    center = grad_block[tok_count : tok_count + tok_count]
    from_upper = passed_along(lower_rim, "seq", -1)
    from_lower = passed_along(upper_rim, "seq", 1)
    return center + from_upper + from_lower


def local(layer_input, query_states, key_states, out_grad, value_weight, segment_ids, pair_split):
    layer_rows = layer_input[0]
    tok_count = layer_rows.shape[0]
    row_base = lax.axis_index("seq") * tok_count
    dp_count = lax.axis_size("dp")
    model_width = layer_rows.shape[1]
    weight_rows, kv_width = value_weight.shape
    weight_copies = jnp.broadcast_to(value_weight[None], (dp_count, weight_rows, kv_width))
    input_pieces = (
        layer_rows.reshape(tok_count, dp_count, model_width // dp_count)
        .transpose(1, 0, 2)
        .reshape(dp_count, -1, kv_width)
    )
    arrived = lax.all_to_all(
        jnp.concatenate([weight_copies, input_pieces], axis=1), "dp", 0, 0, tiled=True
    )
    weight_full = arrived[:, :weight_rows].reshape(-1, kv_width)
    input_blocks = arrived[:, weight_rows:].reshape(dp_count, tok_count, -1)
    key_block = with_halo(key_states[0], (("seq", 0),), tok_count)
    seg_row = segment_ids[0]
    fill_ids = jnp.full((tok_count,), -1, jnp.int32)
    padded_ids = jnp.concatenate([fill_ids, seg_row, fill_ids])
    seg_key = lax.dynamic_slice_in_dim(padded_ids, row_base, tok_count + 2 * tok_count, 0)
    seg_query = lax.dynamic_slice_in_dim(seg_row, row_base, tok_count, 0)
    pair_numbers = jnp.arange(pair_split.shape[1], dtype=jnp.int32)
    split_query = jnp.sum(
        jnp.where(seg_query[:, None] == pair_numbers[None, :], pair_split[0][None, :], 0), axis=1
    )
    pos_query = row_base + jnp.arange(tok_count, dtype=jnp.int32)
    pos_key = row_base - tok_count + jnp.arange(tok_count + 2 * tok_count, dtype=jnp.int32)
    visible = (seg_key[None, :] == seg_query[:, None]) & (
        (pos_key[None, :] <= pos_query[:, None]) | (pos_key[None, :] < split_query[:, None])
    )
    attentions, value_part = attend_first(query_states[0], key_block, out_grad[0], visible)
    value_grad = rim_sum(value_part, tok_count).astype(jnp.bfloat16)
    grad_rows = gathered(value_grad, "dp")
    own_rows = jnp.einsum(
        "rtk,rtc->kc", input_blocks, grad_rows, preferred_element_type=jnp.float32
    )
    summed = scattered_sum(own_rows, "seq")
    devices_all = lax.axis_size("dp") * lax.axis_size("seq")
    weight_grad = summed / devices_all
    value_rows = jnp.dot(layer_rows, weight_full, preferred_element_type=jnp.float32)
    value_block = with_halo(value_rows.astype(jnp.bfloat16), (("seq", 0),), tok_count)
    query_grad, key_part = attend_second(
        query_states[0], key_block, value_block, out_grad[0], attentions
    )
    key_grad = rim_sum(key_part, tok_count).astype(jnp.bfloat16)
    input_grad = lax.dot_general(
        value_grad,
        weight_full,
        (((1,), (1,)), ((), ())),
        preferred_element_type=jnp.float32,
    )
    return (
        query_grad.astype(jnp.bfloat16)[None],
        key_grad[None],
        input_grad.astype(jnp.bfloat16)[None],
        weight_grad,
    )


def solution(mesh):
    return jax.shard_map(
        local,
        mesh=mesh,
        in_specs=(
            P("dp", "seq", None),
            P("dp", "seq", None),
            P("dp", "seq", None),
            P("dp", "seq", None),
            P("dp", None),
            P("dp", None),
            P("dp", None),
        ),
        out_specs=(
            P("dp", "seq", None),
            P("dp", "seq", None),
            P("dp", "seq", None),
            P("dp", "seq"),
        ),
        check_vma=False,
    )
```

```python
import jax
import jax.numpy as jnp
from jax import lax
from jax.sharding import PartitionSpec as P

HD = 128


def with_halo(cells, sides, width):
    for axis, dim in sides:
        count = lax.axis_size(axis)
        ends = count - 1
        head = lax.slice_in_dim(cells, 0, width, axis=dim)
        tail = lax.slice_in_dim(cells, cells.shape[dim] - width, cells.shape[dim], axis=dim)
        cells = jnp.concatenate(
            [
                lax.ppermute(tail, axis, [(i, (i + 1) % count) for i in range(ends)]),
                cells,
                lax.ppermute(head, axis, [((i + 1) % count, i) for i in range(ends)]),
            ],
            axis=dim,
        )
    return cells


def gathered(array, axis):
    count = lax.axis_size(axis)
    copies = jnp.broadcast_to(array[None], (count,) + array.shape)
    return lax.all_to_all(copies, axis, 0, 0, tiled=True)


def gathered_copies(copies, axis):
    return lax.all_to_all(copies, axis, 0, 0, tiled=True)


def scattered_sum(array, axis):
    count = lax.axis_size(axis)
    rows, cols = array.shape
    pieces = array.reshape(rows, count, cols // count).transpose(1, 0, 2)
    return jnp.sum(lax.all_to_all(pieces, axis, 0, 0, tiled=True), axis=0)


def passed_along(array, axis, by):
    count = lax.axis_size(axis)
    pairs = [(i, i + by) for i in range(count) if 0 <= i + by < count]
    return lax.ppermute(array, axis, pairs)


def split_heads(query_rows, key_rows):
    rows_here = query_rows.shape[0]
    keys_here = key_rows.shape[0]
    head_count = key_rows.shape[1] // HD
    group_size = query_rows.shape[1] // key_rows.shape[1]
    return rows_here, keys_here, head_count, group_size


def attend_first(query_rows, key_rows, grad_rows, visible):
    rows_here, keys_here, head_count, group_size = split_heads(query_rows, key_rows)
    score_scale = HD ** (-0.5)
    query_split = query_rows.reshape(rows_here, head_count, group_size, HD)
    grad_split = grad_rows.reshape(rows_here, head_count, group_size, HD)
    key_split = key_rows.reshape(keys_here, head_count, HD)
    attentions = []
    value_parts = []
    for kv_group in range(head_count):
        query_head = query_split[:, kv_group]
        grad_head = grad_split[:, kv_group]
        key_head = key_split[:, kv_group]
        scores = (
            jnp.einsum("qgd,kd->gqk", query_head, key_head, preferred_element_type=jnp.float32)
            * score_scale
        )
        masked = jnp.where(visible[None], scores, -1e30)
        highest = jnp.max(masked, axis=-1, keepdims=True)
        weights = jnp.where(visible[None], jnp.exp(masked - highest), 0.0)
        attention = weights / jnp.sum(weights, axis=-1, keepdims=True)
        attention_low = attention.astype(jnp.bfloat16)
        attentions.append(attention)
        value_parts.append(
            jnp.einsum("gqk,qgd->kd", attention_low, grad_head, preferred_element_type=jnp.float32)
        )
    return attentions, jnp.concatenate(value_parts, axis=1)


def attend_second(query_rows, key_rows, value_rows, grad_rows, attentions):
    rows_here, keys_here, head_count, group_size = split_heads(query_rows, key_rows)
    score_scale = HD ** (-0.5)
    high = lax.Precision.HIGHEST
    query_split = query_rows.reshape(rows_here, head_count, group_size, HD)
    grad_split = grad_rows.reshape(rows_here, head_count, group_size, HD)
    key_split = key_rows.reshape(keys_here, head_count, HD)
    value_split = value_rows.reshape(keys_here, head_count, HD)
    query_parts = []
    key_parts = []
    for kv_group in range(head_count):
        query_head = query_split[:, kv_group]
        grad_head = grad_split[:, kv_group]
        key_head = key_split[:, kv_group]
        value_head = value_split[:, kv_group]
        attention = attentions[kv_group]
        prob_grad = jnp.einsum(
            "qgd,kd->gqk", grad_head, value_head, preferred_element_type=jnp.float32
        )
        row_delta = jnp.sum(attention * prob_grad, axis=-1, keepdims=True)
        score_grad = attention * (prob_grad - row_delta)
        key_wide = key_head.astype(jnp.float32)
        query_wide = query_head.astype(jnp.float32)
        query_parts.append(
            jnp.einsum("gqk,kd->qgd", score_grad, key_wide, precision=high) * score_scale
        )
        key_parts.append(
            jnp.einsum("gqk,qgd->kd", score_grad, query_wide, precision=high) * score_scale
        )
    query_grad = jnp.stack(query_parts, axis=1).reshape(rows_here, -1)
    return query_grad, jnp.concatenate(key_parts, axis=1)


def rim_sum(grad_block, tok_count):
    lower_rim = grad_block[:tok_count]
    upper_rim = grad_block[tok_count + tok_count :]
    center = grad_block[tok_count : tok_count + tok_count]
    from_upper = passed_along(lower_rim, "seq", -1)
    from_lower = passed_along(upper_rim, "seq", 1)
    return center + from_upper + from_lower


def local(layer_input, query_states, key_states, out_grad, value_weight, segment_ids, pair_split):
    layer_rows = layer_input[0]
    tok_count = layer_rows.shape[0]
    row_base = lax.axis_index("seq") * tok_count
    dp_count = lax.axis_size("dp")
    model_width = layer_rows.shape[1]
    weight_rows, kv_width = value_weight.shape
    key_block = with_halo(key_states[0], (("seq", 0),), tok_count)
    weight_copies = jnp.broadcast_to(value_weight[None], (dp_count, weight_rows, kv_width))
    key_block, weight_copies = lax.optimization_barrier((key_block, weight_copies))
    weight_full = gathered_copies(weight_copies, "dp").reshape(-1, kv_width)
    input_pieces = (
        layer_rows.reshape(tok_count, dp_count, model_width // dp_count)
        .transpose(1, 0, 2)
        .reshape(dp_count, -1, kv_width)
    )
    seg_row = segment_ids[0]
    fill_ids = jnp.full((tok_count,), -1, jnp.int32)
    padded_ids = jnp.concatenate([fill_ids, seg_row, fill_ids])
    seg_key = lax.dynamic_slice_in_dim(padded_ids, row_base, tok_count + 2 * tok_count, 0)
    seg_query = lax.dynamic_slice_in_dim(seg_row, row_base, tok_count, 0)
    pair_numbers = jnp.arange(pair_split.shape[1], dtype=jnp.int32)
    split_query = jnp.sum(
        jnp.where(seg_query[:, None] == pair_numbers[None, :], pair_split[0][None, :], 0), axis=1
    )
    pos_query = row_base + jnp.arange(tok_count, dtype=jnp.int32)
    pos_key = row_base - tok_count + jnp.arange(tok_count + 2 * tok_count, dtype=jnp.int32)
    visible = (seg_key[None, :] == seg_query[:, None]) & (
        (pos_key[None, :] <= pos_query[:, None]) | (pos_key[None, :] < split_query[:, None])
    )
    attentions, value_part = attend_first(query_states[0], key_block, out_grad[0], visible)
    value_grad = rim_sum(value_part, tok_count).astype(jnp.bfloat16)
    value_grad, weight_full = lax.optimization_barrier((value_grad, weight_full))
    grad_copies = jnp.broadcast_to(value_grad[None], (dp_count,) + value_grad.shape)
    arrived = gathered_copies(jnp.concatenate([grad_copies, input_pieces], axis=1), "dp")
    grad_rows = arrived[:, :tok_count]
    input_blocks = arrived[:, tok_count:].reshape(dp_count, tok_count, -1)
    own_rows = jnp.einsum(
        "rtk,rtc->kc", input_blocks, grad_rows, preferred_element_type=jnp.float32
    )
    summed = scattered_sum(own_rows, "seq")
    devices_all = lax.axis_size("dp") * lax.axis_size("seq")
    weight_grad = summed / devices_all
    value_rows = jnp.dot(layer_rows, weight_full, preferred_element_type=jnp.float32)
    value_block = with_halo(value_rows.astype(jnp.bfloat16), (("seq", 0),), tok_count)
    query_grad, key_part = attend_second(
        query_states[0], key_block, value_block, out_grad[0], attentions
    )
    key_grad = rim_sum(key_part, tok_count).astype(jnp.bfloat16)
    input_grad = lax.dot_general(
        value_grad,
        weight_full,
        (((1,), (1,)), ((), ())),
        preferred_element_type=jnp.float32,
    )
    return (
        query_grad.astype(jnp.bfloat16)[None],
        key_grad[None],
        input_grad.astype(jnp.bfloat16)[None],
        weight_grad,
    )


def solution(mesh):
    return jax.shard_map(
        local,
        mesh=mesh,
        in_specs=(
            P("dp", "seq", None),
            P("dp", "seq", None),
            P("dp", "seq", None),
            P("dp", "seq", None),
            P("dp", None),
            P("dp", None),
            P("dp", None),
        ),
        out_specs=(
            P("dp", "seq", None),
            P("dp", "seq", None),
            P("dp", "seq", None),
            P("dp", "seq"),
        ),
        check_vma=False,
    )
```

```python
import jax
import jax.numpy as jnp
from jax import lax
from jax.sharding import PartitionSpec as P

HD = 128


def with_halo(cells, sides, width):
    for axis, dim in sides:
        count = lax.axis_size(axis)
        ends = count - 1
        head = lax.slice_in_dim(cells, 0, width, axis=dim)
        tail = lax.slice_in_dim(cells, cells.shape[dim] - width, cells.shape[dim], axis=dim)
        cells = jnp.concatenate(
            [
                lax.ppermute(tail, axis, [(i, (i + 1) % count) for i in range(ends)]),
                cells,
                lax.ppermute(head, axis, [((i + 1) % count, i) for i in range(ends)]),
            ],
            axis=dim,
        )
    return cells


def gathered(array, axis):
    count = lax.axis_size(axis)
    copies = jnp.broadcast_to(array[None], (count,) + array.shape)
    return lax.all_to_all(copies, axis, 0, 0, tiled=True)


def gathered_copies(copies, axis):
    return lax.all_to_all(copies, axis, 0, 0, tiled=True)


def scattered_sum(array, axis):
    count = lax.axis_size(axis)
    rows, cols = array.shape
    pieces = array.reshape(rows, count, cols // count).transpose(1, 0, 2)
    return jnp.sum(lax.all_to_all(pieces, axis, 0, 0, tiled=True), axis=0)


def passed_along(array, axis, by):
    count = lax.axis_size(axis)
    pairs = [(i, i + by) for i in range(count) if 0 <= i + by < count]
    return lax.ppermute(array, axis, pairs)


def split_heads(query_rows, key_rows):
    rows_here = query_rows.shape[0]
    keys_here = key_rows.shape[0]
    head_count = key_rows.shape[1] // HD
    group_size = query_rows.shape[1] // key_rows.shape[1]
    return rows_here, keys_here, head_count, group_size


def attend_first(query_rows, key_rows, grad_rows, visible):
    rows_here, keys_here, head_count, group_size = split_heads(query_rows, key_rows)
    score_scale = HD ** (-0.5)
    query_split = query_rows.reshape(rows_here, head_count, group_size, HD)
    grad_split = grad_rows.reshape(rows_here, head_count, group_size, HD)
    key_split = key_rows.reshape(keys_here, head_count, HD)
    attentions = []
    value_parts = []
    for kv_group in range(head_count):
        query_head = query_split[:, kv_group]
        grad_head = grad_split[:, kv_group]
        key_head = key_split[:, kv_group]
        scores = (
            jnp.einsum("qgd,kd->gqk", query_head, key_head, preferred_element_type=jnp.float32)
            * score_scale
        )
        masked = jnp.where(visible[None], scores, -1e30)
        highest = jnp.max(masked, axis=-1, keepdims=True)
        weights = jnp.where(visible[None], jnp.exp(masked - highest), 0.0)
        attention = weights / jnp.sum(weights, axis=-1, keepdims=True)
        attention_low = attention.astype(jnp.bfloat16)
        attentions.append(attention)
        value_parts.append(
            jnp.einsum("gqk,qgd->kd", attention_low, grad_head, preferred_element_type=jnp.float32)
        )
    return attentions, jnp.concatenate(value_parts, axis=1)


def attend_second(query_rows, key_rows, value_rows, grad_rows, attentions):
    rows_here, keys_here, head_count, group_size = split_heads(query_rows, key_rows)
    score_scale = HD ** (-0.5)
    high = lax.Precision.HIGHEST
    query_split = query_rows.reshape(rows_here, head_count, group_size, HD)
    grad_split = grad_rows.reshape(rows_here, head_count, group_size, HD)
    key_split = key_rows.reshape(keys_here, head_count, HD)
    value_split = value_rows.reshape(keys_here, head_count, HD)
    query_parts = []
    key_parts = []
    for kv_group in range(head_count):
        query_head = query_split[:, kv_group]
        grad_head = grad_split[:, kv_group]
        key_head = key_split[:, kv_group]
        value_head = value_split[:, kv_group]
        attention = attentions[kv_group]
        prob_grad = jnp.einsum(
            "qgd,kd->gqk", grad_head, value_head, preferred_element_type=jnp.float32
        )
        row_delta = jnp.sum(attention * prob_grad, axis=-1, keepdims=True)
        score_grad = attention * (prob_grad - row_delta)
        key_wide = key_head.astype(jnp.float32)
        query_wide = query_head.astype(jnp.float32)
        query_parts.append(
            jnp.einsum("gqk,kd->qgd", score_grad, key_wide, precision=high) * score_scale
        )
        key_parts.append(
            jnp.einsum("gqk,qgd->kd", score_grad, query_wide, precision=high) * score_scale
        )
    query_grad = jnp.stack(query_parts, axis=1).reshape(rows_here, -1)
    return query_grad, jnp.concatenate(key_parts, axis=1)


def rim_sum(grad_block, tok_count):
    lower_rim = grad_block[:tok_count]
    upper_rim = grad_block[tok_count + tok_count :]
    center = grad_block[tok_count : tok_count + tok_count]
    from_upper = passed_along(lower_rim, "seq", -1)
    from_lower = passed_along(upper_rim, "seq", 1)
    return center + from_upper + from_lower


def local(layer_input, query_states, key_states, out_grad, value_weight, segment_ids, pair_split):
    layer_rows = layer_input[0]
    tok_count = layer_rows.shape[0]
    row_base = lax.axis_index("seq") * tok_count
    dp_count = lax.axis_size("dp")
    model_width = layer_rows.shape[1]
    weight_rows, kv_width = value_weight.shape
    key_block = with_halo(key_states[0], (("seq", 0),), tok_count)
    weight_copies = jnp.broadcast_to(value_weight[None], (dp_count, weight_rows, kv_width))
    key_block, weight_copies = lax.optimization_barrier((key_block, weight_copies))
    weight_full = gathered_copies(weight_copies, "dp").reshape(-1, kv_width)
    input_pieces = layer_rows.reshape(tok_count, dp_count, model_width // dp_count).transpose(1, 0, 2)
    seg_row = segment_ids[0]
    fill_ids = jnp.full((tok_count,), -1, jnp.int32)
    padded_ids = jnp.concatenate([fill_ids, seg_row, fill_ids])
    seg_key = lax.dynamic_slice_in_dim(padded_ids, row_base, tok_count + 2 * tok_count, 0)
    seg_query = lax.dynamic_slice_in_dim(seg_row, row_base, tok_count, 0)
    pair_numbers = jnp.arange(pair_split.shape[1], dtype=jnp.int32)
    split_query = jnp.sum(
        jnp.where(seg_query[:, None] == pair_numbers[None, :], pair_split[0][None, :], 0), axis=1
    )
    pos_query = row_base + jnp.arange(tok_count, dtype=jnp.int32)
    pos_key = row_base - tok_count + jnp.arange(tok_count + 2 * tok_count, dtype=jnp.int32)
    visible = (seg_key[None, :] == seg_query[:, None]) & (
        (pos_key[None, :] <= pos_query[:, None]) | (pos_key[None, :] < split_query[:, None])
    )
    attentions, value_part = attend_first(query_states[0], key_block, out_grad[0], visible)
    value_grad = rim_sum(value_part, tok_count).astype(jnp.bfloat16)
    value_grad, weight_full = lax.optimization_barrier((value_grad, weight_full))
    grad_copies = jnp.broadcast_to(value_grad[None], (dp_count,) + value_grad.shape)
    arrived = gathered_copies(jnp.concatenate([grad_copies, input_pieces], axis=2), "dp")
    seq_count = lax.axis_size("seq")
    grad_rows = arrived[:, :, :kv_width].reshape(dp_count, tok_count, seq_count, -1)
    input_blocks = arrived[:, :, kv_width:]
    own_pieces = jnp.einsum(
        "rtk,rtjc->jkc", input_blocks, grad_rows, preferred_element_type=jnp.float32
    )
    summed = jnp.sum(gathered_copies(own_pieces, "seq"), axis=0)
    devices_all = lax.axis_size("dp") * lax.axis_size("seq")
    weight_grad = summed / devices_all
    value_rows = jnp.dot(layer_rows, weight_full, preferred_element_type=jnp.float32)
    value_block = with_halo(value_rows.astype(jnp.bfloat16), (("seq", 0),), tok_count)
    query_grad, key_part = attend_second(
        query_states[0], key_block, value_block, out_grad[0], attentions
    )
    key_grad = rim_sum(key_part, tok_count).astype(jnp.bfloat16)
    input_grad = lax.dot_general(
        value_grad,
        weight_full,
        (((1,), (1,)), ((), ())),
        preferred_element_type=jnp.float32,
    )
    return (
        query_grad.astype(jnp.bfloat16)[None],
        key_grad[None],
        input_grad.astype(jnp.bfloat16)[None],
        weight_grad,
    )


def solution(mesh):
    return jax.shard_map(
        local,
        mesh=mesh,
        in_specs=(
            P("dp", "seq", None),
            P("dp", "seq", None),
            P("dp", "seq", None),
            P("dp", "seq", None),
            P("dp", None),
            P("dp", None),
            P("dp", None),
        ),
        out_specs=(
            P("dp", "seq", None),
            P("dp", "seq", None),
            P("dp", "seq", None),
            P("dp", "seq"),
        ),
        check_vma=False,
    )
```

```python
import jax
import jax.numpy as jnp
from jax import lax
from jax.sharding import PartitionSpec as P

HD = 128


def with_halo(cells, sides, width):
    for axis, dim in sides:
        count = lax.axis_size(axis)
        ends = count - 1
        head = lax.slice_in_dim(cells, 0, width, axis=dim)
        tail = lax.slice_in_dim(cells, cells.shape[dim] - width, cells.shape[dim], axis=dim)
        cells = jnp.concatenate(
            [
                lax.ppermute(tail, axis, [(i, (i + 1) % count) for i in range(ends)]),
                cells,
                lax.ppermute(head, axis, [((i + 1) % count, i) for i in range(ends)]),
            ],
            axis=dim,
        )
    return cells


def gathered(array, axis):
    count = lax.axis_size(axis)
    copies = jnp.broadcast_to(array[None], (count,) + array.shape)
    return lax.all_to_all(copies, axis, 0, 0, tiled=True)


def spread_weight(weight, ready):
    dp_count = lax.axis_size("dp")
    seq_count = lax.axis_size("seq")
    half = dp_count // 2
    cores = 2
    y_count = half // cores
    rows, width = weight.shape
    partner_pairs = [
        (d * seq_count + s, (d ^ half) * seq_count + (s ^ 1))
        for d in range(dp_count)
        for s in range(seq_count)
    ]
    held = jnp.stack([weight, lax.ppermute(weight, ("dp", "seq"), partner_pairs)])
    ring = [held]
    for shift in range(1, y_count):
        pairs = []
        for d in range(dp_count):
            upper, y_here, core = d // half, (d // cores) % y_count, d % cores
            pairs.append((d, upper * half + ((y_here + shift) % y_count) * cores + core))
        ring.append(lax.ppermute(held, "dp", pairs))
    mine, ready = lax.optimization_barrier((jnp.stack(ring), ready))
    sibling = lax.ppermute(mine, "dp", [(d, d ^ 1) for d in range(dp_count)])
    stacked = jnp.stack([mine, sibling]).reshape(dp_count, rows, width)
    me = lax.axis_index("dp")
    upper, y_here, core = me // half, (me // cores) % y_count, me % cores
    core_of = jnp.arange(2)[:, None, None]
    shift_of = jnp.arange(y_count)[None, :, None]
    upper_of = jnp.arange(2)[None, None, :]
    owner = (
        ((upper + upper_of) % 2) * half
        + ((y_here - shift_of) % y_count) * cores
        + (core + core_of) % 2
    )
    order = jnp.argsort(owner.reshape(-1))
    return jnp.take(stacked, order, axis=0).reshape(-1, width), ready


def gathered_copies(copies, axis):
    return lax.all_to_all(copies, axis, 0, 0, tiled=True)


def scattered_sum(array, axis):
    count = lax.axis_size(axis)
    rows, cols = array.shape
    pieces = array.reshape(rows, count, cols // count).transpose(1, 0, 2)
    return jnp.sum(lax.all_to_all(pieces, axis, 0, 0, tiled=True), axis=0)


def passed_along(array, axis, by):
    count = lax.axis_size(axis)
    pairs = [(i, i + by) for i in range(count) if 0 <= i + by < count]
    return lax.ppermute(array, axis, pairs)


def split_heads(query_rows, key_rows):
    rows_here = query_rows.shape[0]
    keys_here = key_rows.shape[0]
    head_count = key_rows.shape[1] // HD
    group_size = query_rows.shape[1] // key_rows.shape[1]
    return rows_here, keys_here, head_count, group_size


def attend_first(query_rows, key_rows, grad_rows, visible):
    rows_here, keys_here, head_count, group_size = split_heads(query_rows, key_rows)
    score_scale = HD ** (-0.5)
    query_split = query_rows.reshape(rows_here, head_count, group_size, HD)
    grad_split = grad_rows.reshape(rows_here, head_count, group_size, HD)
    key_split = key_rows.reshape(keys_here, head_count, HD)
    attentions = []
    value_parts = []
    for kv_group in range(head_count):
        query_head = query_split[:, kv_group]
        grad_head = grad_split[:, kv_group]
        key_head = key_split[:, kv_group]
        scores = (
            jnp.einsum("qgd,kd->gqk", query_head, key_head, preferred_element_type=jnp.float32)
            * score_scale
        )
        masked = jnp.where(visible[None], scores, -1e30)
        highest = jnp.max(masked, axis=-1, keepdims=True)
        weights = jnp.where(visible[None], jnp.exp(masked - highest), 0.0)
        attention = weights / jnp.sum(weights, axis=-1, keepdims=True)
        attention_low = attention.astype(jnp.bfloat16)
        attentions.append(attention)
        value_parts.append(
            jnp.einsum("gqk,qgd->kd", attention_low, grad_head, preferred_element_type=jnp.float32)
        )
    return attentions, jnp.concatenate(value_parts, axis=1)


def attend_second(query_rows, key_rows, value_rows, grad_rows, attentions):
    rows_here, keys_here, head_count, group_size = split_heads(query_rows, key_rows)
    score_scale = HD ** (-0.5)
    high = lax.Precision.HIGHEST
    query_split = query_rows.reshape(rows_here, head_count, group_size, HD)
    grad_split = grad_rows.reshape(rows_here, head_count, group_size, HD)
    key_split = key_rows.reshape(keys_here, head_count, HD)
    value_split = value_rows.reshape(keys_here, head_count, HD)
    query_parts = []
    key_parts = []
    for kv_group in range(head_count):
        query_head = query_split[:, kv_group]
        grad_head = grad_split[:, kv_group]
        key_head = key_split[:, kv_group]
        value_head = value_split[:, kv_group]
        attention = attentions[kv_group]
        prob_grad = jnp.einsum(
            "qgd,kd->gqk", grad_head, value_head, preferred_element_type=jnp.float32
        )
        row_delta = jnp.sum(attention * prob_grad, axis=-1, keepdims=True)
        score_grad = attention * (prob_grad - row_delta)
        key_wide = key_head.astype(jnp.float32)
        query_wide = query_head.astype(jnp.float32)
        query_parts.append(
            jnp.einsum("gqk,kd->qgd", score_grad, key_wide, precision=high) * score_scale
        )
        key_parts.append(
            jnp.einsum("gqk,qgd->kd", score_grad, query_wide, precision=high) * score_scale
        )
    query_grad = jnp.stack(query_parts, axis=1).reshape(rows_here, -1)
    return query_grad, jnp.concatenate(key_parts, axis=1)


def rim_sum(grad_block, tok_count):
    lower_rim = grad_block[:tok_count]
    upper_rim = grad_block[tok_count + tok_count :]
    center = grad_block[tok_count : tok_count + tok_count]
    from_upper = passed_along(lower_rim, "seq", -1)
    from_lower = passed_along(upper_rim, "seq", 1)
    return center + from_upper + from_lower


def local(layer_input, query_states, key_states, out_grad, value_weight, segment_ids, pair_split):
    layer_rows = layer_input[0]
    tok_count = layer_rows.shape[0]
    row_base = lax.axis_index("seq") * tok_count
    dp_count = lax.axis_size("dp")
    model_width = layer_rows.shape[1]
    weight_rows, kv_width = value_weight.shape
    key_block = with_halo(key_states[0], (("seq", 0),), tok_count)
    weight_full, key_block = spread_weight(value_weight, key_block)
    input_pieces = layer_rows.reshape(tok_count, dp_count, model_width // dp_count).transpose(1, 0, 2)
    seg_row = segment_ids[0]
    fill_ids = jnp.full((tok_count,), -1, jnp.int32)
    padded_ids = jnp.concatenate([fill_ids, seg_row, fill_ids])
    seg_key = lax.dynamic_slice_in_dim(padded_ids, row_base, tok_count + 2 * tok_count, 0)
    seg_query = lax.dynamic_slice_in_dim(seg_row, row_base, tok_count, 0)
    pair_numbers = jnp.arange(pair_split.shape[1], dtype=jnp.int32)
    split_query = jnp.sum(
        jnp.where(seg_query[:, None] == pair_numbers[None, :], pair_split[0][None, :], 0), axis=1
    )
    pos_query = row_base + jnp.arange(tok_count, dtype=jnp.int32)
    pos_key = row_base - tok_count + jnp.arange(tok_count + 2 * tok_count, dtype=jnp.int32)
    visible = (seg_key[None, :] == seg_query[:, None]) & (
        (pos_key[None, :] <= pos_query[:, None]) | (pos_key[None, :] < split_query[:, None])
    )
    attentions, value_part = attend_first(query_states[0], key_block, out_grad[0], visible)
    value_part, weight_full = lax.optimization_barrier((value_part, weight_full))
    value_grad = rim_sum(value_part, tok_count).astype(jnp.bfloat16)
    grad_copies = jnp.broadcast_to(value_grad[None], (dp_count,) + value_grad.shape)
    arrived = gathered_copies(jnp.concatenate([grad_copies, input_pieces], axis=2), "dp")
    seq_count = lax.axis_size("seq")
    grad_rows = arrived[:, :, :kv_width].reshape(dp_count, tok_count, seq_count, -1)
    input_blocks = arrived[:, :, kv_width:]
    own_pieces = jnp.einsum(
        "rtk,rtjc->jkc", input_blocks, grad_rows, preferred_element_type=jnp.float32
    )
    summed = jnp.sum(gathered_copies(own_pieces, "seq"), axis=0)
    devices_all = lax.axis_size("dp") * lax.axis_size("seq")
    weight_grad = summed / devices_all
    value_rows = jnp.dot(layer_rows, weight_full, preferred_element_type=jnp.float32)
    value_block = with_halo(value_rows.astype(jnp.bfloat16), (("seq", 0),), tok_count)
    query_grad, key_part = attend_second(
        query_states[0], key_block, value_block, out_grad[0], attentions
    )
    key_grad = rim_sum(key_part, tok_count).astype(jnp.bfloat16)
    input_grad = lax.dot_general(
        value_grad,
        weight_full,
        (((1,), (1,)), ((), ())),
        preferred_element_type=jnp.float32,
    )
    return (
        query_grad.astype(jnp.bfloat16)[None],
        key_grad[None],
        input_grad.astype(jnp.bfloat16)[None],
        weight_grad,
    )


def solution(mesh):
    return jax.shard_map(
        local,
        mesh=mesh,
        in_specs=(
            P("dp", "seq", None),
            P("dp", "seq", None),
            P("dp", "seq", None),
            P("dp", "seq", None),
            P("dp", None),
            P("dp", None),
            P("dp", None),
        ),
        out_specs=(
            P("dp", "seq", None),
            P("dp", "seq", None),
            P("dp", "seq", None),
            P("dp", "seq"),
        ),
        check_vma=False,
    )
```

```python
import jax
import jax.numpy as jnp
from jax import lax
from jax.sharding import PartitionSpec as P

HD = 128


def with_halo(cells, sides, width):
    for axis, dim in sides:
        count = lax.axis_size(axis)
        ends = count - 1
        head = lax.slice_in_dim(cells, 0, width, axis=dim)
        tail = lax.slice_in_dim(cells, cells.shape[dim] - width, cells.shape[dim], axis=dim)
        cells = jnp.concatenate(
            [
                lax.ppermute(tail, axis, [(i, (i + 1) % count) for i in range(ends)]),
                cells,
                lax.ppermute(head, axis, [((i + 1) % count, i) for i in range(ends)]),
            ],
            axis=dim,
        )
    return cells


def gathered(array, axis):
    count = lax.axis_size(axis)
    copies = jnp.broadcast_to(array[None], (count,) + array.shape)
    return lax.all_to_all(copies, axis, 0, 0, tiled=True)


def spread_weight(weight, ready):
    dp_count = lax.axis_size("dp")
    seq_count = lax.axis_size("seq")
    half = dp_count // 2
    cores = 2
    y_count = half // cores
    rows, width = weight.shape
    partner_pairs = [
        (d * seq_count + s, (d ^ half) * seq_count + (s ^ 1))
        for d in range(dp_count)
        for s in range(seq_count)
    ]
    held = jnp.stack([weight, lax.ppermute(weight, ("dp", "seq"), partner_pairs)])
    ring = [held]
    for shift in range(1, y_count):
        pairs = []
        for d in range(dp_count):
            upper, y_here, core = d // half, (d // cores) % y_count, d % cores
            pairs.append((d, upper * half + ((y_here + shift) % y_count) * cores + core))
        ring.append(lax.ppermute(held, "dp", pairs))
    mine, ready = lax.optimization_barrier((jnp.stack(ring), ready))
    sibling = lax.ppermute(mine, "dp", [(d, d ^ 1) for d in range(dp_count)])
    stacked = jnp.stack([mine, sibling]).reshape(dp_count, rows, width)
    me = lax.axis_index("dp")
    upper, y_here, core = me // half, (me // cores) % y_count, me % cores
    core_of = jnp.arange(2)[:, None, None]
    shift_of = jnp.arange(y_count)[None, :, None]
    upper_of = jnp.arange(2)[None, None, :]
    owner = (
        ((upper + upper_of) % 2) * half
        + ((y_here - shift_of) % y_count) * cores
        + (core + core_of) % 2
    )
    return stacked, owner.reshape(-1), ready


def gathered_copies(copies, axis):
    return lax.all_to_all(copies, axis, 0, 0, tiled=True)


def scattered_sum(array, axis):
    count = lax.axis_size(axis)
    rows, cols = array.shape
    pieces = array.reshape(rows, count, cols // count).transpose(1, 0, 2)
    return jnp.sum(lax.all_to_all(pieces, axis, 0, 0, tiled=True), axis=0)


def passed_along(array, axis, by):
    count = lax.axis_size(axis)
    pairs = [(i, i + by) for i in range(count) if 0 <= i + by < count]
    return lax.ppermute(array, axis, pairs)


def split_heads(query_rows, key_rows):
    rows_here = query_rows.shape[0]
    keys_here = key_rows.shape[0]
    head_count = key_rows.shape[1] // HD
    group_size = query_rows.shape[1] // key_rows.shape[1]
    return rows_here, keys_here, head_count, group_size


def attend_first(query_rows, key_rows, grad_rows, visible):
    rows_here, keys_here, head_count, group_size = split_heads(query_rows, key_rows)
    score_scale = HD ** (-0.5)
    query_split = query_rows.reshape(rows_here, head_count, group_size, HD)
    grad_split = grad_rows.reshape(rows_here, head_count, group_size, HD)
    key_split = key_rows.reshape(keys_here, head_count, HD)
    attentions = []
    value_parts = []
    for kv_group in range(head_count):
        query_head = query_split[:, kv_group]
        grad_head = grad_split[:, kv_group]
        key_head = key_split[:, kv_group]
        scores = (
            jnp.einsum("qgd,kd->gqk", query_head, key_head, preferred_element_type=jnp.float32)
            * score_scale
        )
        masked = jnp.where(visible[None], scores, -1e30)
        highest = jnp.max(masked, axis=-1, keepdims=True)
        weights = jnp.where(visible[None], jnp.exp(masked - highest), 0.0)
        attention = weights / jnp.sum(weights, axis=-1, keepdims=True)
        attention_low = attention.astype(jnp.bfloat16)
        attentions.append(attention)
        value_parts.append(
            jnp.einsum("gqk,qgd->kd", attention_low, grad_head, preferred_element_type=jnp.float32)
        )
    return attentions, jnp.concatenate(value_parts, axis=1)


def attend_second(query_rows, key_rows, value_rows, grad_rows, attentions):
    rows_here, keys_here, head_count, group_size = split_heads(query_rows, key_rows)
    score_scale = HD ** (-0.5)
    high = lax.Precision.HIGHEST
    query_split = query_rows.reshape(rows_here, head_count, group_size, HD)
    grad_split = grad_rows.reshape(rows_here, head_count, group_size, HD)
    key_split = key_rows.reshape(keys_here, head_count, HD)
    value_split = value_rows.reshape(keys_here, head_count, HD)
    query_parts = []
    key_parts = []
    for kv_group in range(head_count):
        query_head = query_split[:, kv_group]
        grad_head = grad_split[:, kv_group]
        key_head = key_split[:, kv_group]
        value_head = value_split[:, kv_group]
        attention = attentions[kv_group]
        prob_grad = jnp.einsum(
            "qgd,kd->gqk", grad_head, value_head, preferred_element_type=jnp.float32
        )
        row_delta = jnp.sum(attention * prob_grad, axis=-1, keepdims=True)
        score_grad = attention * (prob_grad - row_delta)
        key_wide = key_head.astype(jnp.float32)
        query_wide = query_head.astype(jnp.float32)
        query_parts.append(
            jnp.einsum("gqk,kd->qgd", score_grad, key_wide, precision=high) * score_scale
        )
        key_parts.append(
            jnp.einsum("gqk,qgd->kd", score_grad, query_wide, precision=high) * score_scale
        )
    query_grad = jnp.stack(query_parts, axis=1).reshape(rows_here, -1)
    return query_grad, jnp.concatenate(key_parts, axis=1)


def rim_sum(grad_block, tok_count):
    lower_rim = grad_block[:tok_count]
    upper_rim = grad_block[tok_count + tok_count :]
    center = grad_block[tok_count : tok_count + tok_count]
    from_upper = passed_along(lower_rim, "seq", -1)
    from_lower = passed_along(upper_rim, "seq", 1)
    return center + from_upper + from_lower


def local(layer_input, query_states, key_states, out_grad, value_weight, segment_ids, pair_split):
    layer_rows = layer_input[0]
    tok_count = layer_rows.shape[0]
    row_base = lax.axis_index("seq") * tok_count
    dp_count = lax.axis_size("dp")
    model_width = layer_rows.shape[1]
    weight_rows, kv_width = value_weight.shape
    key_block = with_halo(key_states[0], (("seq", 0),), tok_count)
    weight_slots, slot_owner, key_block = spread_weight(value_weight, key_block)
    input_pieces = layer_rows.reshape(tok_count, dp_count, model_width // dp_count).transpose(1, 0, 2)
    seg_row = segment_ids[0]
    fill_ids = jnp.full((tok_count,), -1, jnp.int32)
    padded_ids = jnp.concatenate([fill_ids, seg_row, fill_ids])
    seg_key = lax.dynamic_slice_in_dim(padded_ids, row_base, tok_count + 2 * tok_count, 0)
    seg_query = lax.dynamic_slice_in_dim(seg_row, row_base, tok_count, 0)
    pair_numbers = jnp.arange(pair_split.shape[1], dtype=jnp.int32)
    split_query = jnp.sum(
        jnp.where(seg_query[:, None] == pair_numbers[None, :], pair_split[0][None, :], 0), axis=1
    )
    pos_query = row_base + jnp.arange(tok_count, dtype=jnp.int32)
    pos_key = row_base - tok_count + jnp.arange(tok_count + 2 * tok_count, dtype=jnp.int32)
    visible = (seg_key[None, :] == seg_query[:, None]) & (
        (pos_key[None, :] <= pos_query[:, None]) | (pos_key[None, :] < split_query[:, None])
    )
    attentions, value_part = attend_first(query_states[0], key_block, out_grad[0], visible)
    value_grad = rim_sum(value_part, tok_count).astype(jnp.bfloat16)
    value_grad, weight_slots = lax.optimization_barrier((value_grad, weight_slots))
    weight_full = weight_slots.reshape(-1, kv_width)
    grad_copies = jnp.broadcast_to(value_grad[None], (dp_count,) + value_grad.shape)
    arrived = gathered_copies(jnp.concatenate([grad_copies, input_pieces], axis=2), "dp")
    seq_count = lax.axis_size("seq")
    grad_rows = arrived[:, :, :kv_width].reshape(dp_count, tok_count, seq_count, -1)
    input_blocks = arrived[:, :, kv_width:]
    own_pieces = jnp.einsum(
        "rtk,rtjc->jkc", input_blocks, grad_rows, preferred_element_type=jnp.float32
    )
    summed = jnp.sum(gathered_copies(own_pieces, "seq"), axis=0)
    devices_all = lax.axis_size("dp") * lax.axis_size("seq")
    weight_grad = summed / devices_all
    input_slots = jnp.take(
        layer_rows.reshape(tok_count, dp_count, -1), slot_owner, axis=1, mode="clip"
    ).reshape(tok_count, -1)
    value_rows = jnp.dot(input_slots, weight_full, preferred_element_type=jnp.float32)
    value_block = with_halo(value_rows.astype(jnp.bfloat16), (("seq", 0),), tok_count)
    query_grad, key_part = attend_second(
        query_states[0], key_block, value_block, out_grad[0], attentions
    )
    key_grad = rim_sum(key_part, tok_count).astype(jnp.bfloat16)
    grad_slots = lax.dot_general(
        value_grad,
        weight_full,
        (((1,), (1,)), ((), ())),
        preferred_element_type=jnp.float32,
    ).astype(jnp.bfloat16)
    input_grad = jnp.take(
        grad_slots.reshape(tok_count, dp_count, -1), jnp.argsort(slot_owner), axis=1, mode="clip"
    ).reshape(tok_count, -1)
    return (
        query_grad.astype(jnp.bfloat16)[None],
        key_grad[None],
        input_grad[None],
        weight_grad,
    )


def solution(mesh):
    return jax.shard_map(
        local,
        mesh=mesh,
        in_specs=(
            P("dp", "seq", None),
            P("dp", "seq", None),
            P("dp", "seq", None),
            P("dp", "seq", None),
            P("dp", None),
            P("dp", None),
            P("dp", None),
        ),
        out_specs=(
            P("dp", "seq", None),
            P("dp", "seq", None),
            P("dp", "seq", None),
            P("dp", "seq"),
        ),
        check_vma=False,
    )
```

```python
import jax
import jax.numpy as jnp
from jax import lax
from jax.sharding import PartitionSpec as P

HD = 128


def with_halo(cells, sides, width):
    for axis, dim in sides:
        count = lax.axis_size(axis)
        ends = count - 1
        head = lax.slice_in_dim(cells, 0, width, axis=dim)
        tail = lax.slice_in_dim(cells, cells.shape[dim] - width, cells.shape[dim], axis=dim)
        cells = jnp.concatenate(
            [
                lax.ppermute(tail, axis, [(i, (i + 1) % count) for i in range(ends)]),
                cells,
                lax.ppermute(head, axis, [((i + 1) % count, i) for i in range(ends)]),
            ],
            axis=dim,
        )
    return cells


def gathered(array, axis):
    count = lax.axis_size(axis)
    copies = jnp.broadcast_to(array[None], (count,) + array.shape)
    return lax.all_to_all(copies, axis, 0, 0, tiled=True)


def spread_weight(weight, ready):
    dp_count = lax.axis_size("dp")
    seq_count = lax.axis_size("seq")
    half = dp_count // 2
    cores = 2
    y_count = half // cores
    rows, width = weight.shape
    partner_pairs = [
        (d * seq_count + s, (d ^ half) * seq_count + (s ^ 1))
        for d in range(dp_count)
        for s in range(seq_count)
    ]
    held = jnp.stack([weight, lax.ppermute(weight, ("dp", "seq"), partner_pairs)])
    ring = [held]
    for shift in range(1, y_count):
        pairs = []
        for d in range(dp_count):
            upper, y_here, core = d // half, (d // cores) % y_count, d % cores
            pairs.append((d, upper * half + ((y_here + shift) % y_count) * cores + core))
        ring.append(lax.ppermute(held, "dp", pairs))
    mine, ready = lax.optimization_barrier((jnp.stack(ring), ready))
    sibling = lax.ppermute(mine, "dp", [(d, d ^ 1) for d in range(dp_count)])
    stacked = jnp.stack([mine, sibling]).reshape(dp_count, rows, width)
    me = lax.axis_index("dp")
    upper, y_here, core = me // half, (me // cores) % y_count, me % cores
    core_of = jnp.arange(2)[:, None, None]
    shift_of = jnp.arange(y_count)[None, :, None]
    upper_of = jnp.arange(2)[None, None, :]
    owner = (
        ((upper + upper_of) % 2) * half
        + ((y_here - shift_of) % y_count) * cores
        + (core + core_of) % 2
    )
    return stacked, owner.reshape(-1), ready


def gathered_copies(copies, axis):
    return lax.all_to_all(copies, axis, 0, 0, tiled=True)


def scattered_sum(array, axis):
    count = lax.axis_size(axis)
    rows, cols = array.shape
    pieces = array.reshape(rows, count, cols // count).transpose(1, 0, 2)
    return jnp.sum(lax.all_to_all(pieces, axis, 0, 0, tiled=True), axis=0)


def passed_along(array, axis, by):
    count = lax.axis_size(axis)
    pairs = [(i, i + by) for i in range(count) if 0 <= i + by < count]
    return lax.ppermute(array, axis, pairs)


def split_heads(query_rows, key_rows):
    rows_here = query_rows.shape[0]
    keys_here = key_rows.shape[0]
    head_count = key_rows.shape[1] // HD
    group_size = query_rows.shape[1] // key_rows.shape[1]
    return rows_here, keys_here, head_count, group_size


def attend_first(query_rows, key_rows, grad_rows, visible):
    rows_here, keys_here, head_count, group_size = split_heads(query_rows, key_rows)
    score_scale = HD ** (-0.5)
    query_split = query_rows.reshape(rows_here, head_count, group_size, HD)
    grad_split = grad_rows.reshape(rows_here, head_count, group_size, HD)
    key_split = key_rows.reshape(keys_here, head_count, HD)
    attentions = []
    value_parts = []
    for kv_group in range(head_count):
        query_head = query_split[:, kv_group]
        grad_head = grad_split[:, kv_group]
        key_head = key_split[:, kv_group]
        scores = (
            jnp.einsum("qgd,kd->gqk", query_head, key_head, preferred_element_type=jnp.float32)
            * score_scale
        )
        masked = jnp.where(visible[None], scores, -1e30)
        highest = jnp.max(masked, axis=-1, keepdims=True)
        weights = jnp.where(visible[None], jnp.exp(masked - highest), 0.0)
        attention = weights / jnp.sum(weights, axis=-1, keepdims=True)
        attention_low = attention.astype(jnp.bfloat16)
        attentions.append(attention)
        value_parts.append(
            jnp.einsum("gqk,qgd->kd", attention_low, grad_head, preferred_element_type=jnp.float32)
        )
    return attentions, jnp.concatenate(value_parts, axis=1)


def attend_second(query_rows, key_rows, value_rows, grad_rows, attentions):
    rows_here, keys_here, head_count, group_size = split_heads(query_rows, key_rows)
    score_scale = HD ** (-0.5)
    high = lax.Precision.HIGHEST
    query_split = query_rows.reshape(rows_here, head_count, group_size, HD)
    grad_split = grad_rows.reshape(rows_here, head_count, group_size, HD)
    key_split = key_rows.reshape(keys_here, head_count, HD)
    value_split = value_rows.reshape(keys_here, head_count, HD)
    query_parts = []
    key_parts = []
    for kv_group in range(head_count):
        query_head = query_split[:, kv_group]
        grad_head = grad_split[:, kv_group]
        key_head = key_split[:, kv_group]
        value_head = value_split[:, kv_group]
        attention = attentions[kv_group]
        prob_grad = jnp.einsum(
            "qgd,kd->gqk", grad_head, value_head, preferred_element_type=jnp.float32
        )
        row_delta = jnp.sum(attention * prob_grad, axis=-1, keepdims=True)
        score_grad = attention * (prob_grad - row_delta)
        key_wide = key_head.astype(jnp.float32)
        query_wide = query_head.astype(jnp.float32)
        query_parts.append(
            jnp.einsum("gqk,kd->qgd", score_grad, key_wide, precision=high) * score_scale
        )
        key_parts.append(
            jnp.einsum("gqk,qgd->kd", score_grad, query_wide, precision=high) * score_scale
        )
    query_grad = jnp.stack(query_parts, axis=1).reshape(rows_here, -1)
    return query_grad, jnp.concatenate(key_parts, axis=1)


def rim_sum(grad_block, tok_count):
    lower_rim = grad_block[:tok_count]
    upper_rim = grad_block[tok_count + tok_count :]
    center = grad_block[tok_count : tok_count + tok_count]
    from_upper = passed_along(lower_rim, "seq", -1)
    from_lower = passed_along(upper_rim, "seq", 1)
    return center + from_upper + from_lower


def local(layer_input, query_states, key_states, out_grad, value_weight, segment_ids, pair_split):
    layer_rows = layer_input[0]
    tok_count = layer_rows.shape[0]
    row_base = lax.axis_index("seq") * tok_count
    dp_count = lax.axis_size("dp")
    model_width = layer_rows.shape[1]
    weight_rows, kv_width = value_weight.shape
    key_block = with_halo(key_states[0], (("seq", 0),), tok_count)
    weight_slots, slot_owner, key_block = spread_weight(value_weight, key_block)
    input_pieces = layer_rows.reshape(tok_count, dp_count, model_width // dp_count).transpose(1, 0, 2)
    seg_row = segment_ids[0]
    fill_ids = jnp.full((tok_count,), -1, jnp.int32)
    padded_ids = jnp.concatenate([fill_ids, seg_row, fill_ids])
    seg_key = lax.dynamic_slice_in_dim(padded_ids, row_base, tok_count + 2 * tok_count, 0)
    seg_query = lax.dynamic_slice_in_dim(seg_row, row_base, tok_count, 0)
    pair_numbers = jnp.arange(pair_split.shape[1], dtype=jnp.int32)
    split_query = jnp.sum(
        jnp.where(seg_query[:, None] == pair_numbers[None, :], pair_split[0][None, :], 0), axis=1
    )
    pos_query = row_base + jnp.arange(tok_count, dtype=jnp.int32)
    pos_key = row_base - tok_count + jnp.arange(tok_count + 2 * tok_count, dtype=jnp.int32)
    visible = (seg_key[None, :] == seg_query[:, None]) & (
        (pos_key[None, :] <= pos_query[:, None]) | (pos_key[None, :] < split_query[:, None])
    )
    attentions, value_part = attend_first(query_states[0], key_block, out_grad[0], visible)
    value_grad = rim_sum(value_part, tok_count).astype(jnp.bfloat16)
    weight_full = weight_slots.reshape(-1, kv_width)
    grad_copies = jnp.broadcast_to(value_grad[None], (dp_count,) + value_grad.shape)
    arrived = gathered_copies(jnp.concatenate([grad_copies, input_pieces], axis=2), "dp")
    seq_count = lax.axis_size("seq")
    grad_rows = arrived[:, :, :kv_width].reshape(dp_count, tok_count, seq_count, -1)
    input_blocks = arrived[:, :, kv_width:]
    own_pieces = jnp.einsum(
        "rtk,rtjc->jkc", input_blocks, grad_rows, preferred_element_type=jnp.float32
    )
    summed = jnp.sum(gathered_copies(own_pieces, "seq"), axis=0)
    devices_all = lax.axis_size("dp") * lax.axis_size("seq")
    weight_grad = summed / devices_all
    input_slots = jnp.take(
        layer_rows.reshape(tok_count, dp_count, -1), slot_owner, axis=1, mode="clip"
    ).reshape(tok_count, -1)
    value_rows = jnp.dot(input_slots, weight_full, preferred_element_type=jnp.float32)
    value_block = with_halo(value_rows.astype(jnp.bfloat16), (("seq", 0),), tok_count)
    query_grad, key_part = attend_second(
        query_states[0], key_block, value_block, out_grad[0], attentions
    )
    key_grad = rim_sum(key_part, tok_count).astype(jnp.bfloat16)
    grad_slots = lax.dot_general(
        value_grad,
        weight_full,
        (((1,), (1,)), ((), ())),
        preferred_element_type=jnp.float32,
    ).astype(jnp.bfloat16)
    input_grad = jnp.take(
        grad_slots.reshape(tok_count, dp_count, -1), jnp.argsort(slot_owner), axis=1, mode="clip"
    ).reshape(tok_count, -1)
    return (
        query_grad.astype(jnp.bfloat16)[None],
        key_grad[None],
        input_grad[None],
        weight_grad,
    )


def solution(mesh):
    return jax.shard_map(
        local,
        mesh=mesh,
        in_specs=(
            P("dp", "seq", None),
            P("dp", "seq", None),
            P("dp", "seq", None),
            P("dp", "seq", None),
            P("dp", None),
            P("dp", None),
            P("dp", None),
        ),
        out_specs=(
            P("dp", "seq", None),
            P("dp", "seq", None),
            P("dp", "seq", None),
            P("dp", "seq"),
        ),
        check_vma=False,
    )
```

```python
import jax
import jax.numpy as jnp
from jax import lax
from jax.sharding import PartitionSpec as P

HD = 128


def with_halo(cells, sides, width):
    for axis, dim in sides:
        count = lax.axis_size(axis)
        ends = count - 1
        head = lax.slice_in_dim(cells, 0, width, axis=dim)
        tail = lax.slice_in_dim(cells, cells.shape[dim] - width, cells.shape[dim], axis=dim)
        cells = jnp.concatenate(
            [
                lax.ppermute(tail, axis, [(i, (i + 1) % count) for i in range(ends)]),
                cells,
                lax.ppermute(head, axis, [((i + 1) % count, i) for i in range(ends)]),
            ],
            axis=dim,
        )
    return cells


def gathered(array, axis):
    count = lax.axis_size(axis)
    copies = jnp.broadcast_to(array[None], (count,) + array.shape)
    return lax.all_to_all(copies, axis, 0, 0, tiled=True)


def spread_weight(weight, ready, riders):
    dp_count = lax.axis_size("dp")
    seq_count = lax.axis_size("seq")
    half = dp_count // 2
    cores = 2
    y_count = half // cores
    rows, width = weight.shape
    partner_pairs = [
        (d * seq_count + s, (d ^ half) * seq_count + (s ^ 1))
        for d in range(dp_count)
        for s in range(seq_count)
    ]
    held = jnp.stack([weight, lax.ppermute(weight, ("dp", "seq"), partner_pairs)])
    ring = [held]
    for shift in range(1, y_count):
        pairs = []
        for d in range(dp_count):
            upper, y_here, core = d // half, (d // cores) % y_count, d % cores
            pairs.append((d, upper * half + ((y_here + shift) % y_count) * cores + core))
        ring.append(lax.ppermute(held, "dp", pairs))
    mine, ready, riders = lax.optimization_barrier((jnp.stack(ring), ready, riders))
    sibling = lax.ppermute(mine, "dp", [(d, d ^ 1) for d in range(dp_count)])
    stacked = jnp.stack([mine, sibling]).reshape(dp_count, rows, width)
    me = lax.axis_index("dp")
    upper, y_here, core = me // half, (me // cores) % y_count, me % cores
    core_of = jnp.arange(2)[:, None, None]
    shift_of = jnp.arange(y_count)[None, :, None]
    upper_of = jnp.arange(2)[None, None, :]
    owner = (
        ((upper + upper_of) % 2) * half
        + ((y_here - shift_of) % y_count) * cores
        + (core + core_of) % 2
    )
    return stacked, owner.reshape(-1), ready, riders


def gathered_copies(copies, axis):
    return lax.all_to_all(copies, axis, 0, 0, tiled=True)


def scattered_sum(array, axis):
    count = lax.axis_size(axis)
    rows, cols = array.shape
    pieces = array.reshape(rows, count, cols // count).transpose(1, 0, 2)
    return jnp.sum(lax.all_to_all(pieces, axis, 0, 0, tiled=True), axis=0)


def passed_along(array, axis, by):
    count = lax.axis_size(axis)
    pairs = [(i, i + by) for i in range(count) if 0 <= i + by < count]
    return lax.ppermute(array, axis, pairs)


def split_heads(query_rows, key_rows):
    rows_here = query_rows.shape[0]
    keys_here = key_rows.shape[0]
    head_count = key_rows.shape[1] // HD
    group_size = query_rows.shape[1] // key_rows.shape[1]
    return rows_here, keys_here, head_count, group_size


def attend_first(query_rows, key_rows, grad_rows, visible):
    rows_here, keys_here, head_count, group_size = split_heads(query_rows, key_rows)
    score_scale = HD ** (-0.5)
    query_split = query_rows.reshape(rows_here, head_count, group_size, HD)
    grad_split = grad_rows.reshape(rows_here, head_count, group_size, HD)
    key_split = key_rows.reshape(keys_here, head_count, HD)
    attentions = []
    value_parts = []
    for kv_group in range(head_count):
        query_head = query_split[:, kv_group]
        grad_head = grad_split[:, kv_group]
        key_head = key_split[:, kv_group]
        scores = (
            jnp.einsum("qgd,kd->gqk", query_head, key_head, preferred_element_type=jnp.float32)
            * score_scale
        )
        masked = jnp.where(visible[None], scores, -1e30)
        highest = jnp.max(masked, axis=-1, keepdims=True)
        weights = jnp.where(visible[None], jnp.exp(masked - highest), 0.0)
        attention = weights / jnp.sum(weights, axis=-1, keepdims=True)
        attention_low = attention.astype(jnp.bfloat16)
        attentions.append(attention)
        value_parts.append(
            jnp.einsum("gqk,qgd->kd", attention_low, grad_head, preferred_element_type=jnp.float32)
        )
    return attentions, jnp.concatenate(value_parts, axis=1)


def attend_second(query_rows, key_rows, value_rows, grad_rows, attentions):
    rows_here, keys_here, head_count, group_size = split_heads(query_rows, key_rows)
    score_scale = HD ** (-0.5)
    high = lax.Precision.HIGHEST
    query_split = query_rows.reshape(rows_here, head_count, group_size, HD)
    grad_split = grad_rows.reshape(rows_here, head_count, group_size, HD)
    key_split = key_rows.reshape(keys_here, head_count, HD)
    value_split = value_rows.reshape(keys_here, head_count, HD)
    query_parts = []
    key_parts = []
    for kv_group in range(head_count):
        query_head = query_split[:, kv_group]
        grad_head = grad_split[:, kv_group]
        key_head = key_split[:, kv_group]
        value_head = value_split[:, kv_group]
        attention = attentions[kv_group]
        prob_grad = jnp.einsum(
            "qgd,kd->gqk", grad_head, value_head, preferred_element_type=jnp.float32
        )
        row_delta = jnp.sum(attention * prob_grad, axis=-1, keepdims=True)
        score_grad = attention * (prob_grad - row_delta)
        key_wide = key_head.astype(jnp.float32)
        query_wide = query_head.astype(jnp.float32)
        query_parts.append(
            jnp.einsum("gqk,kd->qgd", score_grad, key_wide, precision=high) * score_scale
        )
        key_parts.append(
            jnp.einsum("gqk,qgd->kd", score_grad, query_wide, precision=high) * score_scale
        )
    query_grad = jnp.stack(query_parts, axis=1).reshape(rows_here, -1)
    return query_grad, jnp.concatenate(key_parts, axis=1)


def rim_sum(grad_block, tok_count):
    lower_rim = grad_block[:tok_count]
    upper_rim = grad_block[tok_count + tok_count :]
    center = grad_block[tok_count : tok_count + tok_count]
    from_upper = passed_along(lower_rim, "seq", -1)
    from_lower = passed_along(upper_rim, "seq", 1)
    return center + from_upper + from_lower


def local(layer_input, query_states, key_states, out_grad, value_weight, segment_ids, pair_split):
    layer_rows = layer_input[0]
    tok_count = layer_rows.shape[0]
    row_base = lax.axis_index("seq") * tok_count
    dp_count = lax.axis_size("dp")
    model_width = layer_rows.shape[1]
    weight_rows, kv_width = value_weight.shape
    key_block = with_halo(key_states[0], (("seq", 0),), tok_count)
    input_pieces = layer_rows.reshape(tok_count, dp_count, model_width // dp_count).transpose(1, 0, 2)
    weight_slots, slot_owner, key_block, input_pieces = spread_weight(
        value_weight, key_block, input_pieces
    )
    input_blocks = gathered_copies(input_pieces, "dp")
    seg_row = segment_ids[0]
    fill_ids = jnp.full((tok_count,), -1, jnp.int32)
    padded_ids = jnp.concatenate([fill_ids, seg_row, fill_ids])
    seg_key = lax.dynamic_slice_in_dim(padded_ids, row_base, tok_count + 2 * tok_count, 0)
    seg_query = lax.dynamic_slice_in_dim(seg_row, row_base, tok_count, 0)
    pair_numbers = jnp.arange(pair_split.shape[1], dtype=jnp.int32)
    split_query = jnp.sum(
        jnp.where(seg_query[:, None] == pair_numbers[None, :], pair_split[0][None, :], 0), axis=1
    )
    pos_query = row_base + jnp.arange(tok_count, dtype=jnp.int32)
    pos_key = row_base - tok_count + jnp.arange(tok_count + 2 * tok_count, dtype=jnp.int32)
    visible = (seg_key[None, :] == seg_query[:, None]) & (
        (pos_key[None, :] <= pos_query[:, None]) | (pos_key[None, :] < split_query[:, None])
    )
    attentions, value_part = attend_first(query_states[0], key_block, out_grad[0], visible)
    value_part, input_blocks = lax.optimization_barrier((value_part, input_blocks))
    value_grad = rim_sum(value_part, tok_count).astype(jnp.bfloat16)
    value_grad, weight_slots = lax.optimization_barrier((value_grad, weight_slots))
    weight_full = weight_slots.reshape(-1, kv_width)
    grad_copies = jnp.broadcast_to(value_grad[None], (dp_count,) + value_grad.shape)
    seq_count = lax.axis_size("seq")
    grad_rows = gathered_copies(grad_copies, "dp").reshape(dp_count, tok_count, seq_count, -1)
    own_pieces = jnp.einsum(
        "rtk,rtjc->jkc", input_blocks, grad_rows, preferred_element_type=jnp.float32
    )
    summed = jnp.sum(gathered_copies(own_pieces, "seq"), axis=0)
    devices_all = lax.axis_size("dp") * lax.axis_size("seq")
    weight_grad = summed / devices_all
    input_slots = jnp.take(
        layer_rows.reshape(tok_count, dp_count, -1), slot_owner, axis=1, mode="clip"
    ).reshape(tok_count, -1)
    value_rows = jnp.dot(input_slots, weight_full, preferred_element_type=jnp.float32)
    value_block = with_halo(value_rows.astype(jnp.bfloat16), (("seq", 0),), tok_count)
    query_grad, key_part = attend_second(
        query_states[0], key_block, value_block, out_grad[0], attentions
    )
    key_grad = rim_sum(key_part, tok_count).astype(jnp.bfloat16)
    grad_slots = lax.dot_general(
        value_grad,
        weight_full,
        (((1,), (1,)), ((), ())),
        preferred_element_type=jnp.float32,
    ).astype(jnp.bfloat16)
    input_grad = jnp.take(
        grad_slots.reshape(tok_count, dp_count, -1), jnp.argsort(slot_owner), axis=1, mode="clip"
    ).reshape(tok_count, -1)
    return (
        query_grad.astype(jnp.bfloat16)[None],
        key_grad[None],
        input_grad[None],
        weight_grad,
    )


def solution(mesh):
    return jax.shard_map(
        local,
        mesh=mesh,
        in_specs=(
            P("dp", "seq", None),
            P("dp", "seq", None),
            P("dp", "seq", None),
            P("dp", "seq", None),
            P("dp", None),
            P("dp", None),
            P("dp", None),
        ),
        out_specs=(
            P("dp", "seq", None),
            P("dp", "seq", None),
            P("dp", "seq", None),
            P("dp", "seq"),
        ),
        check_vma=False,
    )
```

```python
import jax
import jax.numpy as jnp
from jax import lax
from jax.sharding import PartitionSpec as P

HD = 128


def with_halo(cells, sides, width):
    for axis, dim in sides:
        count = lax.axis_size(axis)
        ends = count - 1
        head = lax.slice_in_dim(cells, 0, width, axis=dim)
        tail = lax.slice_in_dim(cells, cells.shape[dim] - width, cells.shape[dim], axis=dim)
        cells = jnp.concatenate(
            [
                lax.ppermute(tail, axis, [(i, (i + 1) % count) for i in range(ends)]),
                cells,
                lax.ppermute(head, axis, [((i + 1) % count, i) for i in range(ends)]),
            ],
            axis=dim,
        )
    return cells


def gathered(array, axis):
    count = lax.axis_size(axis)
    copies = jnp.broadcast_to(array[None], (count,) + array.shape)
    return lax.all_to_all(copies, axis, 0, 0, tiled=True)


def spread_weight(weight, ready, riders):
    dp_count = lax.axis_size("dp")
    seq_count = lax.axis_size("seq")
    half = dp_count // 2
    cores = 2
    y_count = half // cores
    rows, width = weight.shape
    partner_pairs = [
        (d * seq_count + s, (d ^ half) * seq_count + (s ^ 1))
        for d in range(dp_count)
        for s in range(seq_count)
    ]
    held = jnp.stack([weight, lax.ppermute(weight, ("dp", "seq"), partner_pairs)])
    ring = [held]
    for shift in range(1, y_count):
        pairs = []
        for d in range(dp_count):
            upper, y_here, core = d // half, (d // cores) % y_count, d % cores
            pairs.append((d, upper * half + ((y_here + shift) % y_count) * cores + core))
        ring.append(lax.ppermute(held, "dp", pairs))
    mine, ready, riders = lax.optimization_barrier((jnp.stack(ring), ready, riders))
    sibling = lax.ppermute(mine, "dp", [(d, d ^ 1) for d in range(dp_count)])
    stacked = jnp.stack([mine, sibling]).reshape(dp_count, rows, width)
    me = lax.axis_index("dp")
    upper, y_here, core = me // half, (me // cores) % y_count, me % cores
    core_of = jnp.arange(2)[:, None, None]
    shift_of = jnp.arange(y_count)[None, :, None]
    upper_of = jnp.arange(2)[None, None, :]
    owner = (
        ((upper + upper_of) % 2) * half
        + ((y_here - shift_of) % y_count) * cores
        + (core + core_of) % 2
    )
    return stacked, owner.reshape(-1), ready, riders


def gathered_copies(copies, axis):
    return lax.all_to_all(copies, axis, 0, 0, tiled=True)


def scattered_sum(array, axis):
    count = lax.axis_size(axis)
    rows, cols = array.shape
    pieces = array.reshape(rows, count, cols // count).transpose(1, 0, 2)
    return jnp.sum(lax.all_to_all(pieces, axis, 0, 0, tiled=True), axis=0)


def passed_along(array, axis, by):
    count = lax.axis_size(axis)
    pairs = [(i, i + by) for i in range(count) if 0 <= i + by < count]
    return lax.ppermute(array, axis, pairs)


def split_heads(query_rows, key_rows):
    rows_here = query_rows.shape[0]
    keys_here = key_rows.shape[0]
    head_count = key_rows.shape[1] // HD
    group_size = query_rows.shape[1] // key_rows.shape[1]
    return rows_here, keys_here, head_count, group_size


def attend_first(query_rows, key_rows, grad_rows, visible):
    rows_here, keys_here, head_count, group_size = split_heads(query_rows, key_rows)
    score_scale = HD ** (-0.5)
    query_split = query_rows.reshape(rows_here, head_count, group_size, HD)
    grad_split = grad_rows.reshape(rows_here, head_count, group_size, HD)
    key_split = key_rows.reshape(keys_here, head_count, HD)
    attentions = []
    value_parts = []
    for kv_group in range(head_count):
        query_head = query_split[:, kv_group]
        grad_head = grad_split[:, kv_group]
        key_head = key_split[:, kv_group]
        scores = (
            jnp.einsum("qgd,kd->gqk", query_head, key_head, preferred_element_type=jnp.float32)
            * score_scale
        )
        masked = jnp.where(visible[None], scores, -1e30)
        highest = jnp.max(masked, axis=-1, keepdims=True)
        weights = jnp.where(visible[None], jnp.exp(masked - highest), 0.0)
        attention = weights / jnp.sum(weights, axis=-1, keepdims=True)
        attention_low = attention.astype(jnp.bfloat16)
        attentions.append(attention)
        value_parts.append(
            jnp.einsum("gqk,qgd->kd", attention_low, grad_head, preferred_element_type=jnp.float32)
        )
    return attentions, jnp.concatenate(value_parts, axis=1)


def attend_second(query_rows, key_rows, value_rows, grad_rows, attentions):
    rows_here, keys_here, head_count, group_size = split_heads(query_rows, key_rows)
    score_scale = HD ** (-0.5)
    high = lax.Precision.HIGHEST
    query_split = query_rows.reshape(rows_here, head_count, group_size, HD)
    grad_split = grad_rows.reshape(rows_here, head_count, group_size, HD)
    key_split = key_rows.reshape(keys_here, head_count, HD)
    value_split = value_rows.reshape(keys_here, head_count, HD)
    query_parts = []
    key_parts = []
    for kv_group in range(head_count):
        query_head = query_split[:, kv_group]
        grad_head = grad_split[:, kv_group]
        key_head = key_split[:, kv_group]
        value_head = value_split[:, kv_group]
        attention = attentions[kv_group]
        prob_grad = jnp.einsum(
            "qgd,kd->gqk", grad_head, value_head, preferred_element_type=jnp.float32
        )
        row_delta = jnp.sum(attention * prob_grad, axis=-1, keepdims=True)
        score_grad = attention * (prob_grad - row_delta)
        key_wide = key_head.astype(jnp.float32)
        query_wide = query_head.astype(jnp.float32)
        query_parts.append(
            jnp.einsum("gqk,kd->qgd", score_grad, key_wide, precision=high) * score_scale
        )
        key_parts.append(
            jnp.einsum("gqk,qgd->kd", score_grad, query_wide, precision=high) * score_scale
        )
    query_grad = jnp.stack(query_parts, axis=1).reshape(rows_here, -1)
    return query_grad, jnp.concatenate(key_parts, axis=1)


def rim_sum(grad_block, tok_count):
    lower_rim = grad_block[:tok_count]
    upper_rim = grad_block[tok_count + tok_count :]
    center = grad_block[tok_count : tok_count + tok_count]
    from_upper = passed_along(lower_rim, "seq", -1)
    from_lower = passed_along(upper_rim, "seq", 1)
    return center + from_upper + from_lower


def local(layer_input, query_states, key_states, out_grad, value_weight, segment_ids, pair_split):
    layer_rows = layer_input[0]
    tok_count = layer_rows.shape[0]
    row_base = lax.axis_index("seq") * tok_count
    dp_count = lax.axis_size("dp")
    model_width = layer_rows.shape[1]
    weight_rows, kv_width = value_weight.shape
    key_block = with_halo(key_states[0], (("seq", 0),), tok_count)
    input_pieces = layer_rows.reshape(tok_count, dp_count, model_width // dp_count).transpose(1, 0, 2)
    weight_slots, slot_owner, key_block, input_pieces = spread_weight(
        value_weight, key_block, input_pieces
    )
    input_blocks = gathered_copies(input_pieces, "dp")
    seg_row = segment_ids[0]
    fill_ids = jnp.full((tok_count,), -1, jnp.int32)
    padded_ids = jnp.concatenate([fill_ids, seg_row, fill_ids])
    seg_key = lax.dynamic_slice_in_dim(padded_ids, row_base, tok_count + 2 * tok_count, 0)
    seg_query = lax.dynamic_slice_in_dim(seg_row, row_base, tok_count, 0)
    pair_numbers = jnp.arange(pair_split.shape[1], dtype=jnp.int32)
    split_query = jnp.sum(
        jnp.where(seg_query[:, None] == pair_numbers[None, :], pair_split[0][None, :], 0), axis=1
    )
    pos_query = row_base + jnp.arange(tok_count, dtype=jnp.int32)
    pos_key = row_base - tok_count + jnp.arange(tok_count + 2 * tok_count, dtype=jnp.int32)
    visible = (seg_key[None, :] == seg_query[:, None]) & (
        (pos_key[None, :] <= pos_query[:, None]) | (pos_key[None, :] < split_query[:, None])
    )
    attentions, value_part = attend_first(query_states[0], key_block, out_grad[0], visible)
    value_part, input_blocks = lax.optimization_barrier((value_part, input_blocks))
    value_grad = rim_sum(value_part, tok_count).astype(jnp.bfloat16)
    value_grad, weight_slots = lax.optimization_barrier((value_grad, weight_slots))
    weight_full = weight_slots.reshape(-1, kv_width)
    grad_copies = jnp.broadcast_to(value_grad[None], (dp_count,) + value_grad.shape)
    seq_count = lax.axis_size("seq")
    grad_rows = gathered_copies(grad_copies, "dp").reshape(dp_count, tok_count, seq_count, -1)
    own_pieces = jnp.einsum(
        "rtk,rtjc->jkc", input_blocks, grad_rows, preferred_element_type=jnp.float32
    )
    input_slots = jnp.take(
        layer_rows.reshape(tok_count, dp_count, -1), slot_owner, axis=1, mode="clip"
    ).reshape(tok_count, -1)
    value_rows = jnp.dot(input_slots, weight_full, preferred_element_type=jnp.float32)
    value_block = with_halo(value_rows.astype(jnp.bfloat16), (("seq", 0),), tok_count)
    query_grad, key_part = attend_second(
        query_states[0], key_block, value_block, out_grad[0], attentions
    )
    key_grad = rim_sum(key_part, tok_count).astype(jnp.bfloat16)
    key_grad, own_pieces = lax.optimization_barrier((key_grad, own_pieces))
    summed = jnp.sum(gathered_copies(own_pieces, "seq"), axis=0)
    devices_all = lax.axis_size("dp") * lax.axis_size("seq")
    weight_grad = summed / devices_all
    grad_slots = lax.dot_general(
        value_grad,
        weight_full,
        (((1,), (1,)), ((), ())),
        preferred_element_type=jnp.float32,
    ).astype(jnp.bfloat16)
    input_grad = jnp.take(
        grad_slots.reshape(tok_count, dp_count, -1), jnp.argsort(slot_owner), axis=1, mode="clip"
    ).reshape(tok_count, -1)
    return (
        query_grad.astype(jnp.bfloat16)[None],
        key_grad[None],
        input_grad[None],
        weight_grad,
    )


def solution(mesh):
    return jax.shard_map(
        local,
        mesh=mesh,
        in_specs=(
            P("dp", "seq", None),
            P("dp", "seq", None),
            P("dp", "seq", None),
            P("dp", "seq", None),
            P("dp", None),
            P("dp", None),
            P("dp", None),
        ),
        out_specs=(
            P("dp", "seq", None),
            P("dp", "seq", None),
            P("dp", "seq", None),
            P("dp", "seq"),
        ),
        check_vma=False,
    )
```

```python
import jax
import jax.numpy as jnp
from jax import lax
from jax.experimental import pallas as pl
from jax.experimental.pallas import tpu as pltpu
from jax.sharding import PartitionSpec as P

HD = 128


def with_halo(cells, sides, width):
    for axis, dim in sides:
        count = lax.axis_size(axis)
        ends = count - 1
        head = lax.slice_in_dim(cells, 0, width, axis=dim)
        tail = lax.slice_in_dim(cells, cells.shape[dim] - width, cells.shape[dim], axis=dim)
        cells = jnp.concatenate(
            [
                lax.ppermute(tail, axis, [(i, (i + 1) % count) for i in range(ends)]),
                cells,
                lax.ppermute(head, axis, [((i + 1) % count, i) for i in range(ends)]),
            ],
            axis=dim,
        )
    return cells


def gathered(array, axis):
    count = lax.axis_size(axis)
    copies = jnp.broadcast_to(array[None], (count,) + array.shape)
    return lax.all_to_all(copies, axis, 0, 0, tiled=True)


def spread_weight(weight, ready, riders):
    dp_count = lax.axis_size("dp")
    seq_count = lax.axis_size("seq")
    half = dp_count // 2
    cores = 2
    y_count = half // cores
    rows, width = weight.shape
    partner_pairs = [
        (d * seq_count + s, (d ^ half) * seq_count + (s ^ 1))
        for d in range(dp_count)
        for s in range(seq_count)
    ]
    held = jnp.stack([weight, lax.ppermute(weight, ("dp", "seq"), partner_pairs)])
    ring = [held]
    for shift in range(1, y_count):
        pairs = []
        for d in range(dp_count):
            upper, y_here, core = d // half, (d // cores) % y_count, d % cores
            pairs.append((d, upper * half + ((y_here + shift) % y_count) * cores + core))
        ring.append(lax.ppermute(held, "dp", pairs))
    mine, ready, riders = lax.optimization_barrier((jnp.stack(ring), ready, riders))
    sibling = lax.ppermute(mine, "dp", [(d, d ^ 1) for d in range(dp_count)])
    stacked = jnp.stack([mine, sibling]).reshape(dp_count, rows, width)
    me = lax.axis_index("dp")
    upper, y_here, core = me // half, (me // cores) % y_count, me % cores
    core_of = jnp.arange(2)[:, None, None]
    shift_of = jnp.arange(y_count)[None, :, None]
    upper_of = jnp.arange(2)[None, None, :]
    owner = (
        ((upper + upper_of) % 2) * half
        + ((y_here - shift_of) % y_count) * cores
        + (core + core_of) % 2
    )
    return stacked, owner.reshape(-1), ready, riders


def summed_pieces_kernel(count, pieces_ref, out_ref, landed, send_sems, recv_sems):
    me = lax.axis_index("seq")
    row = lax.axis_index("dp")
    mesh_kind = pl.DeviceIdType.MESH
    barrier = pltpu.get_barrier_semaphore()
    for offset in range(1, count):
        peer = lax.rem(me + offset, count)
        pl.semaphore_signal(barrier, 1, device_id=(row, peer), device_id_type=mesh_kind)
    pl.semaphore_wait(barrier, count - 1)
    copies = []
    for offset in range(1, count):
        peer = lax.rem(me + offset, count)
        copy = pltpu.make_async_remote_copy(
            src_ref=pieces_ref.at[peer],
            dst_ref=landed.at[offset],
            send_sem=send_sems.at[offset],
            recv_sem=recv_sems.at[offset],
            device_id=(row, peer),
            device_id_type=mesh_kind,
        )
        copy.start()
        copies.append(copy)
    total = pieces_ref[me]
    for offset, copy in zip(range(1, count), copies):
        copy.wait()
        total = total + landed[offset]
    out_ref[...] = total


def summed_pieces(pieces):
    count = pieces.shape[0]
    return pl.pallas_call(
        lambda *refs: summed_pieces_kernel(count, *refs),
        out_shape=jax.ShapeDtypeStruct(pieces.shape[1:], pieces.dtype),
        in_specs=[pl.BlockSpec(memory_space=pltpu.VMEM)],
        out_specs=pl.BlockSpec(memory_space=pltpu.VMEM),
        scratch_shapes=[
            pltpu.VMEM(pieces.shape, pieces.dtype),
            pltpu.SemaphoreType.DMA((count,)),
            pltpu.SemaphoreType.DMA((count,)),
        ],
        compiler_params=pltpu.CompilerParams(collective_id=0, has_side_effects=True),
    )(pieces)


def gathered_copies(copies, axis):
    return lax.all_to_all(copies, axis, 0, 0, tiled=True)


def scattered_sum(array, axis):
    count = lax.axis_size(axis)
    rows, cols = array.shape
    pieces = array.reshape(rows, count, cols // count).transpose(1, 0, 2)
    return jnp.sum(lax.all_to_all(pieces, axis, 0, 0, tiled=True), axis=0)


def passed_along(array, axis, by):
    count = lax.axis_size(axis)
    pairs = [(i, i + by) for i in range(count) if 0 <= i + by < count]
    return lax.ppermute(array, axis, pairs)


def split_heads(query_rows, key_rows):
    rows_here = query_rows.shape[0]
    keys_here = key_rows.shape[0]
    head_count = key_rows.shape[1] // HD
    group_size = query_rows.shape[1] // key_rows.shape[1]
    return rows_here, keys_here, head_count, group_size


def attend_first(query_rows, key_rows, grad_rows, visible):
    rows_here, keys_here, head_count, group_size = split_heads(query_rows, key_rows)
    score_scale = HD ** (-0.5)
    query_split = query_rows.reshape(rows_here, head_count, group_size, HD)
    grad_split = grad_rows.reshape(rows_here, head_count, group_size, HD)
    key_split = key_rows.reshape(keys_here, head_count, HD)
    attentions = []
    value_parts = []
    for kv_group in range(head_count):
        query_head = query_split[:, kv_group]
        grad_head = grad_split[:, kv_group]
        key_head = key_split[:, kv_group]
        scores = (
            jnp.einsum("qgd,kd->gqk", query_head, key_head, preferred_element_type=jnp.float32)
            * score_scale
        )
        masked = jnp.where(visible[None], scores, -1e30)
        highest = jnp.max(masked, axis=-1, keepdims=True)
        weights = jnp.where(visible[None], jnp.exp(masked - highest), 0.0)
        attention = weights / jnp.sum(weights, axis=-1, keepdims=True)
        attention_low = attention.astype(jnp.bfloat16)
        attentions.append(attention)
        value_parts.append(
            jnp.einsum("gqk,qgd->kd", attention_low, grad_head, preferred_element_type=jnp.float32)
        )
    return attentions, jnp.concatenate(value_parts, axis=1)


def attend_second(query_rows, key_rows, value_rows, grad_rows, attentions):
    rows_here, keys_here, head_count, group_size = split_heads(query_rows, key_rows)
    score_scale = HD ** (-0.5)
    high = lax.Precision.HIGHEST
    query_split = query_rows.reshape(rows_here, head_count, group_size, HD)
    grad_split = grad_rows.reshape(rows_here, head_count, group_size, HD)
    key_split = key_rows.reshape(keys_here, head_count, HD)
    value_split = value_rows.reshape(keys_here, head_count, HD)
    query_parts = []
    key_parts = []
    for kv_group in range(head_count):
        query_head = query_split[:, kv_group]
        grad_head = grad_split[:, kv_group]
        key_head = key_split[:, kv_group]
        value_head = value_split[:, kv_group]
        attention = attentions[kv_group]
        prob_grad = jnp.einsum(
            "qgd,kd->gqk", grad_head, value_head, preferred_element_type=jnp.float32
        )
        row_delta = jnp.sum(attention * prob_grad, axis=-1, keepdims=True)
        score_grad = attention * (prob_grad - row_delta)
        key_wide = key_head.astype(jnp.float32)
        query_wide = query_head.astype(jnp.float32)
        query_parts.append(
            jnp.einsum("gqk,kd->qgd", score_grad, key_wide, precision=high) * score_scale
        )
        key_parts.append(
            jnp.einsum("gqk,qgd->kd", score_grad, query_wide, precision=high) * score_scale
        )
    query_grad = jnp.stack(query_parts, axis=1).reshape(rows_here, -1)
    return query_grad, jnp.concatenate(key_parts, axis=1)


def rim_sum(grad_block, tok_count):
    lower_rim = grad_block[:tok_count]
    upper_rim = grad_block[tok_count + tok_count :]
    center = grad_block[tok_count : tok_count + tok_count]
    from_upper = passed_along(lower_rim, "seq", -1)
    from_lower = passed_along(upper_rim, "seq", 1)
    return center + from_upper + from_lower


def local(layer_input, query_states, key_states, out_grad, value_weight, segment_ids, pair_split):
    layer_rows = layer_input[0]
    tok_count = layer_rows.shape[0]
    row_base = lax.axis_index("seq") * tok_count
    dp_count = lax.axis_size("dp")
    model_width = layer_rows.shape[1]
    weight_rows, kv_width = value_weight.shape
    key_block = with_halo(key_states[0], (("seq", 0),), tok_count)
    input_pieces = layer_rows.reshape(tok_count, dp_count, model_width // dp_count).transpose(1, 0, 2)
    weight_slots, slot_owner, key_block, input_pieces = spread_weight(
        value_weight, key_block, input_pieces
    )
    input_blocks = gathered_copies(input_pieces, "dp")
    seg_row = segment_ids[0]
    fill_ids = jnp.full((tok_count,), -1, jnp.int32)
    padded_ids = jnp.concatenate([fill_ids, seg_row, fill_ids])
    seg_key = lax.dynamic_slice_in_dim(padded_ids, row_base, tok_count + 2 * tok_count, 0)
    seg_query = lax.dynamic_slice_in_dim(seg_row, row_base, tok_count, 0)
    pair_numbers = jnp.arange(pair_split.shape[1], dtype=jnp.int32)
    split_query = jnp.sum(
        jnp.where(seg_query[:, None] == pair_numbers[None, :], pair_split[0][None, :], 0), axis=1
    )
    pos_query = row_base + jnp.arange(tok_count, dtype=jnp.int32)
    pos_key = row_base - tok_count + jnp.arange(tok_count + 2 * tok_count, dtype=jnp.int32)
    visible = (seg_key[None, :] == seg_query[:, None]) & (
        (pos_key[None, :] <= pos_query[:, None]) | (pos_key[None, :] < split_query[:, None])
    )
    attentions, value_part = attend_first(query_states[0], key_block, out_grad[0], visible)
    value_part, input_blocks = lax.optimization_barrier((value_part, input_blocks))
    value_grad = rim_sum(value_part, tok_count).astype(jnp.bfloat16)
    value_grad, weight_slots = lax.optimization_barrier((value_grad, weight_slots))
    weight_full = weight_slots.reshape(-1, kv_width)
    grad_copies = jnp.broadcast_to(value_grad[None], (dp_count,) + value_grad.shape)
    seq_count = lax.axis_size("seq")
    grad_rows = gathered_copies(grad_copies, "dp").reshape(dp_count, tok_count, seq_count, -1)
    own_pieces = jnp.einsum(
        "rtk,rtjc->jck", input_blocks, grad_rows, preferred_element_type=jnp.float32
    )
    summed = summed_pieces(own_pieces).T
    devices_all = lax.axis_size("dp") * lax.axis_size("seq")
    weight_grad = summed / devices_all
    input_slots = jnp.take(
        layer_rows.reshape(tok_count, dp_count, -1), slot_owner, axis=1, mode="clip"
    ).reshape(tok_count, -1)
    value_rows = jnp.dot(input_slots, weight_full, preferred_element_type=jnp.float32)
    value_block = with_halo(value_rows.astype(jnp.bfloat16), (("seq", 0),), tok_count)
    query_grad, key_part = attend_second(
        query_states[0], key_block, value_block, out_grad[0], attentions
    )
    key_grad = rim_sum(key_part, tok_count).astype(jnp.bfloat16)
    grad_slots = lax.dot_general(
        value_grad,
        weight_full,
        (((1,), (1,)), ((), ())),
        preferred_element_type=jnp.float32,
    ).astype(jnp.bfloat16)
    input_grad = jnp.take(
        grad_slots.reshape(tok_count, dp_count, -1), jnp.argsort(slot_owner), axis=1, mode="clip"
    ).reshape(tok_count, -1)
    return (
        query_grad.astype(jnp.bfloat16)[None],
        key_grad[None],
        input_grad[None],
        weight_grad,
    )


def solution(mesh):
    return jax.shard_map(
        local,
        mesh=mesh,
        in_specs=(
            P("dp", "seq", None),
            P("dp", "seq", None),
            P("dp", "seq", None),
            P("dp", "seq", None),
            P("dp", None),
            P("dp", None),
            P("dp", None),
        ),
        out_specs=(
            P("dp", "seq", None),
            P("dp", "seq", None),
            P("dp", "seq", None),
            P("dp", "seq"),
        ),
        check_vma=False,
    )
```

```python
import jax
import jax.numpy as jnp
from jax import lax
from jax.sharding import PartitionSpec as P

HD = 128


def with_halo(cells, sides, width):
    for axis, dim in sides:
        count = lax.axis_size(axis)
        ends = count - 1
        head = lax.slice_in_dim(cells, 0, width, axis=dim)
        tail = lax.slice_in_dim(cells, cells.shape[dim] - width, cells.shape[dim], axis=dim)
        cells = jnp.concatenate(
            [
                lax.ppermute(tail, axis, [(i, (i + 1) % count) for i in range(ends)]),
                cells,
                lax.ppermute(head, axis, [((i + 1) % count, i) for i in range(ends)]),
            ],
            axis=dim,
        )
    return cells


def gathered(array, axis):
    count = lax.axis_size(axis)
    copies = jnp.broadcast_to(array[None], (count,) + array.shape)
    return lax.all_to_all(copies, axis, 0, 0, tiled=True)


def spread_weight(weight, ready):
    dp_count = lax.axis_size("dp")
    seq_count = lax.axis_size("seq")
    half = dp_count // 2
    cores = 2
    y_count = half // cores
    rows, width = weight.shape
    partner_pairs = [
        (d * seq_count + s, (d ^ half) * seq_count + (s ^ 1))
        for d in range(dp_count)
        for s in range(seq_count)
    ]
    held = jnp.stack([weight, lax.ppermute(weight, ("dp", "seq"), partner_pairs)])
    held, ready = lax.optimization_barrier((held, ready))
    ring = [held]
    for shift in range(1, y_count):
        pairs = []
        for d in range(dp_count):
            upper, y_here, core = d // half, (d // cores) % y_count, d % cores
            pairs.append((d, upper * half + ((y_here + shift) % y_count) * cores + core))
        ring.append(lax.ppermute(held, "dp", pairs))
    return jnp.stack(ring), ready


def finish_weight(mine):
    dp_count = lax.axis_size("dp")
    half = dp_count // 2
    cores = 2
    y_count = half // cores
    rows, width = mine.shape[-2:]
    sibling = lax.ppermute(mine, "dp", [(d, d ^ 1) for d in range(dp_count)])
    stacked = jnp.stack([mine, sibling]).reshape(dp_count, rows, width)
    me = lax.axis_index("dp")
    upper, y_here, core = me // half, (me // cores) % y_count, me % cores
    core_of = jnp.arange(2)[:, None, None]
    shift_of = jnp.arange(y_count)[None, :, None]
    upper_of = jnp.arange(2)[None, None, :]
    owner = (
        ((upper + upper_of) % 2) * half
        + ((y_here - shift_of) % y_count) * cores
        + (core + core_of) % 2
    )
    return stacked, owner.reshape(-1)


def gathered_copies(copies, axis):
    return lax.all_to_all(copies, axis, 0, 0, tiled=True)


def scattered_sum(array, axis):
    count = lax.axis_size(axis)
    rows, cols = array.shape
    pieces = array.reshape(rows, count, cols // count).transpose(1, 0, 2)
    return jnp.sum(lax.all_to_all(pieces, axis, 0, 0, tiled=True), axis=0)


def passed_along(array, axis, by):
    count = lax.axis_size(axis)
    pairs = [(i, i + by) for i in range(count) if 0 <= i + by < count]
    return lax.ppermute(array, axis, pairs)


def split_heads(query_rows, key_rows):
    rows_here = query_rows.shape[0]
    keys_here = key_rows.shape[0]
    head_count = key_rows.shape[1] // HD
    group_size = query_rows.shape[1] // key_rows.shape[1]
    return rows_here, keys_here, head_count, group_size


def attend_first(query_rows, key_rows, grad_rows, visible, held):
    rows_here, keys_here, head_count, group_size = split_heads(query_rows, key_rows)
    score_scale = HD ** (-0.5)
    query_split = query_rows.reshape(rows_here, head_count, group_size, HD)
    grad_split = grad_rows.reshape(rows_here, head_count, group_size, HD)
    key_split = key_rows.reshape(keys_here, head_count, HD)
    attentions = []
    value_parts = []
    for kv_group in range(head_count):
        if kv_group == head_count // 2:
            held, attentions, value_parts = lax.optimization_barrier(
                (held, attentions, value_parts)
            )
        query_head = query_split[:, kv_group]
        grad_head = grad_split[:, kv_group]
        key_head = key_split[:, kv_group]
        scores = (
            jnp.einsum("qgd,kd->gqk", query_head, key_head, preferred_element_type=jnp.float32)
            * score_scale
        )
        masked = jnp.where(visible[None], scores, -1e30)
        highest = jnp.max(masked, axis=-1, keepdims=True)
        weights = jnp.where(visible[None], jnp.exp(masked - highest), 0.0)
        attention = weights / jnp.sum(weights, axis=-1, keepdims=True)
        attention_low = attention.astype(jnp.bfloat16)
        attentions.append(attention)
        value_parts.append(
            jnp.einsum("gqk,qgd->kd", attention_low, grad_head, preferred_element_type=jnp.float32)
        )
    return attentions, jnp.concatenate(value_parts, axis=1), held


def attend_second(query_rows, key_rows, value_rows, grad_rows, attentions):
    rows_here, keys_here, head_count, group_size = split_heads(query_rows, key_rows)
    score_scale = HD ** (-0.5)
    high = lax.Precision.HIGHEST
    query_split = query_rows.reshape(rows_here, head_count, group_size, HD)
    grad_split = grad_rows.reshape(rows_here, head_count, group_size, HD)
    key_split = key_rows.reshape(keys_here, head_count, HD)
    value_split = value_rows.reshape(keys_here, head_count, HD)
    query_parts = []
    key_parts = []
    for kv_group in range(head_count):
        query_head = query_split[:, kv_group]
        grad_head = grad_split[:, kv_group]
        key_head = key_split[:, kv_group]
        value_head = value_split[:, kv_group]
        attention = attentions[kv_group]
        prob_grad = jnp.einsum(
            "qgd,kd->gqk", grad_head, value_head, preferred_element_type=jnp.float32
        )
        row_delta = jnp.sum(attention * prob_grad, axis=-1, keepdims=True)
        score_grad = attention * (prob_grad - row_delta)
        key_wide = key_head.astype(jnp.float32)
        query_wide = query_head.astype(jnp.float32)
        query_parts.append(
            jnp.einsum("gqk,kd->qgd", score_grad, key_wide, precision=high) * score_scale
        )
        key_parts.append(
            jnp.einsum("gqk,qgd->kd", score_grad, query_wide, precision=high) * score_scale
        )
    query_grad = jnp.stack(query_parts, axis=1).reshape(rows_here, -1)
    return query_grad, jnp.concatenate(key_parts, axis=1)


def rim_sum(grad_block, tok_count):
    lower_rim = grad_block[:tok_count]
    upper_rim = grad_block[tok_count + tok_count :]
    center = grad_block[tok_count : tok_count + tok_count]
    from_upper = passed_along(lower_rim, "seq", -1)
    from_lower = passed_along(upper_rim, "seq", 1)
    return center + from_upper + from_lower


def local(layer_input, query_states, key_states, out_grad, value_weight, segment_ids, pair_split):
    layer_rows = layer_input[0]
    tok_count = layer_rows.shape[0]
    row_base = lax.axis_index("seq") * tok_count
    dp_count = lax.axis_size("dp")
    model_width = layer_rows.shape[1]
    weight_rows, kv_width = value_weight.shape
    key_block = with_halo(key_states[0], (("seq", 0),), tok_count)
    input_pieces = layer_rows.reshape(tok_count, dp_count, model_width // dp_count).transpose(1, 0, 2)
    weight_ring, key_block = spread_weight(value_weight, key_block)
    seg_row = segment_ids[0]
    fill_ids = jnp.full((tok_count,), -1, jnp.int32)
    padded_ids = jnp.concatenate([fill_ids, seg_row, fill_ids])
    seg_key = lax.dynamic_slice_in_dim(padded_ids, row_base, tok_count + 2 * tok_count, 0)
    seg_query = lax.dynamic_slice_in_dim(seg_row, row_base, tok_count, 0)
    pair_numbers = jnp.arange(pair_split.shape[1], dtype=jnp.int32)
    split_query = jnp.sum(
        jnp.where(seg_query[:, None] == pair_numbers[None, :], pair_split[0][None, :], 0), axis=1
    )
    pos_query = row_base + jnp.arange(tok_count, dtype=jnp.int32)
    pos_key = row_base - tok_count + jnp.arange(tok_count + 2 * tok_count, dtype=jnp.int32)
    visible = (seg_key[None, :] == seg_query[:, None]) & (
        (pos_key[None, :] <= pos_query[:, None]) | (pos_key[None, :] < split_query[:, None])
    )
    attentions, value_part, (weight_ring, input_pieces) = attend_first(
        query_states[0], key_block, out_grad[0], visible, (weight_ring, input_pieces)
    )
    weight_slots, slot_owner = finish_weight(weight_ring)
    input_blocks = gathered_copies(input_pieces, "dp")
    value_part, input_blocks = lax.optimization_barrier((value_part, input_blocks))
    value_grad = rim_sum(value_part, tok_count).astype(jnp.bfloat16)
    value_grad, weight_slots = lax.optimization_barrier((value_grad, weight_slots))
    weight_full = weight_slots.reshape(-1, kv_width)
    grad_copies = jnp.broadcast_to(value_grad[None], (dp_count,) + value_grad.shape)
    seq_count = lax.axis_size("seq")
    grad_rows = gathered_copies(grad_copies, "dp").reshape(dp_count, tok_count, seq_count, -1)
    own_pieces = jnp.einsum(
        "rtk,rtjc->jkc", input_blocks, grad_rows, preferred_element_type=jnp.float32
    )
    summed = jnp.sum(gathered_copies(own_pieces, "seq"), axis=0)
    devices_all = lax.axis_size("dp") * lax.axis_size("seq")
    weight_grad = summed / devices_all
    input_slots = jnp.take(
        layer_rows.reshape(tok_count, dp_count, -1), slot_owner, axis=1, mode="clip"
    ).reshape(tok_count, -1)
    value_rows = jnp.dot(input_slots, weight_full, preferred_element_type=jnp.float32)
    value_block = with_halo(value_rows.astype(jnp.bfloat16), (("seq", 0),), tok_count)
    query_grad, key_part = attend_second(
        query_states[0], key_block, value_block, out_grad[0], attentions
    )
    key_grad = rim_sum(key_part, tok_count).astype(jnp.bfloat16)
    grad_slots = lax.dot_general(
        value_grad,
        weight_full,
        (((1,), (1,)), ((), ())),
        preferred_element_type=jnp.float32,
    ).astype(jnp.bfloat16)
    input_grad = jnp.take(
        grad_slots.reshape(tok_count, dp_count, -1), jnp.argsort(slot_owner), axis=1, mode="clip"
    ).reshape(tok_count, -1)
    return (
        query_grad.astype(jnp.bfloat16)[None],
        key_grad[None],
        input_grad[None],
        weight_grad,
    )


def solution(mesh):
    return jax.shard_map(
        local,
        mesh=mesh,
        in_specs=(
            P("dp", "seq", None),
            P("dp", "seq", None),
            P("dp", "seq", None),
            P("dp", "seq", None),
            P("dp", None),
            P("dp", None),
            P("dp", None),
        ),
        out_specs=(
            P("dp", "seq", None),
            P("dp", "seq", None),
            P("dp", "seq", None),
            P("dp", "seq"),
        ),
        check_vma=False,
    )
```

```python
import jax
import jax.numpy as jnp
from jax import lax
from jax.sharding import PartitionSpec as P

HD = 128


def with_halo(cells, sides, width):
    for axis, dim in sides:
        count = lax.axis_size(axis)
        ends = count - 1
        head = lax.slice_in_dim(cells, 0, width, axis=dim)
        tail = lax.slice_in_dim(cells, cells.shape[dim] - width, cells.shape[dim], axis=dim)
        cells = jnp.concatenate(
            [
                lax.ppermute(tail, axis, [(i, (i + 1) % count) for i in range(ends)]),
                cells,
                lax.ppermute(head, axis, [((i + 1) % count, i) for i in range(ends)]),
            ],
            axis=dim,
        )
    return cells


def gathered(array, axis):
    count = lax.axis_size(axis)
    copies = jnp.broadcast_to(array[None], (count,) + array.shape)
    return lax.all_to_all(copies, axis, 0, 0, tiled=True)


def spread_weight(weight, ready, riders):
    dp_count = lax.axis_size("dp")
    seq_count = lax.axis_size("seq")
    half = dp_count // 2
    cores = 2
    y_count = half // cores
    rows, width = weight.shape
    partner_pairs = [
        (d * seq_count + s, (d ^ half) * seq_count + (s ^ 1))
        for d in range(dp_count)
        for s in range(seq_count)
    ]
    held = jnp.stack([weight, lax.ppermute(weight, ("dp", "seq"), partner_pairs)])
    ring = [held]
    for shift in range(1, y_count):
        pairs = []
        for d in range(dp_count):
            upper, y_here, core = d // half, (d // cores) % y_count, d % cores
            pairs.append((d, upper * half + ((y_here + shift) % y_count) * cores + core))
        ring.append(lax.ppermute(held, "dp", pairs))
    mine, ready, riders = lax.optimization_barrier((jnp.stack(ring), ready, riders))
    sibling = lax.ppermute(mine, "dp", [(d, d ^ 1) for d in range(dp_count)])
    stacked = jnp.stack([mine, sibling]).reshape(dp_count, rows, width)
    me = lax.axis_index("dp")
    upper, y_here, core = me // half, (me // cores) % y_count, me % cores
    core_of = jnp.arange(2)[:, None, None]
    shift_of = jnp.arange(y_count)[None, :, None]
    upper_of = jnp.arange(2)[None, None, :]
    owner = (
        ((upper + upper_of) % 2) * half
        + ((y_here - shift_of) % y_count) * cores
        + (core + core_of) % 2
    )
    return stacked, owner.reshape(-1), ready, riders


def gathered_copies(copies, axis):
    return lax.all_to_all(copies, axis, 0, 0, tiled=True)


def scattered_sum(array, axis):
    count = lax.axis_size(axis)
    rows, cols = array.shape
    pieces = array.reshape(rows, count, cols // count).transpose(1, 0, 2)
    return jnp.sum(lax.all_to_all(pieces, axis, 0, 0, tiled=True), axis=0)


def passed_along(array, axis, by):
    count = lax.axis_size(axis)
    pairs = [(i, i + by) for i in range(count) if 0 <= i + by < count]
    return lax.ppermute(array, axis, pairs)


def split_heads(query_rows, key_rows):
    rows_here = query_rows.shape[0]
    keys_here = key_rows.shape[0]
    head_count = key_rows.shape[1] // HD
    group_size = query_rows.shape[1] // key_rows.shape[1]
    return rows_here, keys_here, head_count, group_size


def attend_first(query_rows, key_rows, grad_rows, visible):
    rows_here, keys_here, head_count, group_size = split_heads(query_rows, key_rows)
    score_scale = HD ** (-0.5)
    query_split = query_rows.reshape(rows_here, head_count, group_size, HD)
    grad_split = grad_rows.reshape(rows_here, head_count, group_size, HD)
    key_split = key_rows.reshape(keys_here, head_count, HD)
    attentions = []
    value_parts = []
    for kv_group in range(head_count):
        query_head = query_split[:, kv_group]
        grad_head = grad_split[:, kv_group]
        key_head = key_split[:, kv_group]
        scores = (
            jnp.einsum("qgd,kd->gqk", query_head, key_head, preferred_element_type=jnp.float32)
            * score_scale
        )
        masked = jnp.where(visible[None], scores, -1e30)
        highest = jnp.max(masked, axis=-1, keepdims=True)
        weights = jnp.where(visible[None], jnp.exp(masked - highest), 0.0)
        attention = weights / jnp.sum(weights, axis=-1, keepdims=True)
        attention_low = attention.astype(jnp.bfloat16)
        attentions.append(attention)
        value_parts.append(
            jnp.einsum("gqk,qgd->kd", attention_low, grad_head, preferred_element_type=jnp.float32)
        )
    return attentions, jnp.concatenate(value_parts, axis=1)


def attend_second(query_rows, key_rows, value_rows, grad_rows, attentions):
    rows_here, keys_here, head_count, group_size = split_heads(query_rows, key_rows)
    score_scale = HD ** (-0.5)
    high = lax.Precision.HIGHEST
    query_split = query_rows.reshape(rows_here, head_count, group_size, HD)
    grad_split = grad_rows.reshape(rows_here, head_count, group_size, HD)
    key_split = key_rows.reshape(keys_here, head_count, HD)
    value_split = value_rows.reshape(keys_here, head_count, HD)
    query_parts = []
    key_parts = []
    for kv_group in range(head_count):
        query_head = query_split[:, kv_group]
        grad_head = grad_split[:, kv_group]
        key_head = key_split[:, kv_group]
        value_head = value_split[:, kv_group]
        attention = attentions[kv_group]
        prob_grad = jnp.einsum(
            "qgd,kd->gqk", grad_head, value_head, preferred_element_type=jnp.float32
        )
        row_delta = jnp.sum(attention * prob_grad, axis=-1, keepdims=True)
        score_grad = attention * (prob_grad - row_delta)
        key_wide = key_head.astype(jnp.float32)
        query_wide = query_head.astype(jnp.float32)
        query_parts.append(
            jnp.einsum("gqk,kd->qgd", score_grad, key_wide, precision=high) * score_scale
        )
        key_parts.append(
            jnp.einsum("gqk,qgd->kd", score_grad, query_wide, precision=high) * score_scale
        )
    query_grad = jnp.stack(query_parts, axis=1).reshape(rows_here, -1)
    return query_grad, jnp.concatenate(key_parts, axis=1)


def rim_sum(grad_block, tok_count):
    lower_rim = grad_block[:tok_count]
    upper_rim = grad_block[tok_count + tok_count :]
    center = grad_block[tok_count : tok_count + tok_count]
    from_upper = passed_along(lower_rim.astype(jnp.bfloat16), "seq", -1)
    from_lower = passed_along(upper_rim.astype(jnp.bfloat16), "seq", 1)
    return center + from_upper.astype(jnp.float32) + from_lower.astype(jnp.float32)


def local(layer_input, query_states, key_states, out_grad, value_weight, segment_ids, pair_split):
    layer_rows = layer_input[0]
    tok_count = layer_rows.shape[0]
    row_base = lax.axis_index("seq") * tok_count
    dp_count = lax.axis_size("dp")
    model_width = layer_rows.shape[1]
    weight_rows, kv_width = value_weight.shape
    key_block = with_halo(key_states[0], (("seq", 0),), tok_count)
    input_pieces = layer_rows.reshape(tok_count, dp_count, model_width // dp_count).transpose(1, 0, 2)
    weight_slots, slot_owner, key_block, input_pieces = spread_weight(
        value_weight, key_block, input_pieces
    )
    input_blocks = gathered_copies(input_pieces, "dp")
    seg_row = segment_ids[0]
    fill_ids = jnp.full((tok_count,), -1, jnp.int32)
    padded_ids = jnp.concatenate([fill_ids, seg_row, fill_ids])
    seg_key = lax.dynamic_slice_in_dim(padded_ids, row_base, tok_count + 2 * tok_count, 0)
    seg_query = lax.dynamic_slice_in_dim(seg_row, row_base, tok_count, 0)
    pair_numbers = jnp.arange(pair_split.shape[1], dtype=jnp.int32)
    split_query = jnp.sum(
        jnp.where(seg_query[:, None] == pair_numbers[None, :], pair_split[0][None, :], 0), axis=1
    )
    pos_query = row_base + jnp.arange(tok_count, dtype=jnp.int32)
    pos_key = row_base - tok_count + jnp.arange(tok_count + 2 * tok_count, dtype=jnp.int32)
    visible = (seg_key[None, :] == seg_query[:, None]) & (
        (pos_key[None, :] <= pos_query[:, None]) | (pos_key[None, :] < split_query[:, None])
    )
    attentions, value_part = attend_first(query_states[0], key_block, out_grad[0], visible)
    value_part, input_blocks = lax.optimization_barrier((value_part, input_blocks))
    value_grad = rim_sum(value_part, tok_count).astype(jnp.bfloat16)
    value_grad, weight_slots = lax.optimization_barrier((value_grad, weight_slots))
    weight_full = weight_slots.reshape(-1, kv_width)
    grad_copies = jnp.broadcast_to(value_grad[None], (dp_count,) + value_grad.shape)
    seq_count = lax.axis_size("seq")
    grad_rows = gathered_copies(grad_copies, "dp").reshape(dp_count, tok_count, seq_count, -1)
    own_pieces = jnp.einsum(
        "rtk,rtjc->jkc", input_blocks, grad_rows, preferred_element_type=jnp.float32
    )
    summed = jnp.sum(gathered_copies(own_pieces, "seq"), axis=0)
    devices_all = lax.axis_size("dp") * lax.axis_size("seq")
    weight_grad = summed / devices_all
    input_slots = jnp.take(
        layer_rows.reshape(tok_count, dp_count, -1), slot_owner, axis=1, mode="clip"
    ).reshape(tok_count, -1)
    value_rows = jnp.dot(input_slots, weight_full, preferred_element_type=jnp.float32)
    value_block = with_halo(value_rows.astype(jnp.bfloat16), (("seq", 0),), tok_count)
    query_grad, key_part = attend_second(
        query_states[0], key_block, value_block, out_grad[0], attentions
    )
    key_grad = rim_sum(key_part, tok_count).astype(jnp.bfloat16)
    grad_slots = lax.dot_general(
        value_grad,
        weight_full,
        (((1,), (1,)), ((), ())),
        preferred_element_type=jnp.float32,
    ).astype(jnp.bfloat16)
    input_grad = jnp.take(
        grad_slots.reshape(tok_count, dp_count, -1), jnp.argsort(slot_owner), axis=1, mode="clip"
    ).reshape(tok_count, -1)
    return (
        query_grad.astype(jnp.bfloat16)[None],
        key_grad[None],
        input_grad[None],
        weight_grad,
    )


def solution(mesh):
    return jax.shard_map(
        local,
        mesh=mesh,
        in_specs=(
            P("dp", "seq", None),
            P("dp", "seq", None),
            P("dp", "seq", None),
            P("dp", "seq", None),
            P("dp", None),
            P("dp", None),
            P("dp", None),
        ),
        out_specs=(
            P("dp", "seq", None),
            P("dp", "seq", None),
            P("dp", "seq", None),
            P("dp", "seq"),
        ),
        check_vma=False,
    )
```

```python
import jax
import jax.numpy as jnp
from jax import lax
from jax.sharding import PartitionSpec as P

HD = 128


def with_halo(cells, sides, width):
    for axis, dim in sides:
        count = lax.axis_size(axis)
        ends = count - 1
        head = lax.slice_in_dim(cells, 0, width, axis=dim)
        tail = lax.slice_in_dim(cells, cells.shape[dim] - width, cells.shape[dim], axis=dim)
        cells = jnp.concatenate(
            [
                lax.ppermute(tail, axis, [(i, (i + 1) % count) for i in range(ends)]),
                cells,
                lax.ppermute(head, axis, [((i + 1) % count, i) for i in range(ends)]),
            ],
            axis=dim,
        )
    return cells


def gathered(array, axis):
    count = lax.axis_size(axis)
    copies = jnp.broadcast_to(array[None], (count,) + array.shape)
    return lax.all_to_all(copies, axis, 0, 0, tiled=True)


def spread_weight(weight, ready, riders):
    dp_count = lax.axis_size("dp")
    seq_count = lax.axis_size("seq")
    half = dp_count // 2
    cores = 2
    y_count = half // cores
    rows, width = weight.shape
    partner_pairs = [
        (d * seq_count + s, (d ^ half) * seq_count + (s ^ 1))
        for d in range(dp_count)
        for s in range(seq_count)
    ]
    held = jnp.stack([weight, lax.ppermute(weight, ("dp", "seq"), partner_pairs)])
    ring = [held]
    for shift in range(1, y_count):
        pairs = []
        for d in range(dp_count):
            upper, y_here, core = d // half, (d // cores) % y_count, d % cores
            pairs.append((d, upper * half + ((y_here + shift) % y_count) * cores + core))
        ring.append(lax.ppermute(held, "dp", pairs))
    mine, ready, riders = lax.optimization_barrier((jnp.stack(ring), ready, riders))
    sibling = lax.ppermute(mine, "dp", [(d, d ^ 1) for d in range(dp_count)])
    stacked = jnp.stack([mine, sibling]).reshape(dp_count, rows, width)
    me = lax.axis_index("dp")
    upper, y_here, core = me // half, (me // cores) % y_count, me % cores
    core_of = jnp.arange(2)[:, None, None]
    shift_of = jnp.arange(y_count)[None, :, None]
    upper_of = jnp.arange(2)[None, None, :]
    owner = (
        ((upper + upper_of) % 2) * half
        + ((y_here - shift_of) % y_count) * cores
        + (core + core_of) % 2
    )
    return stacked, owner.reshape(-1), ready, riders


def gathered_copies(copies, axis):
    return lax.all_to_all(copies, axis, 0, 0, tiled=True)


def scattered_sum(array, axis):
    count = lax.axis_size(axis)
    rows, cols = array.shape
    pieces = array.reshape(rows, count, cols // count).transpose(1, 0, 2)
    return jnp.sum(lax.all_to_all(pieces, axis, 0, 0, tiled=True), axis=0)


def passed_along(array, axis, by):
    count = lax.axis_size(axis)
    pairs = [(i, i + by) for i in range(count) if 0 <= i + by < count]
    return lax.ppermute(array, axis, pairs)


def split_heads(query_rows, key_rows):
    rows_here = query_rows.shape[0]
    keys_here = key_rows.shape[0]
    head_count = key_rows.shape[1] // HD
    group_size = query_rows.shape[1] // key_rows.shape[1]
    return rows_here, keys_here, head_count, group_size


def attend_first(query_rows, key_rows, grad_rows, visible):
    rows_here, keys_here, head_count, group_size = split_heads(query_rows, key_rows)
    score_scale = HD ** (-0.5)
    query_split = query_rows.reshape(rows_here, head_count, group_size, HD)
    grad_split = grad_rows.reshape(rows_here, head_count, group_size, HD)
    key_split = key_rows.reshape(keys_here, head_count, HD)
    attentions = []
    value_parts = []
    for kv_group in range(head_count):
        query_head = query_split[:, kv_group]
        grad_head = grad_split[:, kv_group]
        key_head = key_split[:, kv_group]
        scores = (
            jnp.einsum("qgd,kd->gqk", query_head, key_head, preferred_element_type=jnp.float32)
            * score_scale
        )
        masked = jnp.where(visible[None], scores, -1e30)
        highest = jnp.max(masked, axis=-1, keepdims=True)
        weights = jnp.where(visible[None], jnp.exp(masked - highest), 0.0)
        attention = weights / jnp.sum(weights, axis=-1, keepdims=True)
        attention_low = attention.astype(jnp.bfloat16)
        attentions.append(attention)
        value_parts.append(
            jnp.einsum("gqk,qgd->kd", attention_low, grad_head, preferred_element_type=jnp.float32)
        )
    return attentions, jnp.concatenate(value_parts, axis=1)


def attend_second(query_rows, key_rows, value_rows, grad_rows, attentions):
    rows_here, keys_here, head_count, group_size = split_heads(query_rows, key_rows)
    score_scale = HD ** (-0.5)
    high = lax.Precision.HIGHEST
    query_split = query_rows.reshape(rows_here, head_count, group_size, HD)
    grad_split = grad_rows.reshape(rows_here, head_count, group_size, HD)
    key_split = key_rows.reshape(keys_here, head_count, HD)
    value_split = value_rows.reshape(keys_here, head_count, HD)
    query_parts = []
    key_parts = []
    for kv_group in range(head_count):
        query_head = query_split[:, kv_group]
        grad_head = grad_split[:, kv_group]
        key_head = key_split[:, kv_group]
        value_head = value_split[:, kv_group]
        attention = attentions[kv_group]
        prob_grad = jnp.einsum(
            "qgd,kd->gqk", grad_head, value_head, preferred_element_type=jnp.float32
        )
        row_delta = jnp.sum(attention * prob_grad, axis=-1, keepdims=True)
        score_grad = attention * (prob_grad - row_delta)
        key_wide = key_head.astype(jnp.float32)
        query_wide = query_head.astype(jnp.float32)
        query_parts.append(
            jnp.einsum("gqk,kd->qgd", score_grad, key_wide, precision=high) * score_scale
        )
        key_parts.append(
            jnp.einsum("gqk,qgd->kd", score_grad, query_wide, precision=high) * score_scale
        )
    query_grad = jnp.stack(query_parts, axis=1).reshape(rows_here, -1)
    return query_grad, jnp.concatenate(key_parts, axis=1)


def rim_sum(grad_block, tok_count):
    lower_rim = grad_block[:tok_count]
    upper_rim = grad_block[tok_count + tok_count :]
    center = grad_block[tok_count : tok_count + tok_count]
    from_upper = passed_along(lower_rim.astype(jnp.bfloat16), "seq", -1)
    from_lower = passed_along(upper_rim.astype(jnp.bfloat16), "seq", 1)
    return center + from_upper.astype(jnp.float32) + from_lower.astype(jnp.float32)


def local(layer_input, query_states, key_states, out_grad, value_weight, segment_ids, pair_split):
    layer_rows = layer_input[0]
    tok_count = layer_rows.shape[0]
    row_base = lax.axis_index("seq") * tok_count
    dp_count = lax.axis_size("dp")
    model_width = layer_rows.shape[1]
    weight_rows, kv_width = value_weight.shape
    key_block = with_halo(key_states[0], (("seq", 0),), tok_count)
    input_pieces = layer_rows.reshape(tok_count, dp_count, model_width // dp_count).transpose(1, 0, 2)
    weight_slots, slot_owner, key_block, input_pieces = spread_weight(
        value_weight, key_block, input_pieces
    )
    input_blocks = gathered_copies(input_pieces, "dp")
    seg_row = segment_ids[0]
    fill_ids = jnp.full((tok_count,), -1, jnp.int32)
    padded_ids = jnp.concatenate([fill_ids, seg_row, fill_ids])
    seg_key = lax.dynamic_slice_in_dim(padded_ids, row_base, tok_count + 2 * tok_count, 0)
    seg_query = lax.dynamic_slice_in_dim(seg_row, row_base, tok_count, 0)
    pair_numbers = jnp.arange(pair_split.shape[1], dtype=jnp.int32)
    split_query = jnp.sum(
        jnp.where(seg_query[:, None] == pair_numbers[None, :], pair_split[0][None, :], 0), axis=1
    )
    pos_query = row_base + jnp.arange(tok_count, dtype=jnp.int32)
    pos_key = row_base - tok_count + jnp.arange(tok_count + 2 * tok_count, dtype=jnp.int32)
    visible = (seg_key[None, :] == seg_query[:, None]) & (
        (pos_key[None, :] <= pos_query[:, None]) | (pos_key[None, :] < split_query[:, None])
    )
    attentions, value_part = attend_first(query_states[0], key_block, out_grad[0], visible)
    value_part, input_blocks = lax.optimization_barrier((value_part, input_blocks))
    value_grad = rim_sum(value_part, tok_count).astype(jnp.bfloat16)
    value_grad, weight_slots = lax.optimization_barrier((value_grad, weight_slots))
    weight_full = weight_slots.reshape(-1, kv_width)
    grad_copies = jnp.broadcast_to(value_grad[None], (dp_count,) + value_grad.shape)
    seq_count = lax.axis_size("seq")
    grad_rows = gathered_copies(grad_copies, "dp").reshape(dp_count, tok_count, seq_count, -1)
    own_pieces = jnp.einsum(
        "rtk,rtjc->jck", input_blocks, grad_rows, preferred_element_type=jnp.float32
    ).astype(jnp.bfloat16)
    summed = jnp.sum(gathered_copies(own_pieces, "seq").astype(jnp.float32), axis=0).T
    devices_all = lax.axis_size("dp") * lax.axis_size("seq")
    weight_grad = summed / devices_all
    input_slots = jnp.take(
        layer_rows.reshape(tok_count, dp_count, -1), slot_owner, axis=1, mode="clip"
    ).reshape(tok_count, -1)
    value_rows = jnp.dot(input_slots, weight_full, preferred_element_type=jnp.float32)
    value_block = with_halo(value_rows.astype(jnp.bfloat16), (("seq", 0),), tok_count)
    query_grad, key_part = attend_second(
        query_states[0], key_block, value_block, out_grad[0], attentions
    )
    key_grad = rim_sum(key_part, tok_count).astype(jnp.bfloat16)
    grad_slots = lax.dot_general(
        value_grad,
        weight_full,
        (((1,), (1,)), ((), ())),
        preferred_element_type=jnp.float32,
    ).astype(jnp.bfloat16)
    input_grad = jnp.take(
        grad_slots.reshape(tok_count, dp_count, -1), jnp.argsort(slot_owner), axis=1, mode="clip"
    ).reshape(tok_count, -1)
    return (
        query_grad.astype(jnp.bfloat16)[None],
        key_grad[None],
        input_grad[None],
        weight_grad,
    )


def solution(mesh):
    return jax.shard_map(
        local,
        mesh=mesh,
        in_specs=(
            P("dp", "seq", None),
            P("dp", "seq", None),
            P("dp", "seq", None),
            P("dp", "seq", None),
            P("dp", None),
            P("dp", None),
            P("dp", None),
        ),
        out_specs=(
            P("dp", "seq", None),
            P("dp", "seq", None),
            P("dp", "seq", None),
            P("dp", "seq"),
        ),
        check_vma=False,
    )
```

```python
import jax
import jax.numpy as jnp
from jax import lax
from jax.sharding import PartitionSpec as P

HD = 128


def with_halo(cells, sides, width):
    for axis, dim in sides:
        count = lax.axis_size(axis)
        ends = count - 1
        head = lax.slice_in_dim(cells, 0, width, axis=dim)
        tail = lax.slice_in_dim(cells, cells.shape[dim] - width, cells.shape[dim], axis=dim)
        cells = jnp.concatenate(
            [
                lax.ppermute(tail, axis, [(i, (i + 1) % count) for i in range(ends)]),
                cells,
                lax.ppermute(head, axis, [((i + 1) % count, i) for i in range(ends)]),
            ],
            axis=dim,
        )
    return cells


def gathered(array, axis):
    count = lax.axis_size(axis)
    copies = jnp.broadcast_to(array[None], (count,) + array.shape)
    return lax.all_to_all(copies, axis, 0, 0, tiled=True)


def spread_weight(weight, ready, riders):
    dp_count = lax.axis_size("dp")
    seq_count = lax.axis_size("seq")
    half = dp_count // 2
    cores = 2
    y_count = half // cores
    rows, width = weight.shape
    partner_pairs = [
        (d * seq_count + s, (d ^ half) * seq_count + (s ^ 1))
        for d in range(dp_count)
        for s in range(seq_count)
    ]
    held = jnp.stack([weight, lax.ppermute(weight, ("dp", "seq"), partner_pairs)])
    ring = [held]
    for shift in range(1, y_count):
        pairs = []
        for d in range(dp_count):
            upper, y_here, core = d // half, (d // cores) % y_count, d % cores
            pairs.append((d, upper * half + ((y_here + shift) % y_count) * cores + core))
        ring.append(lax.ppermute(held, "dp", pairs))
    mine, ready, riders = lax.optimization_barrier((jnp.stack(ring), ready, riders))
    sibling = lax.ppermute(mine, "dp", [(d, d ^ 1) for d in range(dp_count)])
    stacked = jnp.stack([mine, sibling]).reshape(dp_count, rows, width)
    me = lax.axis_index("dp")
    upper, y_here, core = me // half, (me // cores) % y_count, me % cores
    core_of = jnp.arange(2)[:, None, None]
    shift_of = jnp.arange(y_count)[None, :, None]
    upper_of = jnp.arange(2)[None, None, :]
    owner = (
        ((upper + upper_of) % 2) * half
        + ((y_here - shift_of) % y_count) * cores
        + (core + core_of) % 2
    )
    return stacked, owner.reshape(-1), ready, riders


def gathered_copies(copies, axis):
    return lax.all_to_all(copies, axis, 0, 0, tiled=True)


def scattered_sum(array, axis):
    count = lax.axis_size(axis)
    rows, cols = array.shape
    pieces = array.reshape(rows, count, cols // count).transpose(1, 0, 2)
    return jnp.sum(lax.all_to_all(pieces, axis, 0, 0, tiled=True), axis=0)


def passed_along(array, axis, by):
    count = lax.axis_size(axis)
    pairs = [(i, i + by) for i in range(count) if 0 <= i + by < count]
    return lax.ppermute(array, axis, pairs)


def split_heads(query_rows, key_rows):
    rows_here = query_rows.shape[0]
    keys_here = key_rows.shape[0]
    head_count = key_rows.shape[1] // HD
    group_size = query_rows.shape[1] // key_rows.shape[1]
    return rows_here, keys_here, head_count, group_size


def attend_first(query_rows, key_rows, grad_rows, visible):
    rows_here, keys_here, head_count, group_size = split_heads(query_rows, key_rows)
    score_scale = HD ** (-0.5)
    query_split = query_rows.reshape(rows_here, head_count, group_size, HD)
    grad_split = grad_rows.reshape(rows_here, head_count, group_size, HD)
    key_split = key_rows.reshape(keys_here, head_count, HD)
    attentions = []
    value_parts = []
    for kv_group in range(head_count):
        query_head = query_split[:, kv_group]
        grad_head = grad_split[:, kv_group]
        key_head = key_split[:, kv_group]
        scores = (
            jnp.einsum("qgd,kd->gqk", query_head, key_head, preferred_element_type=jnp.float32)
            * score_scale
        )
        masked = jnp.where(visible[None], scores, -1e30)
        highest = jnp.max(masked, axis=-1, keepdims=True)
        weights = jnp.where(visible[None], jnp.exp(masked - highest), 0.0)
        attention = weights / jnp.sum(weights, axis=-1, keepdims=True)
        attention_low = attention.astype(jnp.bfloat16)
        attentions.append(attention)
        value_parts.append(
            jnp.einsum("gqk,qgd->kd", attention_low, grad_head, preferred_element_type=jnp.float32)
        )
    return attentions, jnp.concatenate(value_parts, axis=1)


def attend_second(query_rows, key_rows, value_rows, grad_rows, attentions):
    rows_here, keys_here, head_count, group_size = split_heads(query_rows, key_rows)
    score_scale = HD ** (-0.5)
    high = lax.Precision.HIGHEST
    query_split = query_rows.reshape(rows_here, head_count, group_size, HD)
    grad_split = grad_rows.reshape(rows_here, head_count, group_size, HD)
    key_split = key_rows.reshape(keys_here, head_count, HD)
    value_split = value_rows.reshape(keys_here, head_count, HD)
    query_parts = []
    key_parts = []
    for kv_group in range(head_count):
        query_head = query_split[:, kv_group]
        grad_head = grad_split[:, kv_group]
        key_head = key_split[:, kv_group]
        value_head = value_split[:, kv_group]
        attention = attentions[kv_group]
        prob_grad = jnp.einsum(
            "qgd,kd->gqk", grad_head, value_head, preferred_element_type=jnp.float32
        )
        row_delta = jnp.sum(attention * prob_grad, axis=-1, keepdims=True)
        score_grad = attention * (prob_grad - row_delta)
        key_wide = key_head.astype(jnp.float32)
        query_wide = query_head.astype(jnp.float32)
        query_parts.append(
            jnp.einsum("gqk,kd->qgd", score_grad, key_wide, precision=high) * score_scale
        )
        key_parts.append(
            jnp.einsum("gqk,qgd->kd", score_grad, query_wide, precision=high) * score_scale
        )
    query_grad = jnp.stack(query_parts, axis=1).reshape(rows_here, -1)
    return query_grad, jnp.concatenate(key_parts, axis=1)


def rim_sum(grad_block, tok_count):
    lower_rim = grad_block[:tok_count]
    upper_rim = grad_block[tok_count + tok_count :]
    center = grad_block[tok_count : tok_count + tok_count]
    from_upper = passed_along(lower_rim.astype(jnp.bfloat16), "seq", -1)
    from_lower = passed_along(upper_rim.astype(jnp.bfloat16), "seq", 1)
    return center + from_upper.astype(jnp.float32) + from_lower.astype(jnp.float32)


def local(layer_input, query_states, key_states, out_grad, value_weight, segment_ids, pair_split):
    layer_rows = layer_input[0]
    tok_count = layer_rows.shape[0]
    row_base = lax.axis_index("seq") * tok_count
    dp_count = lax.axis_size("dp")
    model_width = layer_rows.shape[1]
    weight_rows, kv_width = value_weight.shape
    key_block = with_halo(key_states[0], (("seq", 0),), tok_count)
    input_pieces = layer_rows.reshape(tok_count, dp_count, model_width // dp_count).transpose(1, 0, 2)
    weight_slots, slot_owner, key_block, input_pieces = spread_weight(
        value_weight, key_block, input_pieces
    )
    input_blocks = gathered_copies(input_pieces, "dp")
    seg_row = segment_ids[0]
    fill_ids = jnp.full((tok_count,), -1, jnp.int32)
    padded_ids = jnp.concatenate([fill_ids, seg_row, fill_ids])
    seg_key = lax.dynamic_slice_in_dim(padded_ids, row_base, tok_count + 2 * tok_count, 0)
    seg_query = lax.dynamic_slice_in_dim(seg_row, row_base, tok_count, 0)
    pair_numbers = jnp.arange(pair_split.shape[1], dtype=jnp.int32)
    split_query = jnp.sum(
        jnp.where(seg_query[:, None] == pair_numbers[None, :], pair_split[0][None, :], 0), axis=1
    )
    pos_query = row_base + jnp.arange(tok_count, dtype=jnp.int32)
    pos_key = row_base - tok_count + jnp.arange(tok_count + 2 * tok_count, dtype=jnp.int32)
    visible = (seg_key[None, :] == seg_query[:, None]) & (
        (pos_key[None, :] <= pos_query[:, None]) | (pos_key[None, :] < split_query[:, None])
    )
    attentions, value_part = attend_first(query_states[0], key_block, out_grad[0], visible)
    value_part, input_blocks = lax.optimization_barrier((value_part, input_blocks))
    value_grad = rim_sum(value_part, tok_count).astype(jnp.bfloat16)
    value_grad, weight_slots = lax.optimization_barrier((value_grad, weight_slots))
    weight_full = weight_slots.reshape(-1, kv_width)
    grad_copies = jnp.broadcast_to(value_grad[None], (dp_count,) + value_grad.shape)
    seq_count = lax.axis_size("seq")
    grad_rows = gathered_copies(grad_copies, "dp").reshape(dp_count, tok_count, seq_count, -1)
    own_pieces = jnp.einsum(
        "rtk,rtjc->jck", input_blocks, grad_rows, preferred_element_type=jnp.float32
    ).astype(jnp.bfloat16)
    piece_shape = own_pieces.shape[1:]
    dense_pieces = own_pieces.reshape(own_pieces.shape[0], -1, 128)
    summed = jnp.sum(gathered_copies(dense_pieces, "seq").astype(jnp.float32), axis=0)
    summed = summed.reshape(piece_shape).T
    devices_all = lax.axis_size("dp") * lax.axis_size("seq")
    weight_grad = summed / devices_all
    input_slots = jnp.take(
        layer_rows.reshape(tok_count, dp_count, -1), slot_owner, axis=1, mode="clip"
    ).reshape(tok_count, -1)
    value_rows = jnp.dot(input_slots, weight_full, preferred_element_type=jnp.float32)
    value_block = with_halo(value_rows.astype(jnp.bfloat16), (("seq", 0),), tok_count)
    query_grad, key_part = attend_second(
        query_states[0], key_block, value_block, out_grad[0], attentions
    )
    key_grad = rim_sum(key_part, tok_count).astype(jnp.bfloat16)
    grad_slots = lax.dot_general(
        value_grad,
        weight_full,
        (((1,), (1,)), ((), ())),
        preferred_element_type=jnp.float32,
    ).astype(jnp.bfloat16)
    input_grad = jnp.take(
        grad_slots.reshape(tok_count, dp_count, -1), jnp.argsort(slot_owner), axis=1, mode="clip"
    ).reshape(tok_count, -1)
    return (
        query_grad.astype(jnp.bfloat16)[None],
        key_grad[None],
        input_grad[None],
        weight_grad,
    )


def solution(mesh):
    return jax.shard_map(
        local,
        mesh=mesh,
        in_specs=(
            P("dp", "seq", None),
            P("dp", "seq", None),
            P("dp", "seq", None),
            P("dp", "seq", None),
            P("dp", None),
            P("dp", None),
            P("dp", None),
        ),
        out_specs=(
            P("dp", "seq", None),
            P("dp", "seq", None),
            P("dp", "seq", None),
            P("dp", "seq"),
        ),
        check_vma=False,
    )
```

```python
import jax
import jax.numpy as jnp
from jax import lax
from jax.sharding import PartitionSpec as P

HD = 128


def with_halo(cells, sides, width):
    for axis, dim in sides:
        count = lax.axis_size(axis)
        ends = count - 1
        head = lax.slice_in_dim(cells, 0, width, axis=dim)
        tail = lax.slice_in_dim(cells, cells.shape[dim] - width, cells.shape[dim], axis=dim)
        cells = jnp.concatenate(
            [
                lax.ppermute(tail, axis, [(i, (i + 1) % count) for i in range(ends)]),
                cells,
                lax.ppermute(head, axis, [((i + 1) % count, i) for i in range(ends)]),
            ],
            axis=dim,
        )
    return cells


def gathered(array, axis):
    count = lax.axis_size(axis)
    copies = jnp.broadcast_to(array[None], (count,) + array.shape)
    return lax.all_to_all(copies, axis, 0, 0, tiled=True)


def spread_weight(weight, ready, riders):
    dp_count = lax.axis_size("dp")
    seq_count = lax.axis_size("seq")
    half = dp_count // 2
    cores = 2
    y_count = half // cores
    rows, width = weight.shape
    partner_pairs = [
        (d * seq_count + s, (d ^ half) * seq_count + (s ^ 1))
        for d in range(dp_count)
        for s in range(seq_count)
    ]
    held = jnp.stack([weight, lax.ppermute(weight, ("dp", "seq"), partner_pairs)])
    held, riders = lax.optimization_barrier((held, riders))
    ring = [held]
    for shift in range(1, y_count):
        pairs = []
        for d in range(dp_count):
            upper, y_here, core = d // half, (d // cores) % y_count, d % cores
            pairs.append((d, upper * half + ((y_here + shift) % y_count) * cores + core))
        ring.append(lax.ppermute(held, "dp", pairs))
    mine, ready = lax.optimization_barrier((jnp.stack(ring), ready))
    sibling = lax.ppermute(mine, "dp", [(d, d ^ 1) for d in range(dp_count)])
    stacked = jnp.stack([mine, sibling]).reshape(dp_count, rows, width)
    me = lax.axis_index("dp")
    upper, y_here, core = me // half, (me // cores) % y_count, me % cores
    core_of = jnp.arange(2)[:, None, None]
    shift_of = jnp.arange(y_count)[None, :, None]
    upper_of = jnp.arange(2)[None, None, :]
    owner = (
        ((upper + upper_of) % 2) * half
        + ((y_here - shift_of) % y_count) * cores
        + (core + core_of) % 2
    )
    return stacked, owner.reshape(-1), ready, riders


def gathered_copies(copies, axis):
    return lax.all_to_all(copies, axis, 0, 0, tiled=True)


def scattered_sum(array, axis):
    count = lax.axis_size(axis)
    rows, cols = array.shape
    pieces = array.reshape(rows, count, cols // count).transpose(1, 0, 2)
    return jnp.sum(lax.all_to_all(pieces, axis, 0, 0, tiled=True), axis=0)


def passed_along(array, axis, by):
    count = lax.axis_size(axis)
    pairs = [(i, i + by) for i in range(count) if 0 <= i + by < count]
    return lax.ppermute(array, axis, pairs)


def split_heads(query_rows, key_rows):
    rows_here = query_rows.shape[0]
    keys_here = key_rows.shape[0]
    head_count = key_rows.shape[1] // HD
    group_size = query_rows.shape[1] // key_rows.shape[1]
    return rows_here, keys_here, head_count, group_size


def attend_first(query_rows, key_rows, grad_rows, visible):
    rows_here, keys_here, head_count, group_size = split_heads(query_rows, key_rows)
    score_scale = HD ** (-0.5)
    query_split = query_rows.reshape(rows_here, head_count, group_size, HD)
    grad_split = grad_rows.reshape(rows_here, head_count, group_size, HD)
    key_split = key_rows.reshape(keys_here, head_count, HD)
    attentions = []
    value_parts = []
    for kv_group in range(head_count):
        query_head = query_split[:, kv_group]
        grad_head = grad_split[:, kv_group]
        key_head = key_split[:, kv_group]
        scores = (
            jnp.einsum("qgd,kd->gqk", query_head, key_head, preferred_element_type=jnp.float32)
            * score_scale
        )
        masked = jnp.where(visible[None], scores, -1e30)
        highest = jnp.max(masked, axis=-1, keepdims=True)
        weights = jnp.where(visible[None], jnp.exp(masked - highest), 0.0)
        attention = weights / jnp.sum(weights, axis=-1, keepdims=True)
        attention_low = attention.astype(jnp.bfloat16)
        attentions.append(attention)
        value_parts.append(
            jnp.einsum("gqk,qgd->kd", attention_low, grad_head, preferred_element_type=jnp.float32)
        )
    return attentions, jnp.concatenate(value_parts, axis=1)


def attend_second(query_rows, key_rows, value_rows, grad_rows, attentions):
    rows_here, keys_here, head_count, group_size = split_heads(query_rows, key_rows)
    score_scale = HD ** (-0.5)
    high = lax.Precision.HIGHEST
    query_split = query_rows.reshape(rows_here, head_count, group_size, HD)
    grad_split = grad_rows.reshape(rows_here, head_count, group_size, HD)
    key_split = key_rows.reshape(keys_here, head_count, HD)
    value_split = value_rows.reshape(keys_here, head_count, HD)
    query_parts = []
    key_parts = []
    for kv_group in range(head_count):
        query_head = query_split[:, kv_group]
        grad_head = grad_split[:, kv_group]
        key_head = key_split[:, kv_group]
        value_head = value_split[:, kv_group]
        attention = attentions[kv_group]
        prob_grad = jnp.einsum(
            "qgd,kd->gqk", grad_head, value_head, preferred_element_type=jnp.float32
        )
        row_delta = jnp.sum(attention * prob_grad, axis=-1, keepdims=True)
        score_grad = attention * (prob_grad - row_delta)
        key_wide = key_head.astype(jnp.float32)
        query_wide = query_head.astype(jnp.float32)
        query_parts.append(
            jnp.einsum("gqk,kd->qgd", score_grad, key_wide, precision=high) * score_scale
        )
        key_parts.append(
            jnp.einsum("gqk,qgd->kd", score_grad, query_wide, precision=high) * score_scale
        )
    query_grad = jnp.stack(query_parts, axis=1).reshape(rows_here, -1)
    return query_grad, jnp.concatenate(key_parts, axis=1)


def rim_sum(grad_block, tok_count):
    lower_rim = grad_block[:tok_count]
    upper_rim = grad_block[tok_count + tok_count :]
    center = grad_block[tok_count : tok_count + tok_count]
    from_upper = passed_along(lower_rim.astype(jnp.bfloat16), "seq", -1)
    from_lower = passed_along(upper_rim.astype(jnp.bfloat16), "seq", 1)
    return center + from_upper.astype(jnp.float32) + from_lower.astype(jnp.float32)


def local(layer_input, query_states, key_states, out_grad, value_weight, segment_ids, pair_split):
    layer_rows = layer_input[0]
    tok_count = layer_rows.shape[0]
    row_base = lax.axis_index("seq") * tok_count
    dp_count = lax.axis_size("dp")
    model_width = layer_rows.shape[1]
    weight_rows, kv_width = value_weight.shape
    key_block = with_halo(key_states[0], (("seq", 0),), tok_count)
    input_pieces = layer_rows.reshape(tok_count, dp_count, model_width // dp_count).transpose(1, 0, 2)
    weight_slots, slot_owner, key_block, input_pieces = spread_weight(
        value_weight, key_block, input_pieces
    )
    input_blocks = gathered_copies(input_pieces, "dp")
    seg_row = segment_ids[0]
    fill_ids = jnp.full((tok_count,), -1, jnp.int32)
    padded_ids = jnp.concatenate([fill_ids, seg_row, fill_ids])
    seg_key = lax.dynamic_slice_in_dim(padded_ids, row_base, tok_count + 2 * tok_count, 0)
    seg_query = lax.dynamic_slice_in_dim(seg_row, row_base, tok_count, 0)
    pair_numbers = jnp.arange(pair_split.shape[1], dtype=jnp.int32)
    split_query = jnp.sum(
        jnp.where(seg_query[:, None] == pair_numbers[None, :], pair_split[0][None, :], 0), axis=1
    )
    pos_query = row_base + jnp.arange(tok_count, dtype=jnp.int32)
    pos_key = row_base - tok_count + jnp.arange(tok_count + 2 * tok_count, dtype=jnp.int32)
    visible = (seg_key[None, :] == seg_query[:, None]) & (
        (pos_key[None, :] <= pos_query[:, None]) | (pos_key[None, :] < split_query[:, None])
    )
    attentions, value_part = attend_first(query_states[0], key_block, out_grad[0], visible)
    value_part, input_blocks = lax.optimization_barrier((value_part, input_blocks))
    value_grad = rim_sum(value_part, tok_count).astype(jnp.bfloat16)
    value_grad, weight_slots = lax.optimization_barrier((value_grad, weight_slots))
    weight_full = weight_slots.reshape(-1, kv_width)
    grad_copies = jnp.broadcast_to(value_grad[None], (dp_count,) + value_grad.shape)
    seq_count = lax.axis_size("seq")
    grad_rows = gathered_copies(grad_copies, "dp").reshape(dp_count, tok_count, seq_count, -1)
    own_pieces = jnp.einsum(
        "rtk,rtjc->jck", input_blocks, grad_rows, preferred_element_type=jnp.float32
    ).astype(jnp.bfloat16)
    summed = jnp.sum(gathered_copies(own_pieces, "seq").astype(jnp.float32), axis=0).T
    devices_all = lax.axis_size("dp") * lax.axis_size("seq")
    weight_grad = summed / devices_all
    input_slots = jnp.take(
        layer_rows.reshape(tok_count, dp_count, -1), slot_owner, axis=1, mode="clip"
    ).reshape(tok_count, -1)
    value_rows = jnp.dot(input_slots, weight_full, preferred_element_type=jnp.float32)
    value_block = with_halo(value_rows.astype(jnp.bfloat16), (("seq", 0),), tok_count)
    query_grad, key_part = attend_second(
        query_states[0], key_block, value_block, out_grad[0], attentions
    )
    key_grad = rim_sum(key_part, tok_count).astype(jnp.bfloat16)
    grad_slots = lax.dot_general(
        value_grad,
        weight_full,
        (((1,), (1,)), ((), ())),
        preferred_element_type=jnp.float32,
    ).astype(jnp.bfloat16)
    input_grad = jnp.take(
        grad_slots.reshape(tok_count, dp_count, -1), jnp.argsort(slot_owner), axis=1, mode="clip"
    ).reshape(tok_count, -1)
    return (
        query_grad.astype(jnp.bfloat16)[None],
        key_grad[None],
        input_grad[None],
        weight_grad,
    )


def solution(mesh):
    return jax.shard_map(
        local,
        mesh=mesh,
        in_specs=(
            P("dp", "seq", None),
            P("dp", "seq", None),
            P("dp", "seq", None),
            P("dp", "seq", None),
            P("dp", None),
            P("dp", None),
            P("dp", None),
        ),
        out_specs=(
            P("dp", "seq", None),
            P("dp", "seq", None),
            P("dp", "seq", None),
            P("dp", "seq"),
        ),
        check_vma=False,
    )
```

```python
import jax
import jax.numpy as jnp
from jax import lax
from jax.sharding import PartitionSpec as P

HD = 128


def with_halo(cells, sides, width):
    for axis, dim in sides:
        count = lax.axis_size(axis)
        ends = count - 1
        head = lax.slice_in_dim(cells, 0, width, axis=dim)
        tail = lax.slice_in_dim(cells, cells.shape[dim] - width, cells.shape[dim], axis=dim)
        cells = jnp.concatenate(
            [
                lax.ppermute(tail, axis, [(i, (i + 1) % count) for i in range(ends)]),
                cells,
                lax.ppermute(head, axis, [((i + 1) % count, i) for i in range(ends)]),
            ],
            axis=dim,
        )
    return cells


def gathered(array, axis):
    count = lax.axis_size(axis)
    copies = jnp.broadcast_to(array[None], (count,) + array.shape)
    return lax.all_to_all(copies, axis, 0, 0, tiled=True)


def spread_weight(weight, ready, riders):
    dp_count = lax.axis_size("dp")
    seq_count = lax.axis_size("seq")
    half = dp_count // 2
    cores = 2
    y_count = half // cores
    rows, width = weight.shape
    partner_pairs = [
        (d * seq_count + s, (d ^ half) * seq_count + (s ^ 1))
        for d in range(dp_count)
        for s in range(seq_count)
    ]
    held = jnp.stack([weight, lax.ppermute(weight, ("dp", "seq"), partner_pairs)])
    ring = [held]
    for shift in range(1, y_count):
        pairs = []
        for d in range(dp_count):
            upper, y_here, core = d // half, (d // cores) % y_count, d % cores
            pairs.append((d, upper * half + ((y_here + shift) % y_count) * cores + core))
        ring.append(lax.ppermute(held, "dp", pairs))
    mine, ready, riders = lax.optimization_barrier((jnp.stack(ring), ready, riders))
    sibling = lax.ppermute(mine, "dp", [(d, d ^ 1) for d in range(dp_count)])
    stacked = jnp.stack([mine, sibling]).reshape(dp_count, rows, width)
    me = lax.axis_index("dp")
    upper, y_here, core = me // half, (me // cores) % y_count, me % cores
    core_of = jnp.arange(2)[:, None, None]
    shift_of = jnp.arange(y_count)[None, :, None]
    upper_of = jnp.arange(2)[None, None, :]
    owner = (
        ((upper + upper_of) % 2) * half
        + ((y_here - shift_of) % y_count) * cores
        + (core + core_of) % 2
    )
    return stacked, owner.reshape(-1), ready, riders


def gathered_copies(copies, axis):
    return lax.all_to_all(copies, axis, 0, 0, tiled=True)


def scattered_sum(array, axis):
    count = lax.axis_size(axis)
    rows, cols = array.shape
    pieces = array.reshape(rows, count, cols // count).transpose(1, 0, 2)
    return jnp.sum(lax.all_to_all(pieces, axis, 0, 0, tiled=True), axis=0)


def passed_along(array, axis, by):
    count = lax.axis_size(axis)
    pairs = [(i, i + by) for i in range(count) if 0 <= i + by < count]
    return lax.ppermute(array, axis, pairs)


def split_heads(query_rows, key_rows):
    rows_here = query_rows.shape[0]
    keys_here = key_rows.shape[0]
    head_count = key_rows.shape[1] // HD
    group_size = query_rows.shape[1] // key_rows.shape[1]
    return rows_here, keys_here, head_count, group_size


def attend_first(query_rows, key_rows, grad_rows, visible):
    rows_here, keys_here, head_count, group_size = split_heads(query_rows, key_rows)
    score_scale = HD ** (-0.5)
    query_split = query_rows.reshape(rows_here, head_count, group_size, HD)
    grad_split = grad_rows.reshape(rows_here, head_count, group_size, HD)
    key_split = key_rows.reshape(keys_here, head_count, HD)
    attentions = []
    value_parts = []
    for kv_group in range(head_count):
        query_head = query_split[:, kv_group]
        grad_head = grad_split[:, kv_group]
        key_head = key_split[:, kv_group]
        scores = (
            jnp.einsum("qgd,kd->gqk", query_head, key_head, preferred_element_type=jnp.float32)
            * score_scale
        )
        masked = jnp.where(visible[None], scores, -1e30)
        highest = jnp.max(masked, axis=-1, keepdims=True)
        weights = jnp.where(visible[None], jnp.exp(masked - highest), 0.0)
        attention = weights / jnp.sum(weights, axis=-1, keepdims=True)
        attention_low = attention.astype(jnp.bfloat16)
        attentions.append(attention)
        value_parts.append(
            jnp.einsum("gqk,qgd->kd", attention_low, grad_head, preferred_element_type=jnp.float32)
        )
    return attentions, jnp.concatenate(value_parts, axis=1)


def attend_second(query_rows, key_rows, value_rows, grad_rows, attentions):
    rows_here, keys_here, head_count, group_size = split_heads(query_rows, key_rows)
    score_scale = HD ** (-0.5)
    high = lax.Precision.HIGHEST
    query_split = query_rows.reshape(rows_here, head_count, group_size, HD)
    grad_split = grad_rows.reshape(rows_here, head_count, group_size, HD)
    key_split = key_rows.reshape(keys_here, head_count, HD)
    value_split = value_rows.reshape(keys_here, head_count, HD)
    query_parts = []
    key_parts = []
    for kv_group in range(head_count):
        query_head = query_split[:, kv_group]
        grad_head = grad_split[:, kv_group]
        key_head = key_split[:, kv_group]
        value_head = value_split[:, kv_group]
        attention = attentions[kv_group]
        prob_grad = jnp.einsum(
            "qgd,kd->gqk", grad_head, value_head, preferred_element_type=jnp.float32
        )
        row_delta = jnp.sum(attention * prob_grad, axis=-1, keepdims=True)
        score_grad = attention * (prob_grad - row_delta)
        key_wide = key_head.astype(jnp.float32)
        query_wide = query_head.astype(jnp.float32)
        query_parts.append(
            jnp.einsum("gqk,kd->qgd", score_grad, key_wide, precision=high) * score_scale
        )
        key_parts.append(
            jnp.einsum("gqk,qgd->kd", score_grad, query_wide, precision=high) * score_scale
        )
    query_grad = jnp.stack(query_parts, axis=1).reshape(rows_here, -1)
    return query_grad, jnp.concatenate(key_parts, axis=1)


def rim_sum(grad_block, tok_count):
    lower_rim = grad_block[:tok_count]
    upper_rim = grad_block[tok_count + tok_count :]
    center = grad_block[tok_count : tok_count + tok_count]
    from_upper = passed_along(lower_rim.astype(jnp.bfloat16), "seq", -1)
    from_lower = passed_along(upper_rim.astype(jnp.bfloat16), "seq", 1)
    return center + from_upper.astype(jnp.float32) + from_lower.astype(jnp.float32)


def local(layer_input, query_states, key_states, out_grad, value_weight, segment_ids, pair_split):
    layer_rows = layer_input[0]
    tok_count = layer_rows.shape[0]
    row_base = lax.axis_index("seq") * tok_count
    dp_count = lax.axis_size("dp")
    model_width = layer_rows.shape[1]
    weight_rows, kv_width = value_weight.shape
    key_block = with_halo(key_states[0], (("seq", 0),), tok_count)
    input_pieces = layer_rows.reshape(tok_count, dp_count, model_width // dp_count).transpose(1, 0, 2)
    weight_slots, slot_owner, key_block, input_pieces = spread_weight(
        value_weight, key_block, input_pieces
    )
    input_blocks = gathered_copies(input_pieces, "dp")
    seg_row = segment_ids[0]
    fill_ids = jnp.full((tok_count,), -1, jnp.int32)
    padded_ids = jnp.concatenate([fill_ids, seg_row, fill_ids])
    seg_key = lax.dynamic_slice_in_dim(padded_ids, row_base, tok_count + 2 * tok_count, 0)
    seg_query = lax.dynamic_slice_in_dim(seg_row, row_base, tok_count, 0)
    pair_numbers = jnp.arange(pair_split.shape[1], dtype=jnp.int32)
    split_query = jnp.sum(
        jnp.where(seg_query[:, None] == pair_numbers[None, :], pair_split[0][None, :], 0), axis=1
    )
    pos_query = row_base + jnp.arange(tok_count, dtype=jnp.int32)
    pos_key = row_base - tok_count + jnp.arange(tok_count + 2 * tok_count, dtype=jnp.int32)
    visible = (seg_key[None, :] == seg_query[:, None]) & (
        (pos_key[None, :] <= pos_query[:, None]) | (pos_key[None, :] < split_query[:, None])
    )
    attentions, value_part = attend_first(query_states[0], key_block, out_grad[0], visible)
    value_part, input_blocks = lax.optimization_barrier((value_part, input_blocks))
    weight_full = weight_slots.reshape(-1, kv_width)
    input_slots = jnp.take(
        layer_rows.reshape(tok_count, dp_count, -1), slot_owner, axis=1, mode="clip"
    ).reshape(tok_count, -1)
    value_rows = jnp.dot(input_slots, weight_full, preferred_element_type=jnp.float32)
    value_low = value_rows.astype(jnp.bfloat16)
    rim_low = value_part[:tok_count].astype(jnp.bfloat16)
    rim_high = value_part[tok_count + tok_count :].astype(jnp.bfloat16)
    from_below = passed_along(jnp.concatenate([value_low[-tok_count:], rim_high], axis=1), "seq", 1)
    from_above = passed_along(jnp.concatenate([value_low[:tok_count], rim_low], axis=1), "seq", -1)
    value_block = jnp.concatenate(
        [from_below[:, :kv_width], value_low, from_above[:, :kv_width]], axis=0
    )
    value_grad = (
        value_part[tok_count : tok_count + tok_count]
        + from_above[:, kv_width:].astype(jnp.float32)
        + from_below[:, kv_width:].astype(jnp.float32)
    ).astype(jnp.bfloat16)
    grad_copies = jnp.broadcast_to(value_grad[None], (dp_count,) + value_grad.shape)
    seq_count = lax.axis_size("seq")
    grad_rows = gathered_copies(grad_copies, "dp").reshape(dp_count, tok_count, seq_count, -1)
    own_pieces = jnp.einsum(
        "rtk,rtjc->jck", input_blocks, grad_rows, preferred_element_type=jnp.float32
    ).astype(jnp.bfloat16)
    summed = jnp.sum(gathered_copies(own_pieces, "seq").astype(jnp.float32), axis=0).T
    devices_all = lax.axis_size("dp") * lax.axis_size("seq")
    weight_grad = summed / devices_all
    query_grad, key_part = attend_second(
        query_states[0], key_block, value_block, out_grad[0], attentions
    )
    key_grad = rim_sum(key_part, tok_count).astype(jnp.bfloat16)
    grad_slots = lax.dot_general(
        value_grad,
        weight_full,
        (((1,), (1,)), ((), ())),
        preferred_element_type=jnp.float32,
    ).astype(jnp.bfloat16)
    input_grad = jnp.take(
        grad_slots.reshape(tok_count, dp_count, -1), jnp.argsort(slot_owner), axis=1, mode="clip"
    ).reshape(tok_count, -1)
    return (
        query_grad.astype(jnp.bfloat16)[None],
        key_grad[None],
        input_grad[None],
        weight_grad,
    )


def solution(mesh):
    return jax.shard_map(
        local,
        mesh=mesh,
        in_specs=(
            P("dp", "seq", None),
            P("dp", "seq", None),
            P("dp", "seq", None),
            P("dp", "seq", None),
            P("dp", None),
            P("dp", None),
            P("dp", None),
        ),
        out_specs=(
            P("dp", "seq", None),
            P("dp", "seq", None),
            P("dp", "seq", None),
            P("dp", "seq"),
        ),
        check_vma=False,
    )
```

```python
import jax
import jax.numpy as jnp
from jax import lax
from jax.sharding import PartitionSpec as P

HD = 128


def with_halo(cells, sides, width):
    for axis, dim in sides:
        count = lax.axis_size(axis)
        ends = count - 1
        head = lax.slice_in_dim(cells, 0, width, axis=dim)
        tail = lax.slice_in_dim(cells, cells.shape[dim] - width, cells.shape[dim], axis=dim)
        cells = jnp.concatenate(
            [
                lax.ppermute(tail, axis, [(i, (i + 1) % count) for i in range(ends)]),
                cells,
                lax.ppermute(head, axis, [((i + 1) % count, i) for i in range(ends)]),
            ],
            axis=dim,
        )
    return cells


def gathered(array, axis):
    count = lax.axis_size(axis)
    copies = jnp.broadcast_to(array[None], (count,) + array.shape)
    return lax.all_to_all(copies, axis, 0, 0, tiled=True)


def spread_weight(weight, ready, riders):
    dp_count = lax.axis_size("dp")
    seq_count = lax.axis_size("seq")
    half = dp_count // 2
    cores = 2
    y_count = half // cores
    rows, width = weight.shape
    partner_pairs = [
        (d * seq_count + s, (d ^ half) * seq_count + (s ^ 1))
        for d in range(dp_count)
        for s in range(seq_count)
    ]
    held = jnp.stack([weight, lax.ppermute(weight, ("dp", "seq"), partner_pairs)])
    def shifted(array, shift):
        pairs = []
        for d in range(dp_count):
            upper, y_here, core = d // half, (d // cores) % y_count, d % cores
            pairs.append((d, upper * half + ((y_here + shift) % y_count) * cores + core))
        return lax.ppermute(array, "dp", pairs)

    from_before = shifted(held, 1)
    from_after = shifted(held, y_count - 1)
    two_away = jnp.stack([shifted(from_before[0], 1), shifted(from_after[1], y_count - 1)])
    ring = [held, from_before, two_away, from_after]
    mine, ready, riders = lax.optimization_barrier((jnp.stack(ring), ready, riders))
    sibling = lax.ppermute(mine, "dp", [(d, d ^ 1) for d in range(dp_count)])
    stacked = jnp.stack([mine, sibling]).reshape(dp_count, rows, width)
    me = lax.axis_index("dp")
    upper, y_here, core = me // half, (me // cores) % y_count, me % cores
    core_of = jnp.arange(2)[:, None, None]
    shift_of = jnp.arange(y_count)[None, :, None]
    upper_of = jnp.arange(2)[None, None, :]
    owner = (
        ((upper + upper_of) % 2) * half
        + ((y_here - shift_of) % y_count) * cores
        + (core + core_of) % 2
    )
    return stacked, owner.reshape(-1), ready, riders


def gathered_copies(copies, axis):
    return lax.all_to_all(copies, axis, 0, 0, tiled=True)


def scattered_sum(array, axis):
    count = lax.axis_size(axis)
    rows, cols = array.shape
    pieces = array.reshape(rows, count, cols // count).transpose(1, 0, 2)
    return jnp.sum(lax.all_to_all(pieces, axis, 0, 0, tiled=True), axis=0)


def passed_along(array, axis, by):
    count = lax.axis_size(axis)
    pairs = [(i, i + by) for i in range(count) if 0 <= i + by < count]
    return lax.ppermute(array, axis, pairs)


def split_heads(query_rows, key_rows):
    rows_here = query_rows.shape[0]
    keys_here = key_rows.shape[0]
    head_count = key_rows.shape[1] // HD
    group_size = query_rows.shape[1] // key_rows.shape[1]
    return rows_here, keys_here, head_count, group_size


def attend_first(query_rows, key_rows, grad_rows, visible):
    rows_here, keys_here, head_count, group_size = split_heads(query_rows, key_rows)
    score_scale = HD ** (-0.5)
    query_split = query_rows.reshape(rows_here, head_count, group_size, HD)
    grad_split = grad_rows.reshape(rows_here, head_count, group_size, HD)
    key_split = key_rows.reshape(keys_here, head_count, HD)
    attentions = []
    value_parts = []
    for kv_group in range(head_count):
        query_head = query_split[:, kv_group]
        grad_head = grad_split[:, kv_group]
        key_head = key_split[:, kv_group]
        scores = (
            jnp.einsum("qgd,kd->gqk", query_head, key_head, preferred_element_type=jnp.float32)
            * score_scale
        )
        masked = jnp.where(visible[None], scores, -1e30)
        highest = jnp.max(masked, axis=-1, keepdims=True)
        weights = jnp.where(visible[None], jnp.exp(masked - highest), 0.0)
        attention = weights / jnp.sum(weights, axis=-1, keepdims=True)
        attention_low = attention.astype(jnp.bfloat16)
        attentions.append(attention)
        value_parts.append(
            jnp.einsum("gqk,qgd->kd", attention_low, grad_head, preferred_element_type=jnp.float32)
        )
    return attentions, jnp.concatenate(value_parts, axis=1)


def attend_second(query_rows, key_rows, value_rows, grad_rows, attentions):
    rows_here, keys_here, head_count, group_size = split_heads(query_rows, key_rows)
    score_scale = HD ** (-0.5)
    high = lax.Precision.HIGHEST
    query_split = query_rows.reshape(rows_here, head_count, group_size, HD)
    grad_split = grad_rows.reshape(rows_here, head_count, group_size, HD)
    key_split = key_rows.reshape(keys_here, head_count, HD)
    value_split = value_rows.reshape(keys_here, head_count, HD)
    query_parts = []
    key_parts = []
    for kv_group in range(head_count):
        query_head = query_split[:, kv_group]
        grad_head = grad_split[:, kv_group]
        key_head = key_split[:, kv_group]
        value_head = value_split[:, kv_group]
        attention = attentions[kv_group]
        prob_grad = jnp.einsum(
            "qgd,kd->gqk", grad_head, value_head, preferred_element_type=jnp.float32
        )
        row_delta = jnp.sum(attention * prob_grad, axis=-1, keepdims=True)
        score_grad = attention * (prob_grad - row_delta)
        key_wide = key_head.astype(jnp.float32)
        query_wide = query_head.astype(jnp.float32)
        query_parts.append(
            jnp.einsum("gqk,kd->qgd", score_grad, key_wide, precision=high) * score_scale
        )
        key_parts.append(
            jnp.einsum("gqk,qgd->kd", score_grad, query_wide, precision=high) * score_scale
        )
    query_grad = jnp.stack(query_parts, axis=1).reshape(rows_here, -1)
    return query_grad, jnp.concatenate(key_parts, axis=1)


def rim_sum(grad_block, tok_count):
    lower_rim = grad_block[:tok_count]
    upper_rim = grad_block[tok_count + tok_count :]
    center = grad_block[tok_count : tok_count + tok_count]
    from_upper = passed_along(lower_rim.astype(jnp.bfloat16), "seq", -1)
    from_lower = passed_along(upper_rim.astype(jnp.bfloat16), "seq", 1)
    return center + from_upper.astype(jnp.float32) + from_lower.astype(jnp.float32)


def local(layer_input, query_states, key_states, out_grad, value_weight, segment_ids, pair_split):
    layer_rows = layer_input[0]
    tok_count = layer_rows.shape[0]
    row_base = lax.axis_index("seq") * tok_count
    dp_count = lax.axis_size("dp")
    model_width = layer_rows.shape[1]
    weight_rows, kv_width = value_weight.shape
    key_block = with_halo(key_states[0], (("seq", 0),), tok_count)
    input_pieces = layer_rows.reshape(tok_count, dp_count, model_width // dp_count).transpose(1, 0, 2)
    weight_slots, slot_owner, key_block, input_pieces = spread_weight(
        value_weight, key_block, input_pieces
    )
    input_blocks = gathered_copies(input_pieces, "dp")
    seg_row = segment_ids[0]
    fill_ids = jnp.full((tok_count,), -1, jnp.int32)
    padded_ids = jnp.concatenate([fill_ids, seg_row, fill_ids])
    seg_key = lax.dynamic_slice_in_dim(padded_ids, row_base, tok_count + 2 * tok_count, 0)
    seg_query = lax.dynamic_slice_in_dim(seg_row, row_base, tok_count, 0)
    pair_numbers = jnp.arange(pair_split.shape[1], dtype=jnp.int32)
    split_query = jnp.sum(
        jnp.where(seg_query[:, None] == pair_numbers[None, :], pair_split[0][None, :], 0), axis=1
    )
    pos_query = row_base + jnp.arange(tok_count, dtype=jnp.int32)
    pos_key = row_base - tok_count + jnp.arange(tok_count + 2 * tok_count, dtype=jnp.int32)
    visible = (seg_key[None, :] == seg_query[:, None]) & (
        (pos_key[None, :] <= pos_query[:, None]) | (pos_key[None, :] < split_query[:, None])
    )
    attentions, value_part = attend_first(query_states[0], key_block, out_grad[0], visible)
    value_part, input_blocks = lax.optimization_barrier((value_part, input_blocks))
    value_grad = rim_sum(value_part, tok_count).astype(jnp.bfloat16)
    value_grad, weight_slots = lax.optimization_barrier((value_grad, weight_slots))
    weight_full = weight_slots.reshape(-1, kv_width)
    grad_copies = jnp.broadcast_to(value_grad[None], (dp_count,) + value_grad.shape)
    seq_count = lax.axis_size("seq")
    grad_rows = gathered_copies(grad_copies, "dp").reshape(dp_count, tok_count, seq_count, -1)
    own_pieces = jnp.einsum(
        "rtk,rtjc->jck", input_blocks, grad_rows, preferred_element_type=jnp.float32
    ).astype(jnp.bfloat16)
    summed = jnp.sum(gathered_copies(own_pieces, "seq").astype(jnp.float32), axis=0).T
    devices_all = lax.axis_size("dp") * lax.axis_size("seq")
    weight_grad = summed / devices_all
    input_slots = jnp.take(
        layer_rows.reshape(tok_count, dp_count, -1), slot_owner, axis=1, mode="clip"
    ).reshape(tok_count, -1)
    value_rows = jnp.dot(input_slots, weight_full, preferred_element_type=jnp.float32)
    value_block = with_halo(value_rows.astype(jnp.bfloat16), (("seq", 0),), tok_count)
    query_grad, key_part = attend_second(
        query_states[0], key_block, value_block, out_grad[0], attentions
    )
    key_grad = rim_sum(key_part, tok_count).astype(jnp.bfloat16)
    grad_slots = lax.dot_general(
        value_grad,
        weight_full,
        (((1,), (1,)), ((), ())),
        preferred_element_type=jnp.float32,
    ).astype(jnp.bfloat16)
    input_grad = jnp.take(
        grad_slots.reshape(tok_count, dp_count, -1), jnp.argsort(slot_owner), axis=1, mode="clip"
    ).reshape(tok_count, -1)
    return (
        query_grad.astype(jnp.bfloat16)[None],
        key_grad[None],
        input_grad[None],
        weight_grad,
    )


def solution(mesh):
    return jax.shard_map(
        local,
        mesh=mesh,
        in_specs=(
            P("dp", "seq", None),
            P("dp", "seq", None),
            P("dp", "seq", None),
            P("dp", "seq", None),
            P("dp", None),
            P("dp", None),
            P("dp", None),
        ),
        out_specs=(
            P("dp", "seq", None),
            P("dp", "seq", None),
            P("dp", "seq", None),
            P("dp", "seq"),
        ),
        check_vma=False,
    )
```

```python
import jax
import jax.numpy as jnp
from jax import lax
from jax.sharding import PartitionSpec as P

HD = 128


def with_halo(cells, sides, width):
    for axis, dim in sides:
        count = lax.axis_size(axis)
        ends = count - 1
        head = lax.slice_in_dim(cells, 0, width, axis=dim)
        tail = lax.slice_in_dim(cells, cells.shape[dim] - width, cells.shape[dim], axis=dim)
        cells = jnp.concatenate(
            [
                lax.ppermute(tail, axis, [(i, (i + 1) % count) for i in range(ends)]),
                cells,
                lax.ppermute(head, axis, [((i + 1) % count, i) for i in range(ends)]),
            ],
            axis=dim,
        )
    return cells


def gathered(array, axis):
    count = lax.axis_size(axis)
    copies = jnp.broadcast_to(array[None], (count,) + array.shape)
    return lax.all_to_all(copies, axis, 0, 0, tiled=True)


def spread_weight(weight, ready, riders):
    dp_count = lax.axis_size("dp")
    seq_count = lax.axis_size("seq")
    half = dp_count // 2
    cores = 2
    y_count = half // cores
    rows, width = weight.shape
    partner_pairs = [
        (d * seq_count + s, (d ^ half) * seq_count + (s ^ 1))
        for d in range(dp_count)
        for s in range(seq_count)
    ]
    held = jnp.stack([weight, lax.ppermute(weight, ("dp", "seq"), partner_pairs)])
    def shifted(array, shift):
        pairs = []
        for d in range(dp_count):
            upper, y_here, core = d // half, (d // cores) % y_count, d % cores
            pairs.append((d, upper * half + ((y_here + shift) % y_count) * cores + core))
        return lax.ppermute(array, "dp", pairs)

    before_own = shifted(held[0], 1)
    after_partner = shifted(held[1], y_count - 1)
    two_away = jnp.stack([shifted(before_own, 1), shifted(after_partner, y_count - 1)])
    from_before = jnp.stack([before_own, shifted(held[1], 1)])
    from_after = jnp.stack([shifted(held[0], y_count - 1), after_partner])
    ring = [held, from_before, two_away, from_after]
    mine, ready, riders = lax.optimization_barrier((jnp.stack(ring), ready, riders))
    sibling = lax.ppermute(mine, "dp", [(d, d ^ 1) for d in range(dp_count)])
    stacked = jnp.stack([mine, sibling]).reshape(dp_count, rows, width)
    me = lax.axis_index("dp")
    upper, y_here, core = me // half, (me // cores) % y_count, me % cores
    core_of = jnp.arange(2)[:, None, None]
    shift_of = jnp.arange(y_count)[None, :, None]
    upper_of = jnp.arange(2)[None, None, :]
    owner = (
        ((upper + upper_of) % 2) * half
        + ((y_here - shift_of) % y_count) * cores
        + (core + core_of) % 2
    )
    return stacked, owner.reshape(-1), ready, riders


def gathered_copies(copies, axis):
    return lax.all_to_all(copies, axis, 0, 0, tiled=True)


def scattered_sum(array, axis):
    count = lax.axis_size(axis)
    rows, cols = array.shape
    pieces = array.reshape(rows, count, cols // count).transpose(1, 0, 2)
    return jnp.sum(lax.all_to_all(pieces, axis, 0, 0, tiled=True), axis=0)


def passed_along(array, axis, by):
    count = lax.axis_size(axis)
    pairs = [(i, i + by) for i in range(count) if 0 <= i + by < count]
    return lax.ppermute(array, axis, pairs)


def split_heads(query_rows, key_rows):
    rows_here = query_rows.shape[0]
    keys_here = key_rows.shape[0]
    head_count = key_rows.shape[1] // HD
    group_size = query_rows.shape[1] // key_rows.shape[1]
    return rows_here, keys_here, head_count, group_size


def attend_first(query_rows, key_rows, grad_rows, visible):
    rows_here, keys_here, head_count, group_size = split_heads(query_rows, key_rows)
    score_scale = HD ** (-0.5)
    query_split = query_rows.reshape(rows_here, head_count, group_size, HD)
    grad_split = grad_rows.reshape(rows_here, head_count, group_size, HD)
    key_split = key_rows.reshape(keys_here, head_count, HD)
    attentions = []
    value_parts = []
    for kv_group in range(head_count):
        query_head = query_split[:, kv_group]
        grad_head = grad_split[:, kv_group]
        key_head = key_split[:, kv_group]
        scores = (
            jnp.einsum("qgd,kd->gqk", query_head, key_head, preferred_element_type=jnp.float32)
            * score_scale
        )
        masked = jnp.where(visible[None], scores, -1e30)
        highest = jnp.max(masked, axis=-1, keepdims=True)
        weights = jnp.where(visible[None], jnp.exp(masked - highest), 0.0)
        attention = weights / jnp.sum(weights, axis=-1, keepdims=True)
        attention_low = attention.astype(jnp.bfloat16)
        attentions.append(attention)
        value_parts.append(
            jnp.einsum("gqk,qgd->kd", attention_low, grad_head, preferred_element_type=jnp.float32)
        )
    return attentions, jnp.concatenate(value_parts, axis=1)


def attend_second(query_rows, key_rows, value_rows, grad_rows, attentions):
    rows_here, keys_here, head_count, group_size = split_heads(query_rows, key_rows)
    score_scale = HD ** (-0.5)
    high = lax.Precision.HIGHEST
    query_split = query_rows.reshape(rows_here, head_count, group_size, HD)
    grad_split = grad_rows.reshape(rows_here, head_count, group_size, HD)
    key_split = key_rows.reshape(keys_here, head_count, HD)
    value_split = value_rows.reshape(keys_here, head_count, HD)
    query_parts = []
    key_parts = []
    for kv_group in range(head_count):
        query_head = query_split[:, kv_group]
        grad_head = grad_split[:, kv_group]
        key_head = key_split[:, kv_group]
        value_head = value_split[:, kv_group]
        attention = attentions[kv_group]
        prob_grad = jnp.einsum(
            "qgd,kd->gqk", grad_head, value_head, preferred_element_type=jnp.float32
        )
        row_delta = jnp.sum(attention * prob_grad, axis=-1, keepdims=True)
        score_grad = attention * (prob_grad - row_delta)
        key_wide = key_head.astype(jnp.float32)
        query_wide = query_head.astype(jnp.float32)
        query_parts.append(
            jnp.einsum("gqk,kd->qgd", score_grad, key_wide, precision=high) * score_scale
        )
        key_parts.append(
            jnp.einsum("gqk,qgd->kd", score_grad, query_wide, precision=high) * score_scale
        )
    query_grad = jnp.stack(query_parts, axis=1).reshape(rows_here, -1)
    return query_grad, jnp.concatenate(key_parts, axis=1)


def rim_sum(grad_block, tok_count):
    lower_rim = grad_block[:tok_count]
    upper_rim = grad_block[tok_count + tok_count :]
    center = grad_block[tok_count : tok_count + tok_count]
    from_upper = passed_along(lower_rim.astype(jnp.bfloat16), "seq", -1)
    from_lower = passed_along(upper_rim.astype(jnp.bfloat16), "seq", 1)
    return center + from_upper.astype(jnp.float32) + from_lower.astype(jnp.float32)


def local(layer_input, query_states, key_states, out_grad, value_weight, segment_ids, pair_split):
    layer_rows = layer_input[0]
    tok_count = layer_rows.shape[0]
    row_base = lax.axis_index("seq") * tok_count
    dp_count = lax.axis_size("dp")
    model_width = layer_rows.shape[1]
    weight_rows, kv_width = value_weight.shape
    key_block = with_halo(key_states[0], (("seq", 0),), tok_count)
    input_pieces = layer_rows.reshape(tok_count, dp_count, model_width // dp_count).transpose(1, 0, 2)
    weight_slots, slot_owner, key_block, input_pieces = spread_weight(
        value_weight, key_block, input_pieces
    )
    input_blocks = gathered_copies(input_pieces, "dp")
    seg_row = segment_ids[0]
    fill_ids = jnp.full((tok_count,), -1, jnp.int32)
    padded_ids = jnp.concatenate([fill_ids, seg_row, fill_ids])
    seg_key = lax.dynamic_slice_in_dim(padded_ids, row_base, tok_count + 2 * tok_count, 0)
    seg_query = lax.dynamic_slice_in_dim(seg_row, row_base, tok_count, 0)
    pair_numbers = jnp.arange(pair_split.shape[1], dtype=jnp.int32)
    split_query = jnp.sum(
        jnp.where(seg_query[:, None] == pair_numbers[None, :], pair_split[0][None, :], 0), axis=1
    )
    pos_query = row_base + jnp.arange(tok_count, dtype=jnp.int32)
    pos_key = row_base - tok_count + jnp.arange(tok_count + 2 * tok_count, dtype=jnp.int32)
    visible = (seg_key[None, :] == seg_query[:, None]) & (
        (pos_key[None, :] <= pos_query[:, None]) | (pos_key[None, :] < split_query[:, None])
    )
    attentions, value_part = attend_first(query_states[0], key_block, out_grad[0], visible)
    value_part, input_blocks = lax.optimization_barrier((value_part, input_blocks))
    value_grad = rim_sum(value_part, tok_count).astype(jnp.bfloat16)
    value_grad, weight_slots = lax.optimization_barrier((value_grad, weight_slots))
    weight_full = weight_slots.reshape(-1, kv_width)
    grad_copies = jnp.broadcast_to(value_grad[None], (dp_count,) + value_grad.shape)
    seq_count = lax.axis_size("seq")
    grad_rows = gathered_copies(grad_copies, "dp").reshape(dp_count, tok_count, seq_count, -1)
    own_pieces = jnp.einsum(
        "rtk,rtjc->jck", input_blocks, grad_rows, preferred_element_type=jnp.float32
    ).astype(jnp.bfloat16)
    summed = jnp.sum(gathered_copies(own_pieces, "seq").astype(jnp.float32), axis=0).T
    devices_all = lax.axis_size("dp") * lax.axis_size("seq")
    weight_grad = summed / devices_all
    input_slots = jnp.take(
        layer_rows.reshape(tok_count, dp_count, -1), slot_owner, axis=1, mode="clip"
    ).reshape(tok_count, -1)
    value_rows = jnp.dot(input_slots, weight_full, preferred_element_type=jnp.float32)
    value_block = with_halo(value_rows.astype(jnp.bfloat16), (("seq", 0),), tok_count)
    query_grad, key_part = attend_second(
        query_states[0], key_block, value_block, out_grad[0], attentions
    )
    key_grad = rim_sum(key_part, tok_count).astype(jnp.bfloat16)
    grad_slots = lax.dot_general(
        value_grad,
        weight_full,
        (((1,), (1,)), ((), ())),
        preferred_element_type=jnp.float32,
    ).astype(jnp.bfloat16)
    input_grad = jnp.take(
        grad_slots.reshape(tok_count, dp_count, -1), jnp.argsort(slot_owner), axis=1, mode="clip"
    ).reshape(tok_count, -1)
    return (
        query_grad.astype(jnp.bfloat16)[None],
        key_grad[None],
        input_grad[None],
        weight_grad,
    )


def solution(mesh):
    return jax.shard_map(
        local,
        mesh=mesh,
        in_specs=(
            P("dp", "seq", None),
            P("dp", "seq", None),
            P("dp", "seq", None),
            P("dp", "seq", None),
            P("dp", None),
            P("dp", None),
            P("dp", None),
        ),
        out_specs=(
            P("dp", "seq", None),
            P("dp", "seq", None),
            P("dp", "seq", None),
            P("dp", "seq"),
        ),
        check_vma=False,
    )
```

```python
import jax
import jax.numpy as jnp
from jax import lax
from jax.sharding import PartitionSpec as P

HD = 128


def with_halo(cells, sides, width):
    for axis, dim in sides:
        count = lax.axis_size(axis)
        ends = count - 1
        head = lax.slice_in_dim(cells, 0, width, axis=dim)
        tail = lax.slice_in_dim(cells, cells.shape[dim] - width, cells.shape[dim], axis=dim)
        cells = jnp.concatenate(
            [
                lax.ppermute(tail, axis, [(i, (i + 1) % count) for i in range(ends)]),
                cells,
                lax.ppermute(head, axis, [((i + 1) % count, i) for i in range(ends)]),
            ],
            axis=dim,
        )
    return cells


def gathered(array, axis):
    count = lax.axis_size(axis)
    copies = jnp.broadcast_to(array[None], (count,) + array.shape)
    return lax.all_to_all(copies, axis, 0, 0, tiled=True)


def spread_weight(weight, ready, riders):
    dp_count = lax.axis_size("dp")
    seq_count = lax.axis_size("seq")
    half = dp_count // 2
    cores = 2
    y_count = half // cores
    rows, width = weight.shape
    partner_pairs = [
        (d * seq_count + s, (d ^ half) * seq_count + (s ^ 1))
        for d in range(dp_count)
        for s in range(seq_count)
    ]
    held = jnp.stack([weight, lax.ppermute(weight, ("dp", "seq"), partner_pairs)])
    def shifted(array, shift):
        pairs = []
        for d in range(dp_count):
            upper, y_here, core = d // half, (d // cores) % y_count, d % cores
            pairs.append((d, upper * half + ((y_here + shift) % y_count) * cores + core))
        return lax.ppermute(array, "dp", pairs)

    before_own = shifted(held[0], 1)
    after_partner = shifted(held[1], y_count - 1)
    two_away = jnp.stack([shifted(before_own, 1), shifted(after_partner, y_count - 1)])
    from_before = jnp.stack([before_own, shifted(held[1], 1)])
    from_after = jnp.stack([shifted(held[0], y_count - 1), after_partner])
    ring = [held, from_before, two_away, from_after]
    swap_pairs = [(d, d ^ 1) for d in range(dp_count)]
    near = lax.ppermute(jnp.stack([held, from_before, from_after]), "dp", swap_pairs)
    mine, ready, riders = lax.optimization_barrier((jnp.stack(ring), ready, riders))
    far = lax.ppermute(mine[2], "dp", swap_pairs)
    sibling = jnp.stack([near[0], near[1], far, near[2]])
    stacked = jnp.stack([mine, sibling]).reshape(dp_count, rows, width)
    me = lax.axis_index("dp")
    upper, y_here, core = me // half, (me // cores) % y_count, me % cores
    core_of = jnp.arange(2)[:, None, None]
    shift_of = jnp.arange(y_count)[None, :, None]
    upper_of = jnp.arange(2)[None, None, :]
    owner = (
        ((upper + upper_of) % 2) * half
        + ((y_here - shift_of) % y_count) * cores
        + (core + core_of) % 2
    )
    return stacked, owner.reshape(-1), ready, riders


def gathered_copies(copies, axis):
    return lax.all_to_all(copies, axis, 0, 0, tiled=True)


def scattered_sum(array, axis):
    count = lax.axis_size(axis)
    rows, cols = array.shape
    pieces = array.reshape(rows, count, cols // count).transpose(1, 0, 2)
    return jnp.sum(lax.all_to_all(pieces, axis, 0, 0, tiled=True), axis=0)


def passed_along(array, axis, by):
    count = lax.axis_size(axis)
    pairs = [(i, i + by) for i in range(count) if 0 <= i + by < count]
    return lax.ppermute(array, axis, pairs)


def split_heads(query_rows, key_rows):
    rows_here = query_rows.shape[0]
    keys_here = key_rows.shape[0]
    head_count = key_rows.shape[1] // HD
    group_size = query_rows.shape[1] // key_rows.shape[1]
    return rows_here, keys_here, head_count, group_size


def attend_first(query_rows, key_rows, grad_rows, visible):
    rows_here, keys_here, head_count, group_size = split_heads(query_rows, key_rows)
    score_scale = HD ** (-0.5)
    query_split = query_rows.reshape(rows_here, head_count, group_size, HD)
    grad_split = grad_rows.reshape(rows_here, head_count, group_size, HD)
    key_split = key_rows.reshape(keys_here, head_count, HD)
    attentions = []
    value_parts = []
    for kv_group in range(head_count):
        query_head = query_split[:, kv_group]
        grad_head = grad_split[:, kv_group]
        key_head = key_split[:, kv_group]
        scores = (
            jnp.einsum("qgd,kd->gqk", query_head, key_head, preferred_element_type=jnp.float32)
            * score_scale
        )
        masked = jnp.where(visible[None], scores, -1e30)
        highest = jnp.max(masked, axis=-1, keepdims=True)
        weights = jnp.where(visible[None], jnp.exp(masked - highest), 0.0)
        attention = weights / jnp.sum(weights, axis=-1, keepdims=True)
        attention_low = attention.astype(jnp.bfloat16)
        attentions.append(attention)
        value_parts.append(
            jnp.einsum("gqk,qgd->kd", attention_low, grad_head, preferred_element_type=jnp.float32)
        )
    return attentions, jnp.concatenate(value_parts, axis=1)


def attend_second(query_rows, key_rows, value_rows, grad_rows, attentions):
    rows_here, keys_here, head_count, group_size = split_heads(query_rows, key_rows)
    score_scale = HD ** (-0.5)
    high = lax.Precision.HIGHEST
    query_split = query_rows.reshape(rows_here, head_count, group_size, HD)
    grad_split = grad_rows.reshape(rows_here, head_count, group_size, HD)
    key_split = key_rows.reshape(keys_here, head_count, HD)
    value_split = value_rows.reshape(keys_here, head_count, HD)
    query_parts = []
    key_parts = []
    for kv_group in range(head_count):
        query_head = query_split[:, kv_group]
        grad_head = grad_split[:, kv_group]
        key_head = key_split[:, kv_group]
        value_head = value_split[:, kv_group]
        attention = attentions[kv_group]
        prob_grad = jnp.einsum(
            "qgd,kd->gqk", grad_head, value_head, preferred_element_type=jnp.float32
        )
        row_delta = jnp.sum(attention * prob_grad, axis=-1, keepdims=True)
        score_grad = attention * (prob_grad - row_delta)
        key_wide = key_head.astype(jnp.float32)
        query_wide = query_head.astype(jnp.float32)
        query_parts.append(
            jnp.einsum("gqk,kd->qgd", score_grad, key_wide, precision=high) * score_scale
        )
        key_parts.append(
            jnp.einsum("gqk,qgd->kd", score_grad, query_wide, precision=high) * score_scale
        )
    query_grad = jnp.stack(query_parts, axis=1).reshape(rows_here, -1)
    return query_grad, jnp.concatenate(key_parts, axis=1)


def rim_sum(grad_block, tok_count):
    lower_rim = grad_block[:tok_count]
    upper_rim = grad_block[tok_count + tok_count :]
    center = grad_block[tok_count : tok_count + tok_count]
    from_upper = passed_along(lower_rim.astype(jnp.bfloat16), "seq", -1)
    from_lower = passed_along(upper_rim.astype(jnp.bfloat16), "seq", 1)
    return center + from_upper.astype(jnp.float32) + from_lower.astype(jnp.float32)


def local(layer_input, query_states, key_states, out_grad, value_weight, segment_ids, pair_split):
    layer_rows = layer_input[0]
    tok_count = layer_rows.shape[0]
    row_base = lax.axis_index("seq") * tok_count
    dp_count = lax.axis_size("dp")
    model_width = layer_rows.shape[1]
    weight_rows, kv_width = value_weight.shape
    key_block = with_halo(key_states[0], (("seq", 0),), tok_count)
    input_pieces = layer_rows.reshape(tok_count, dp_count, model_width // dp_count).transpose(1, 0, 2)
    weight_slots, slot_owner, key_block, input_pieces = spread_weight(
        value_weight, key_block, input_pieces
    )
    input_blocks = gathered_copies(input_pieces, "dp")
    seg_row = segment_ids[0]
    fill_ids = jnp.full((tok_count,), -1, jnp.int32)
    padded_ids = jnp.concatenate([fill_ids, seg_row, fill_ids])
    seg_key = lax.dynamic_slice_in_dim(padded_ids, row_base, tok_count + 2 * tok_count, 0)
    seg_query = lax.dynamic_slice_in_dim(seg_row, row_base, tok_count, 0)
    pair_numbers = jnp.arange(pair_split.shape[1], dtype=jnp.int32)
    split_query = jnp.sum(
        jnp.where(seg_query[:, None] == pair_numbers[None, :], pair_split[0][None, :], 0), axis=1
    )
    pos_query = row_base + jnp.arange(tok_count, dtype=jnp.int32)
    pos_key = row_base - tok_count + jnp.arange(tok_count + 2 * tok_count, dtype=jnp.int32)
    visible = (seg_key[None, :] == seg_query[:, None]) & (
        (pos_key[None, :] <= pos_query[:, None]) | (pos_key[None, :] < split_query[:, None])
    )
    attentions, value_part = attend_first(query_states[0], key_block, out_grad[0], visible)
    value_part, input_blocks = lax.optimization_barrier((value_part, input_blocks))
    value_grad = rim_sum(value_part, tok_count).astype(jnp.bfloat16)
    value_grad, weight_slots = lax.optimization_barrier((value_grad, weight_slots))
    weight_full = weight_slots.reshape(-1, kv_width)
    grad_copies = jnp.broadcast_to(value_grad[None], (dp_count,) + value_grad.shape)
    seq_count = lax.axis_size("seq")
    grad_rows = gathered_copies(grad_copies, "dp").reshape(dp_count, tok_count, seq_count, -1)
    own_pieces = jnp.einsum(
        "rtk,rtjc->jck", input_blocks, grad_rows, preferred_element_type=jnp.float32
    ).astype(jnp.bfloat16)
    summed = jnp.sum(gathered_copies(own_pieces, "seq").astype(jnp.float32), axis=0).T
    devices_all = lax.axis_size("dp") * lax.axis_size("seq")
    weight_grad = summed / devices_all
    input_slots = jnp.take(
        layer_rows.reshape(tok_count, dp_count, -1), slot_owner, axis=1, mode="clip"
    ).reshape(tok_count, -1)
    value_rows = jnp.dot(input_slots, weight_full, preferred_element_type=jnp.float32)
    value_block = with_halo(value_rows.astype(jnp.bfloat16), (("seq", 0),), tok_count)
    query_grad, key_part = attend_second(
        query_states[0], key_block, value_block, out_grad[0], attentions
    )
    key_grad = rim_sum(key_part, tok_count).astype(jnp.bfloat16)
    grad_slots = lax.dot_general(
        value_grad,
        weight_full,
        (((1,), (1,)), ((), ())),
        preferred_element_type=jnp.float32,
    ).astype(jnp.bfloat16)
    input_grad = jnp.take(
        grad_slots.reshape(tok_count, dp_count, -1), jnp.argsort(slot_owner), axis=1, mode="clip"
    ).reshape(tok_count, -1)
    return (
        query_grad.astype(jnp.bfloat16)[None],
        key_grad[None],
        input_grad[None],
        weight_grad,
    )


def solution(mesh):
    return jax.shard_map(
        local,
        mesh=mesh,
        in_specs=(
            P("dp", "seq", None),
            P("dp", "seq", None),
            P("dp", "seq", None),
            P("dp", "seq", None),
            P("dp", None),
            P("dp", None),
            P("dp", None),
        ),
        out_specs=(
            P("dp", "seq", None),
            P("dp", "seq", None),
            P("dp", "seq", None),
            P("dp", "seq"),
        ),
        check_vma=False,
    )
```
